32 devices in a mesh: dp: 4 (over z), fsdp: 8 (over y, x, core).
Axes of the slice: x: 2, y: 2, z: 4, core: 2. Of those that a mesh axis runs over, the one named last changes fastest.
Arguments:
- tokens: bfloat16 [32768, 512], P(('dp', 'fsdp')), may hold values from -6 to 6
- halt_in: float32 [32768], P(('dp', 'fsdp')), may hold values from 0 to 0.7
- depths: int32 [32768], P(('dp', 'fsdp')), may hold values from 1 to 8, as said below
- attn_routes: int32 [32768, 4], P(('dp', 'fsdp')), may hold values from 0 to 23, all different within a row
- ffn_routes: int32 [32768, 2], P(('dp', 'fsdp')), may hold values from 0 to 7, all different within a row; in each aligned block of 1024 rows (0 to 1023, 1024 to 2047, ...) at most 512 rows name the same one
- w_query: bfloat16 [512, 1536], P(('dp', 'fsdp')), may hold values from -0.25 to 0.25
- w_out: bfloat16 [1536, 512], P(None, ('dp', 'fsdp')), may hold values from -12 to 12
- w_kv: bfloat16 [512, 128], P(('dp', 'fsdp')), may hold values from -0.25 to 0.25
- router: bfloat16 [512, 32], P(('dp', 'fsdp')), may hold values from -0.15820312 to 0.15820312
- vectors: bfloat16 [5, 512], P(None, ('dp', 'fsdp')), may hold values from -1 to 2
- w_up: bfloat16 [8, 512, 2048], P('fsdp', None, 'dp'), may hold values from -0.25 to 0.25
- w_down: bfloat16 [8, 2048, 512], P('fsdp', 'dp'), may hold values from -0.25 to 0.25
- cot_out: bfloat16 [32768, 512], P(('dp', 'fsdp')), may hold values from -6 to 6
- cot_halt: float32 [32768], P(('dp', 'fsdp')), may hold values from -6 to 6
Outputs:
- block_out: bfloat16 [32768, 512], P(('dp', 'fsdp'))
- halt_out: float32 [32768], P(('dp', 'fsdp'))
- grad_in: bfloat16 [32768, 512], P(('dp', 'fsdp'))
- grad_query: float32 [512, 1536], P(('dp', 'fsdp'))
- grad_out_proj: float32 [1536, 512], P(None, ('dp', 'fsdp'))
- grad_kv: float32 [512, 128], P(('dp', 'fsdp'))
- grad_router: float32 [512, 32], P(('dp', 'fsdp'))
- grad_vectors: float32 [5, 512], P(None, ('dp', 'fsdp'))
- grad_up: float32 [8, 512, 2048], P('fsdp', None, 'dp')
- grad_down: float32 [8, 2048, 512], P('fsdp', 'dp')
The draws below stay inside these ranges and needn't reach their ends.
Inputs may be any that keep to these rules, and one draw needn't show every extreme that they name: `depths`: halting depth of each token; the first token of every sequence has depth 8. `attn_routes`: each token names 4 different attention experts. `ffn_routes`: each token names 2 different feed-forward experts; among the 1024 rows of one device no expert is named more than 512 times, and in some devices' rows an expert is named exactly 512 times.
All inputs are finite; a program needn't handle non-finite values.
Results may differ from the reference program's by a relative error of at most 0.019.
Values may be sent and summed in bfloat16 or wider, within the bound.
No kernel may reach another device: no remote copies, remote signals or barrier semaphores. Data moves between devices by JAX's collectives and lax.ppermute only.
A program may use at most 256 MiB of HBM per device.

```python
import math
import jax
import jax.numpy as jnp
import numpy as np
from jax import lax

D = 512
HEAD = 64
A_EXP = 24
A_TOP = 4
F_TOP = 2
FF = 2048
LENGTH = 1024
QUERY_BLOCK = 128
STEP = 2
MAX_DEPTH = 8
F_EXP = 8
TOK_DEV = 1024
CAPACITY = 512
TOKENS = 32768


def draw_depths(key, part):
    seq_total = TOKENS // LENGTH
    rate_key, step_key = jax.random.split(key)
    seq_rates = jax.random.randint(rate_key, (seq_total, 1, 1), 5, 10)
    trials = jax.random.randint(step_key, (seq_total, LENGTH, MAX_DEPTH - 1), 0, 10)
    continues = (trials < seq_rates).astype(jnp.int32)
    depth_rows = 1 + jnp.sum(jnp.cumprod(continues, axis=2), axis=2)
    depth_rows = depth_rows.at[:, 0].set(MAX_DEPTH)
    return depth_rows.reshape(TOKENS).astype(jnp.int32)


def draw_vectors(key, part):
    keys_all = jax.random.split(key, 5)
    gain_one = 1.0 + 0.25 * jnp.clip(jax.random.normal(keys_all[0], (D,), jnp.float32), -2.0, 2.0)
    shift_one = 0.1 * jnp.clip(jax.random.normal(keys_all[1], (D,), jnp.float32), -3.0, 3.0)
    gain_two = 1.0 + 0.25 * jnp.clip(jax.random.normal(keys_all[2], (D,), jnp.float32), -2.0, 2.0)
    shift_two = 0.1 * jnp.clip(jax.random.normal(keys_all[3], (D,), jnp.float32), -3.0, 3.0)
    halt_row = jnp.clip(jax.random.normal(keys_all[4], (D,), jnp.float32), -4.0, 4.0) * D ** (-0.5)
    return jnp.stack([gain_one, shift_one, gain_two, shift_two, halt_row]).astype(jnp.bfloat16)


def strengthened(result, key, source, target, parts, factor):
    def block_of(dim):
        return (jnp.arange(result.shape[dim]) // (result.shape[dim] // parts)).reshape((-1,) + (1,) * (result.ndim - 1 - dim))

    one_side = jax.random.permutation(key, parts)[block_of(target)]
    second = (block_of(target) + parts // 2) % parts
    return jnp.where((block_of(source) == one_side) | (block_of(source) == second), factor * result, result)


def level_of(rng, extent, cuts, least, largest):
    gain, own = 1.0, jax.random.fold_in(rng, 6)
    for position, blocks in cuts:
        draws = jnp.exp(jax.random.uniform(jax.random.fold_in(own, position), (blocks,), jnp.float32, least / len(cuts), largest / len(cuts)))
        gain = gain * jnp.repeat(draws, extent[position] // blocks).reshape([-1 if axis == position else 1 for axis in range(len(extent))])
    return gain


def choose_distinct(rng, rows, amount, top, lift):
    order = jax.random.permutation(jax.random.fold_in(rng, 1), amount)
    pull = order
    for power in range(3):
        pull = pull * pull // amount
    pull = pull * lift // amount
    chance = jax.random.randint(jax.random.fold_in(rng, 2), (rows, amount), 0, 4096) + pull
    fixed_rows = jax.random.permutation(jax.random.fold_in(rng, 3), rows)[jnp.arange(amount) % rows]
    chance = jnp.where(jnp.arange(rows)[:, None] == fixed_rows[None, :], 1 << 14, chance)
    merit = chance * amount + jnp.arange(amount)
    return lax.top_k(merit.astype(jnp.int32), top)[1].astype(jnp.int32)


def assign_block(rng, own, number, rows, amount, top, reach, slope):
    sequence = jax.random.permutation(rng, amount)
    heavy_load, ordinary = shares(amount, rows * top, reach, slope, True), shares(amount, rows * top, reach, slope, False)
    places = jnp.arange(amount)

    def named(sizes, turn):
        used = int((sizes > 0).sum())
        fixed = max(1, used // 4)
        passed = fixed + (places - fixed + turn * (used - fixed)) % max(1, amount - fixed)
        return jnp.zeros((amount,), jnp.int32).at[sequence[jnp.where(places < fixed, places, passed)]].set(jnp.asarray(sizes, jnp.int32))

    sizes = jnp.where(number % 4 == 0, named(heavy_load, number // 4), named(ordinary, number - number // 4 - 1))
    mixed = jax.random.permutation(jax.random.fold_in(own, 3), amount)
    source_of, sink = mixed[0:amount // 2 * 2:2], mixed[1:amount // 2 * 2:2]
    slack = jnp.minimum(sizes[source_of] - 1, reach - sizes[sink]) // 2
    slack = jnp.where((source_of == sequence[0]) | (sink == sequence[0]) | (sizes[sink] == 0), 0, jnp.maximum(slack, 0))
    passed = jax.random.randint(jax.random.fold_in(own, 4), (amount // 2,), 0, 1 << 20) % (slack + 1)
    sizes = sizes.at[source_of].add(-passed).at[sink].add(passed)
    labels = jnp.searchsorted(jnp.cumsum(sizes), jnp.arange(rows * top), side="right").astype(jnp.int32)
    grid = labels.reshape(top, rows).T
    grid = grid[jax.random.permutation(jax.random.fold_in(own, 1), rows)]
    turn = jax.random.randint(jax.random.fold_in(own, 2), (rows, 1), 0, top)
    return jnp.take_along_axis(grid, (jnp.arange(top)[None, :] + turn) % top, axis=1)


def shares(number_of, total, limit, skew, full):
    loads = [(1 << 20) // math.isqrt(rank ** skew) + 1 for rank in range(1, number_of + 1)]
    largest = limit if full else min(limit, max(-(-total // number_of), total * loads[0] // sum(loads)))
    least = 1 if total - largest >= number_of - 1 else 0
    holding, spare = [largest] + [least] * (number_of - 1), total - largest - least * (number_of - 1)
    while spare > 0:
        candidates = [i for i in range(1, number_of) if holding[i] < largest] or [i for i in range(1, number_of) if holding[i] < limit]
        mass, budget = sum([loads[i] for i in candidates]), spare
        for i in candidates:
            addition = min(limit - holding[i], max(1, budget * loads[i] // mass), spare)
            holding[i] = holding[i] + addition
            spare = spare - addition
    return np.array(holding)


def normal_values(key, extent, deviation, limit, cuts=(), kind=jnp.bfloat16):
    drawn = jax.random.normal(key, extent, jnp.float32) * deviation
    if len(cuts) > 0:
        drawn = level_of(key, extent, cuts, -0.22, 0.18) * drawn
    return jnp.clip(drawn, min=-limit, max=limit).astype(kind)


def bell_draw_with(rng, dims, spread, reach, shards, heavy, kind=jnp.bfloat16):
    result = spread * jax.random.normal(rng, dims, jnp.float32)
    if shards:
        result = result * level_of(rng, dims, shards, -0.22, 0.18)
    return jnp.clip(strengthened(result, jax.random.fold_in(rng, 3), *heavy), -reach, reach).astype(kind)


def setup_inputs(seed: int = 0) -> dict:
    seeds = jax.random.split(jax.random.key(seed), 15)
    tokens = bell_draw_with(seeds[0], (TOKENS, D), 1.0, 6.0, ((0, 32),), (0, 1, 32, 2.75))
    halt_in = jnp.clip(0.7 * jax.random.uniform(seeds[1], (TOKENS,), jnp.float32) ** level_of(seeds[1], (TOKENS,), ((0, 32),), -0.2, 0.2), 0.0, 0.7)
    depths = draw_depths(jax.random.fold_in(seeds[14], 71), 0)
    attn_routes = choose_distinct(seeds[3], TOKENS, A_EXP, A_TOP, 1365)
    ffn_routes_keys = jax.random.split(jax.random.fold_in(seeds[4], 1), TOKENS // TOK_DEV)
    ffn_routes_turns = jax.random.permutation(jax.random.fold_in(seeds[4], 3), TOKENS // TOK_DEV)
    ffn_routes = jax.vmap(lambda own, number: assign_block(jax.random.fold_in(seeds[4], 2), own, number, TOK_DEV, F_EXP, F_TOP, CAPACITY, 2))(ffn_routes_keys, ffn_routes_turns).reshape((TOKENS, F_TOP))
    w_query = normal_values(seeds[5], (D, A_EXP * HEAD), D ** -0.5, 0.25, ((0, 32),))
    w_out = normal_values(seeds[6], (A_EXP * HEAD, D), 2.0, 12.0, ((1, 32),))
    w_kv = normal_values(seeds[7], (D, 2 * HEAD), D ** -0.5, 0.25, ((0, 32),))
    router = normal_values(seeds[8], (D, A_EXP + F_EXP), (0.6 * D ** -0.5), 0.15820312, ((0, 32),))
    vectors = draw_vectors(jax.random.fold_in(seeds[14], 71), 0)
    w_up = normal_values(seeds[10], (F_EXP, D, FF), D ** -0.5, 0.25, ((0, 8), (2, 4)))
    w_down = normal_values(seeds[11], (F_EXP, FF, D), (FF // 4) ** -0.5, 0.25, ((0, 8), (1, 4)))
    cot_out = bell_draw_with(seeds[12], (TOKENS, D), 1.0, 6.0, ((0, 32),), (0, 1, 32, 2.75))
    cot_halt = normal_values(seeds[13], (TOKENS,), 1.0, 6.0, ((0, 32),), jnp.float32)
    return dict(tokens=tokens, halt_in=halt_in, depths=depths, attn_routes=attn_routes, ffn_routes=ffn_routes, w_query=w_query, w_out=w_out, w_kv=w_kv, router=router, vectors=vectors, w_up=w_up, w_down=w_down, cot_out=cot_out, cot_halt=cot_halt)


PRECISE = lax.Precision.HIGHEST
EPSILON = 1e-05

@jax.custom_vjp
def low(v):
    return lax.optimization_barrier(v.astype(jnp.bfloat16)).astype(jnp.float32)

@jax.custom_vjp
def low_back(v):
    return v

def low_keep(v):
    return (low(v), None)

def low_pass(kept, grad):
    return (grad,)

def back_keep(v):
    return (v, None)

def back_low(kept, grad):
    return (low(grad),)
low.defvjp(low_keep, low_pass)
low_back.defvjp(back_keep, back_low)

def layer_norm(values, gain_row, shift_row):
    center = values - lax.optimization_barrier(jnp.mean(values, axis=-1, keepdims=True))
    inv_std = lax.rsqrt(lax.optimization_barrier(jnp.mean(center * center, axis=-1, keepdims=True)) + EPSILON)
    return center * inv_std * gain_row + shift_row

def slot_table(ffn_routes, active_mask, tok_count):
    pick_bool = (ffn_routes[:, :, None] == jnp.arange(F_EXP, dtype=jnp.int32)[None, None, :]) & active_mask[:, None, None]
    flat_pick = pick_bool.reshape(tok_count * F_TOP, F_EXP).astype(jnp.int32)
    slot_place = jnp.cumsum(flat_pick, axis=0).astype(jnp.int32) - 1
    own_place = lax.optimization_barrier(jnp.sum(flat_pick * slot_place, axis=1)).astype(jnp.int32)
    expert = ffn_routes.reshape(tok_count * F_TOP).astype(jnp.int32)
    is_live = lax.optimization_barrier(jnp.sum(flat_pick, axis=1)) > 0
    slot_dest = jnp.where(is_live, expert * CAPACITY + own_place, F_EXP * CAPACITY).astype(jnp.int32)
    owners = (jnp.arange(tok_count * F_TOP, dtype=jnp.int32) // F_TOP).astype(jnp.int32)
    slot_source = jnp.full((F_EXP * CAPACITY + 1,), tok_count, jnp.int32).at[slot_dest].set(owners)
    return (slot_dest, slot_source[:F_EXP * CAPACITY])

def attend_block(key_rows, value_rows, block_query, first_row):
    score_scale = HEAD ** (-0.5)
    scores = low_back(jnp.einsum('tkh,jh->tkj', block_query, key_rows, precision=PRECISE)) * score_scale
    positions = first_row + jnp.arange(QUERY_BLOCK, dtype=jnp.int32)
    allowed = jnp.arange(LENGTH, dtype=jnp.int32)[None, None, :] <= positions[:, None, None]
    scores = jnp.where(allowed, scores, -1e+30)
    weights = low(jax.nn.softmax(scores, axis=-1))
    return jnp.einsum('tkj,jh->tkh', weights, value_rows, precision=PRECISE)

def attend_sequence(seq_pair):
    seq_query, seq_kv = seq_pair
    key_rows = seq_kv[:, :HEAD]
    value_rows = seq_kv[:, HEAD:]
    block_count = LENGTH // QUERY_BLOCK
    blocks = seq_query.reshape(block_count, QUERY_BLOCK, A_TOP, HEAD)
    firsts = jnp.arange(block_count, dtype=jnp.int32) * QUERY_BLOCK
    checked = jax.checkpoint(attend_block)
    outputs = lax.map(lambda block_item: checked(key_rows, value_rows, block_item[0], block_item[1]), (blocks, firsts))
    return outputs.reshape(LENGTH, A_TOP, HEAD)

def block_rows(weights, row_set):
    w_query, w_out, w_kv, router, vectors, w_up, w_down = weights
    tokens, halt_in, depths, attn_routes, ffn_routes = row_set
    tok_count = tokens.shape[0]
    seq_count = tok_count // LENGTH
    active_mask = depths >= STEP
    active = active_mask.astype(jnp.float32)
    normed = low(layer_norm(tokens, vectors[0], vectors[1]))
    queries = low(low_back(jnp.dot(normed, w_query, precision=PRECISE)))
    key_value = low(low_back(jnp.dot(normed, w_kv, precision=PRECISE)))
    attn_pick = (attn_routes[:, :, None] == jnp.arange(A_EXP, dtype=jnp.int32)[None, None, :]).astype(jnp.float32)
    attn_logits = jnp.dot(normed, router[:, :A_EXP], precision=PRECISE)
    attn_gates = jax.nn.softmax(jnp.einsum('tke,te->tk', attn_pick, attn_logits, precision=PRECISE), axis=-1)
    slot_query = jnp.einsum('tke,teh->tkh', attn_pick, queries.reshape(tok_count, A_EXP, HEAD), precision=PRECISE)
    slot_out = lax.map(attend_sequence, (slot_query.reshape(seq_count, LENGTH, A_TOP, HEAD), key_value.reshape(seq_count, LENGTH, 2 * HEAD)))
    slot_out = low_back(slot_out.reshape(tok_count, A_TOP, HEAD))
    mixed_heads = low(jnp.einsum('tke,tkh->teh', attn_pick * attn_gates[:, :, None], slot_out, precision=PRECISE).reshape(tok_count, A_EXP * HEAD))
    attn_branch = low_back(jnp.dot(mixed_heads, w_out, precision=PRECISE))
    hidden = tokens + active[:, None] * attn_branch
    normed_two = low(layer_norm(hidden, vectors[2], vectors[3]))
    ffn_pick = (ffn_routes[:, :, None] == jnp.arange(F_EXP, dtype=jnp.int32)[None, None, :]).astype(jnp.float32)
    ffn_logits = jnp.dot(normed_two, router[:, A_EXP:], precision=PRECISE)
    ffn_gates = jax.nn.softmax(jnp.einsum('tke,te->tk', ffn_pick, ffn_logits, precision=PRECISE), axis=-1)
    slot_dest, slot_source = slot_table(ffn_routes, active_mask, tok_count)
    padded_rows = jnp.concatenate([normed_two, jnp.zeros((1, D), jnp.float32)], axis=0)
    slot_rows = padded_rows[slot_source].reshape(F_EXP, CAPACITY, D)
    pre_act = low_back(jnp.einsum('ecd,edf->ecf', slot_rows, w_up, precision=PRECISE))
    gelu_out = low(jax.nn.gelu(pre_act, approximate=False))
    expert_out = low(low_back(jnp.einsum('ecf,efd->ecd', gelu_out, w_down, precision=PRECISE)))
    padded_out = jnp.concatenate([expert_out.reshape(F_EXP * CAPACITY, D), jnp.zeros((1, D), jnp.float32)], axis=0)
    assigned = padded_out[slot_dest].reshape(tok_count, F_TOP, D)
    ffn_branch = lax.optimization_barrier(jnp.sum(ffn_gates[:, :, None] * assigned, axis=1))
    block_out = hidden + active[:, None] * ffn_branch
    halt_prob = jax.nn.sigmoid(jnp.dot(block_out, vectors[4], precision=PRECISE))
    halt_out = halt_in + active * (1.0 - halt_in) * halt_prob
    return (block_out, halt_out)

def reference(tokens, halt_in, depths, attn_routes, ffn_routes, w_query, w_out, w_kv, router, vectors, w_up, w_down, cot_out, cot_halt):
    block_count = TOKENS // TOK_DEV
    weights = (w_query.astype(jnp.float32), w_out.astype(jnp.float32), w_kv.astype(jnp.float32), router.astype(jnp.float32), vectors.astype(jnp.float32), w_up.astype(jnp.float32), w_down.astype(jnp.float32))
    split_rows = (halt_in.reshape(block_count, TOK_DEV), depths.reshape(block_count, TOK_DEV), attn_routes.reshape(block_count, TOK_DEV, A_TOP), ffn_routes.reshape(block_count, TOK_DEV, F_TOP))
    checked = jax.checkpoint(block_rows)

    def forward(tok_float, weight_set):
        tok_blocks = tok_float.reshape(block_count, TOK_DEV, D)
        outputs, halt_blocks = lax.map(lambda block_item: checked(weight_set, (block_item[0],) + block_item[1]), (tok_blocks, split_rows))
        return (outputs.reshape(TOKENS, D), halt_blocks.reshape(TOKENS))
    (block_out, halt_out), pull_back = jax.vjp(forward, tokens.astype(jnp.float32), weights)
    grad_tokens, grad_weights = pull_back((cot_out.astype(jnp.float32), cot_halt))
    return (block_out.astype(jnp.bfloat16), halt_out, grad_tokens.astype(jnp.bfloat16), grad_weights[0], grad_weights[1], grad_weights[2], grad_weights[3], grad_weights[4], grad_weights[5], grad_weights[6])
```

```python
from functools import partial

import jax
import jax.numpy as jnp
from jax import lax
from jax.experimental import pallas as pl
from jax.experimental.pallas import tpu as pltpu
from jax.sharding import PartitionSpec as P

D = 512
HEAD = 64
A_EXP = 24
A_TOP = 4
F_TOP = 2
STEP = 2
LANES = 128
BLOCK = 256
PAIRS = A_EXP // 2
WIDTH = A_EXP * HEAD
KV_AT = 2 * WIDTH
RV_AT = KV_AT + LANES
PACK = RV_AT + LANES
EPSILON = 1e-05
NEG = -1e30
BF = jnp.bfloat16
F32 = jnp.float32

NN = (((1,), (0,)), ((), ()))
NT = (((1,), (1,)), ((), ()))
TN = (((0,), (0,)), ((), ()))

TAIL_P = 0.3
TAIL = (
    0.11962930113077164,
    0.1207539290189743,
    0.09991367161273956,
    0.12856101989746094,
    -0.053682513535022736,
    0.20635227859020233,
    -0.15720237791538239,
    0.03567460551857948,
)


def dot(a, b, dims=NN):
    return lax.dot_general(a, b, dims, preferred_element_type=F32)


def lane_ids(rows):
    return lax.broadcasted_iota(jnp.int32, (rows, LANES), 1)


def norm_stats(values):
    center = values - jnp.mean(values, axis=-1, keepdims=True)
    inv_std = lax.rsqrt(jnp.mean(center * center, axis=-1, keepdims=True) + EPSILON)
    return center * inv_std, inv_std


def norm_back(grad_normed, normal_part, inv_std, gain_row):
    grad_hat = grad_normed * gain_row
    mean_one = jnp.mean(grad_hat, axis=-1, keepdims=True)
    mean_two = jnp.mean(grad_hat * normal_part, axis=-1, keepdims=True)
    return inv_std * (grad_hat - mean_one - normal_part * mean_two)


def transposed_tail(w_ref):
    eye = (
        lax.broadcasted_iota(jnp.int32, (LANES, LANES), 0)
        == lax.broadcasted_iota(jnp.int32, (LANES, LANES), 1)
    )
    eye = jnp.where(eye, 1.0, 0.0).astype(BF)
    return dot(eye, w_ref[:, RV_AT:PACK], NT)


def vector_row(rows_t, first, index):
    return rows_t[first + index : first + index + 1, :]


def split_two(values):
    high = values.astype(BF)
    return high, (values - high.astype(F32)).astype(BF)


def slots_kernel(experts, capacity, meta_ref, cot_ref, rank_ref, rank_t_ref, slots_ref):
    tok = cot_ref.shape[0]
    tri = lax.broadcasted_iota(jnp.int32, (BLOCK, BLOCK), 0) >= lax.broadcasted_iota(
        jnp.int32, (BLOCK, BLOCK), 1
    )
    tri = jnp.where(tri, 1.0, 0.0).astype(BF)
    carry = jnp.zeros((1, LANES), F32)
    lane = lane_ids(BLOCK)
    for b in range(tok // BLOCK):
        rows = slice(b * BLOCK, (b + 1) * BLOCK)
        meta = meta_ref[rows, :]
        pick = ((lane == meta[:, 4:5]) | (lane == meta[:, 5:6])) & (meta[:, 6:7] >= STEP)
        ones = jnp.where(pick, 1.0, 0.0)
        count = dot(tri, ones.astype(BF)) + carry
        carry = count[BLOCK - 1 :, :]
        rank_ref[rows, :] = jnp.where(pick, count - 1.0, -1.0)
    rank_t_ref[...] = jnp.transpose(rank_ref[...]).astype(jnp.int32)

    def gather(e, _):
        slots_ref[e] = dot(one_hot(rank_t_ref, e, capacity), cot_ref[...]).astype(BF)
        return 0

    lax.fori_loop(0, experts, gather, 0)


def one_hot(rank_t_ref, e, capacity):
    row = rank_t_ref[pl.ds(e, 1), :]
    place = lax.broadcasted_iota(jnp.int32, (capacity, row.shape[1]), 0)
    return jnp.where(place == row, 1.0, 0.0).astype(BF)


def select_heads(values, route, lane_half):
    shifted = route - lane_half
    acc = jnp.zeros((values.shape[0], LANES), F32)
    for p in range(PAIRS):
        acc = jnp.where(shifted == 2 * p, values[:, p * LANES : (p + 1) * LANES], acc)
    return acc + pltpu.roll(acc, HEAD, 1)


def spread_heads(pairs, meta, lane, lane_half, store):
    doubled, shifted = [], []
    for k in range(A_TOP):
        half = (lane >= HEAD) if k % 2 else (lane < HEAD)
        part = jnp.where(half, pairs[k // 2], 0.0)
        doubled.append(part + pltpu.roll(part, HEAD, 1))
        shifted.append(meta[:, k : k + 1] - lane_half)
    for p in range(PAIRS):
        acc = jnp.zeros(doubled[0].shape, F32)
        for k in range(A_TOP):
            acc = jnp.where(shifted[k] == 2 * p, doubled[k], acc)
        store(p, acc.astype(BF))


def attend_kernel(
    experts,
    capacity,
    tok_ref,
    w_ref,
    meta_ref,
    rank_t_ref,
    slotq_ref,
    kv_ref,
    so_ref,
    lse_ref,
    gates_ref,
    mixed_ref,
    hidden_ref,
    fgate_ref,
    slots_ref,
    kx_ref,
    vx_ref,
    n2_ref,
):
    tok = tok_ref.shape[0]
    first = A_EXP + experts
    rows_t = transposed_tail(w_ref)
    gain_one, shift_one, gain_two, shift_two = (vector_row(rows_t, first, i) for i in range(4))
    lane = lane_ids(BLOCK)
    upper = lane >= HEAD
    lane_half = jnp.where(upper, 1, 0)

    def project(b, _):
        rows = pl.ds(b * BLOCK, BLOCK)
        meta = meta_ref[rows, :]
        hat, _inv = norm_stats(tok_ref[rows, :].astype(F32))
        normed = (hat * gain_one + shift_one).astype(BF)
        queries = dot(normed, w_ref[:, :WIDTH])
        kv = dot(normed, w_ref[:, KV_AT:RV_AT])
        logits = dot(normed, w_ref[:, RV_AT:PACK])
        kv_ref[rows, :] = kv.astype(BF)
        swapped = pltpu.roll(kv, HEAD, 1)
        kx_ref[0, rows, :] = jnp.where(upper, 0.0, kv).astype(BF)
        kx_ref[1, rows, :] = jnp.where(upper, swapped, 0.0).astype(BF)
        vx_ref[0, rows, :] = jnp.where(upper, 0.0, swapped).astype(BF)
        vx_ref[1, rows, :] = jnp.where(upper, kv, 0.0).astype(BF)
        picked = [select_heads(queries, meta[:, k : k + 1], lane_half) for k in range(A_TOP)]
        for j in range(A_TOP // 2):
            slotq_ref[j, rows, :] = jnp.where(upper, picked[2 * j + 1], picked[2 * j]).astype(BF)
        chosen = [
            jnp.sum(jnp.where(lane == meta[:, k : k + 1], logits, 0.0), axis=1, keepdims=True)
            for k in range(A_TOP)
        ]
        top = jnp.maximum(jnp.maximum(chosen[0], chosen[1]), jnp.maximum(chosen[2], chosen[3]))
        raised = [jnp.exp(c - top) for c in chosen]
        scale = 1.0 / (raised[0] + raised[1] + raised[2] + raised[3])
        gates = jnp.zeros((BLOCK, LANES), F32)
        for k in range(A_TOP):
            gates = jnp.where(lane == k, raised[k] * scale, gates)
        gates_ref[rows, :] = gates
        return 0

    lax.fori_loop(0, tok // BLOCK, project, 0)

    below = lax.broadcasted_iota(jnp.int32, (BLOCK, BLOCK), 1) <= lax.broadcasted_iota(
        jnp.int32, (BLOCK, BLOCK), 0
    )
    for i in range(tok // BLOCK):
        rows = slice(i * BLOCK, (i + 1) * BLOCK)
        seen = (i + 1) * BLOCK
        lse_ref[rows, :] = jnp.zeros((BLOCK, LANES), F32)

        def pair(j, _, rows=rows, seen=seen, i=i):
            out = jnp.zeros((BLOCK, LANES), F32)
            query = slotq_ref[j, rows, :]
            logs = lse_ref[rows, :]
            for h in range(2):
                scores = dot(query, kx_ref[h, :seen, :], NT) * (HEAD**-0.5)
                last = jnp.where(below, scores[:, i * BLOCK :], NEG)
                scores = last if i == 0 else jnp.concatenate([scores[:, : i * BLOCK], last], axis=1)
                top = jnp.max(scores, axis=1, keepdims=True)
                raised = jnp.exp(scores - top)
                total = jnp.sum(raised, axis=1, keepdims=True)
                probs = (raised * (1.0 / total)).astype(BF)
                out = out + dot(probs, vx_ref[h, :seen, :])
                logs = jnp.where(lane == 2 * j + h, top + jnp.log(total), logs)
            so_ref[j, rows, :] = out
            lse_ref[rows, :] = logs
            return 0

        lax.fori_loop(0, A_TOP // 2, pair, 0)

    def finish(b, _):
        rows = pl.ds(b * BLOCK, BLOCK)
        meta = meta_ref[rows, :]
        gates = gates_ref[rows, :]
        active = jnp.where(meta[:, 6:7] >= STEP, 1.0, 0.0)
        pairs = [
            so_ref[j, rows, :]
            * jnp.where(upper, gates[:, 2 * j + 1 : 2 * j + 2], gates[:, 2 * j : 2 * j + 1])
            for j in range(A_TOP // 2)
        ]

        def store(p, block):
            mixed_ref[rows, p * LANES : (p + 1) * LANES] = block

        spread_heads(pairs, meta, lane, lane_half, store)
        branch = dot(mixed_ref[rows, :], w_ref[:, WIDTH:KV_AT], NT)
        hidden = tok_ref[rows, :].astype(F32) + active * branch
        hidden_ref[rows, :] = hidden
        hat, _inv = norm_stats(hidden)
        normed = (hat * gain_two + shift_two).astype(BF)
        n2_ref[rows, :] = normed
        logits = pltpu.roll(dot(normed, w_ref[:, RV_AT:PACK]), LANES - A_EXP, 1)
        named = (lane == meta[:, 4:5]) | (lane == meta[:, 5:6])
        top = jnp.max(jnp.where(named, logits, NEG), axis=1, keepdims=True)
        raised = jnp.where(named, jnp.exp(jnp.where(named, logits, NEG) - top), 0.0)
        fgate_ref[rows, :] = raised * (1.0 / jnp.sum(raised, axis=1, keepdims=True))
        return 0

    lax.fori_loop(0, tok // BLOCK, finish, 0)

    def gather(e, _):
        slots_ref[e] = dot(one_hot(rank_t_ref, e, capacity), n2_ref[...]).astype(BF)
        return 0

    lax.fori_loop(0, experts, gather, 0)


def expert_kernel(parts, x_ref, up_ref, down_ref, out_ref, act_ref, slope_ref):
    width = up_ref.shape[2]
    rows = x_ref[...]

    def part(c, total):
        pre = dot(rows, up_ref[c])
        size = jnp.abs(pre)
        bell = jnp.exp(pre * pre * -0.5)
        inv = 1.0 / (1.0 + TAIL_P * size)
        tail = TAIL[-1] * inv
        for coef in TAIL[-2::-1]:
            tail = (tail + coef) * inv
        tail = tail * bell
        phi = jnp.where(pre >= 0.0, 1.0 - tail, tail)
        act = (pre * phi).astype(BF)
        act_ref[c] = act
        slope_ref[c] = (phi + pre * bell * 0.3989422804014327).astype(BF)
        return total + dot(act, down_ref[c])

    total = part(0, jnp.zeros(out_ref.shape, F32))
    for c in range(1, parts):
        total = part(c, total)
    out_ref[...] = total.astype(BF)


def combine_kernel(
    experts,
    capacity,
    back_ref,
    rank_ref,
    rank_t_ref,
    hidden_ref,
    w_ref,
    meta_ref,
    fgate_ref,
    scal_ref,
    cot_ref,
    out_ref,
    halt_ref,
    slope_ref,
    glf_ref,
    row_ref,
    ab_ref,
    cols_ref,
):
    tok = hidden_ref.shape[0]
    rows_t = transposed_tail(w_ref)
    halt_row = vector_row(rows_t, A_EXP + experts, 4)
    lane = lane_ids(BLOCK)
    row_ref[...] = jnp.zeros(row_ref.shape, F32)

    def block(b, _):
        rows = pl.ds(b * BLOCK, BLOCK)
        meta = meta_ref[rows, :]
        rank = rank_ref[rows, :].astype(jnp.int32)
        fgate = fgate_ref[rows, :]
        scal = scal_ref[rows, :]
        active = jnp.where(meta[:, 6:7] >= STEP, 1.0, 0.0)
        cot = cot_ref[rows, :].astype(F32)
        place = lax.broadcasted_iota(jnp.int32, (BLOCK, capacity), 1)
        branch = jnp.zeros((BLOCK, D), F32)
        with_cot = jnp.zeros((BLOCK, LANES), F32)
        with_row = jnp.zeros((BLOCK, LANES), F32)
        for e in range(experts):
            hot = jnp.where(place == rank[:, e : e + 1], 1.0, 0.0).astype(BF)
            came = dot(hot, back_ref[e])
            branch = branch + fgate[:, e : e + 1] * came
            with_cot = jnp.where(lane == e, jnp.sum(came * cot, axis=1, keepdims=True), with_cot)
            with_row = jnp.where(
                lane == e, jnp.sum(came * halt_row, axis=1, keepdims=True), with_row
            )
        z = hidden_ref[rows, :] + active * branch
        out_ref[rows, :] = z.astype(BF)
        prob = 1.0 / (1.0 + jnp.exp(-jnp.sum(z * halt_row, axis=1, keepdims=True)))
        halt_in, cot_halt = scal[:, 0:1], scal[:, 1:2]
        room = active * (1.0 - halt_in) * prob
        slope = cot_halt * room * (1.0 - prob)
        halt_ref[rows, :] = jnp.broadcast_to(halt_in + room, (BLOCK, LANES))
        slope_ref[rows, :] = jnp.broadcast_to(slope, (BLOCK, LANES))
        row_ref[0:1, :] += jnp.sum(slope * z, axis=0, keepdims=True)
        gfg = active * (with_cot + slope * with_row)
        inner = jnp.sum(fgate * gfg, axis=1, keepdims=True)
        glf_ref[rows, :] = pltpu.roll(fgate * (gfg - inner), A_EXP, 1)
        live = active * fgate
        bent = live * slope
        for index, part in enumerate((live, bent)):
            high = part.astype(BF)
            rest = part - high.astype(F32)
            middle = rest.astype(BF)
            cols_ref[3 * index, rows, :] = high
            cols_ref[3 * index + 1, rows, :] = middle
            cols_ref[3 * index + 2, rows, :] = (rest - middle.astype(F32)).astype(BF)
        return 0

    lax.fori_loop(0, tok // BLOCK, block, 0)
    turned = [jnp.transpose(cols_ref[i].astype(F32)) for i in range(6)]
    for e in range(experts):
        rows = jnp.concatenate(
            [t[e : e + 1, :] for t in turned] + [jnp.zeros((2, tok), F32)], axis=0
        )
        ab_ref[e] = dot(rows.astype(BF), one_hot(rank_t_ref, e, capacity), NT).astype(BF)


def data_back_kernel(
    experts, parts, cot_ref, ab_ref, tail_ref, slope_ref, up_ref, down_ref, gpre_ref, gy_ref, rows_ref
):
    rows = cot_ref.shape[0]
    eye = (
        lax.broadcasted_iota(jnp.int32, (LANES, LANES), 0)
        == lax.broadcasted_iota(jnp.int32, (LANES, LANES), 1)
    )
    rows_t = dot(jnp.where(eye, 1.0, 0.0).astype(BF), tail_ref[...], NT)
    halt_row = vector_row(rows_t, A_EXP + experts, 4)
    ab = ab_ref[0].astype(F32)
    live = ab[0:1, :] + ab[1:2, :] + ab[2:3, :]
    bent = ab[3:4, :] + ab[4:5, :] + ab[5:6, :]
    cols = jnp.transpose(jnp.concatenate([live, bent, jnp.zeros((LANES - 2, rows), F32)], axis=0))
    gy = (cols[:, 0:1] * cot_ref[...].astype(F32) + cols[:, 1:2] * halt_row).astype(BF)
    gy_ref[...] = gy
    total = jnp.zeros((rows, D), F32)
    for c in range(parts):
        gpre = (dot(gy, down_ref[c], NT) * slope_ref[c].astype(F32)).astype(BF)
        gpre_ref[c] = gpre
        total = total + dot(gpre, up_ref[c], NT)
    rows_ref[...] = total.astype(BF)


def weight_back_kernel(parts, x_ref, gy_ref, gpre_ref, act_ref, gup_ref, gdown_ref, up_acc, down_acc):
    step = pl.program_id(0)

    @pl.when(step == 0)
    def _():
        up_acc[...] = jnp.zeros(up_acc.shape, F32)
        down_acc[...] = jnp.zeros(down_acc.shape, F32)

    for c in range(parts):
        up_acc[c] += dot(x_ref[...], gpre_ref[c], TN)
        down_acc[c] += dot(gy_ref[...], act_ref[c], TN)

    @pl.when(step == pl.num_programs(0) - 1)
    def _():
        for c in range(parts):
            gup_ref[c] = up_acc[c].astype(BF)
            gdown_ref[c] = jnp.transpose(down_acc[c]).astype(BF)


def attend_back_kernel(
    experts,
    capacity,
    back_ref,
    rank_ref,
    hidden_ref,
    tok_ref,
    w_ref,
    meta_ref,
    cot_ref,
    slope_ref,
    glf_ref,
    row_ref,
    mixed_ref,
    so_ref,
    lse_ref,
    gates_ref,
    slotq_ref,
    kv_ref,
    gin_ref,
    pack_ref,
    gh_ref,
    n1_ref,
    gx_ref,
    gslot_ref,
    gla_ref,
    wide_ref,
    acc_ref,
    rv_ref,
    vec_ref,
    kx_ref,
    vx_ref,
    lset_ref,
    gq_ref,
):
    tok = hidden_ref.shape[0]
    blocks = tok // BLOCK
    first = A_EXP + experts
    rows_t = transposed_tail(w_ref)
    low_t = rows_t.astype(BF)
    gain_one, shift_one, gain_two, shift_two, halt_row = (
        vector_row(rows_t, first, i) for i in range(5)
    )
    lane = lane_ids(BLOCK)
    upper = lane >= HEAD
    lane_half = jnp.where(upper, 1, 0)
    vec_ref[...] = jnp.zeros(vec_ref.shape, F32)
    vec_ref[4:5, :] = row_ref[0:1, :]
    acc_ref[...] = jnp.zeros(acc_ref.shape, F32)
    rv_ref[...] = jnp.zeros(rv_ref.shape, F32)

    def hidden_back(b, _):
        rows = pl.ds(b * BLOCK, BLOCK)
        meta = meta_ref[rows, :]
        rank = rank_ref[rows, :].astype(jnp.int32)
        active = jnp.where(meta[:, 6:7] >= STEP, 1.0, 0.0)
        place = lax.broadcasted_iota(jnp.int32, (BLOCK, capacity), 1)
        glf_high, glf_low = split_two(glf_ref[rows, :])
        grad = dot(glf_high, low_t) + dot(glf_low, low_t)
        for e in range(experts):
            hot = jnp.where(place == rank[:, e : e + 1], 1.0, 0.0).astype(BF)
            grad = grad + dot(hot, back_ref[e])
        hat, inv = norm_stats(hidden_ref[rows, :])
        normed = (hat * gain_two + shift_two).astype(BF)
        rv_ref[...] += dot(normed, glf_high, TN) + dot(normed, glf_low, TN)
        vec_ref[2:3, :] += jnp.sum(grad * hat, axis=0, keepdims=True)
        vec_ref[3:4, :] += jnp.sum(grad, axis=0, keepdims=True)
        gz = cot_ref[rows, :].astype(F32) + slope_ref[rows, 0:1] * halt_row
        gh = gz + norm_back(grad, hat, inv, gain_two)
        gh_ref[rows, :] = gh
        ga = (active * gh).astype(BF)
        acc_ref[...] += dot(ga, mixed_ref[rows, :], TN)
        gm = dot(ga, w_ref[:, WIDTH:KV_AT])
        gates = gates_ref[rows, :]
        weighted = jnp.zeros((BLOCK, 1), F32)
        grads = []
        picked = [select_heads(gm, meta[:, k : k + 1], lane_half) for k in range(A_TOP)]
        for j in range(A_TOP // 2):
            both = jnp.where(upper, picked[2 * j + 1], picked[2 * j])
            prod = both * so_ref[j, rows, :]
            scale = jnp.where(upper, gates[:, 2 * j + 1 : 2 * j + 2], gates[:, 2 * j : 2 * j + 1])
            gslot_ref[j, rows, :] = (both * scale).astype(BF)
            grads.append(jnp.sum(jnp.where(upper, 0.0, prod), axis=1, keepdims=True))
            grads.append(jnp.sum(jnp.where(upper, prod, 0.0), axis=1, keepdims=True))
        for k in range(A_TOP):
            weighted = weighted + gates[:, k : k + 1] * grads[k]
        gla = jnp.zeros((BLOCK, LANES), F32)
        for k in range(A_TOP):
            value = gates[:, k : k + 1] * (grads[k] - weighted)
            gla = jnp.where(lane == meta[:, k : k + 1], value, gla)
        gla_ref[rows, :] = gla
        kv = kv_ref[rows, :].astype(F32)
        swapped = pltpu.roll(kv, HEAD, 1)
        kx_ref[0, rows, :] = jnp.where(upper, 0.0, kv).astype(BF)
        kx_ref[1, rows, :] = jnp.where(upper, swapped, 0.0).astype(BF)
        vx_ref[0, rows, :] = jnp.where(upper, 0.0, swapped).astype(BF)
        vx_ref[1, rows, :] = jnp.where(upper, kv, 0.0).astype(BF)
        return 0

    lax.fori_loop(0, blocks, hidden_back, 0)
    pack_ref[:, WIDTH:KV_AT] = acc_ref[...].astype(BF)
    lset_ref[...] = jnp.transpose(lse_ref[...])

    above = lax.broadcasted_iota(jnp.int32, (BLOCK, BLOCK), 0) <= lax.broadcasted_iota(
        jnp.int32, (BLOCK, BLOCK), 1
    )
    gx_ref[...] = jnp.zeros(gx_ref.shape, F32)
    for i in range(blocks):
        rows = slice(i * BLOCK, (i + 1) * BLOCK)
        seen = (i + 1) * BLOCK

        def pair(j, _, rows=rows, seen=seen, i=i):
            query = slotq_ref[j, rows, :]
            gslot = gslot_ref[j, rows, :]
            gq = jnp.zeros((BLOCK, LANES), F32)
            for h in range(2):
                keys = kx_ref[h, :seen, :]
                log = lset_ref[pl.ds(2 * j + h, 1), rows]
                scores = dot(keys, query, NT) * (HEAD**-0.5) - log
                last = jnp.where(above, scores[i * BLOCK :, :], NEG)
                scores = last if i == 0 else jnp.concatenate([scores[: i * BLOCK], last], axis=0)
                probs = jnp.exp(scores)
                gprob = dot(vx_ref[h, :seen, :], gslot, NT)
                inner = jnp.sum(probs * gprob, axis=0, keepdims=True)
                gs = (probs * (gprob - inner) * (HEAD**-0.5)).astype(BF)
                gq = gq + dot(gs, keys, TN)
                gx_ref[0, h, :seen, :] += dot(gs, query)
                gx_ref[1, h, :seen, :] += dot(probs.astype(BF), gslot)
            gq_ref[j, rows, :] = gq
            return 0

        lax.fori_loop(0, A_TOP // 2, pair, 0)

    acc_ref[...] = jnp.zeros(acc_ref.shape, F32)

    def input_back(b, gkv_sum):
        rows = pl.ds(b * BLOCK, BLOCK)
        meta = meta_ref[rows, :]
        pairs = [gq_ref[j, rows, :] for j in range(A_TOP // 2)]

        def store(p, block):
            wide_ref[:, p * LANES : (p + 1) * LANES] = block

        spread_heads(pairs, meta, lane, lane_half, store)
        gkeys = gx_ref[0, 0, rows, :] + pltpu.roll(gx_ref[0, 1, rows, :], HEAD, 1)
        gvals = pltpu.roll(gx_ref[1, 0, rows, :], HEAD, 1) + gx_ref[1, 1, rows, :]
        gkv = jnp.where(upper, gvals, gkeys).astype(BF)
        gla_high, gla_low = split_two(gla_ref[rows, :])
        grad = dot(wide_ref[...], w_ref[:, :WIDTH], NT)
        grad = grad + dot(gkv, w_ref[:, KV_AT:RV_AT], NT)
        grad = grad + dot(gla_high, low_t) + dot(gla_low, low_t)
        hat, inv = norm_stats(tok_ref[rows, :].astype(F32))
        normed = (hat * gain_one + shift_one).astype(BF)
        acc_ref[...] += dot(normed, wide_ref[...], TN)
        rv_ref[...] += dot(normed, gla_high, TN) + dot(normed, gla_low, TN)
        vec_ref[0:1, :] += jnp.sum(grad * hat, axis=0, keepdims=True)
        vec_ref[1:2, :] += jnp.sum(grad, axis=0, keepdims=True)
        gin_ref[rows, :] = (gh_ref[rows, :] + norm_back(grad, hat, inv, gain_one)).astype(BF)
        return gkv_sum + dot(normed, gkv, TN)

    gkv_sum = lax.fori_loop(0, blocks, input_back, jnp.zeros((D, LANES), F32))
    pack_ref[:, :WIDTH] = acc_ref[...].astype(BF)
    pack_ref[:, KV_AT:RV_AT] = gkv_sum.astype(BF)
    turned = jnp.transpose(vec_ref[...])
    turned = pltpu.roll(turned, first, 1)
    wide_lane = lane_ids(D)
    tail = jnp.where(wide_lane < first, rv_ref[...], turned)
    pack_ref[:, RV_AT:PACK] = tail.astype(BF)


VMEM_LIMIT = 60 * 1024 * 1024


def whole(shape, dtype):
    return jax.ShapeDtypeStruct(shape, dtype)


def in_vmem(count):
    return [pl.BlockSpec(memory_space=pltpu.VMEM)] * count


def call(kernel, name, inputs, outs, scratch=()):
    return pl.pallas_call(
        kernel,
        name=name,
        out_shape=outs,
        in_specs=in_vmem(len(inputs)),
        out_specs=in_vmem(len(outs)),
        scratch_shapes=list(scratch),
        compiler_params=pltpu.CompilerParams(vmem_limit_bytes=VMEM_LIMIT),
    )(*inputs)


def constant_spec(shape):
    return pl.BlockSpec(shape, lambda s: (0,) * len(shape), pipeline_mode=pl.Buffered(1))


def on_device(
    tokens,
    halt_in,
    depths,
    attn_routes,
    ffn_routes,
    w_query,
    w_out,
    w_kv,
    router,
    vectors,
    w_up,
    w_down,
    cot_out,
    cot_halt,
):
    tok = tokens.shape[0]
    groups, experts = lax.axis_size("dp"), lax.axis_size("fsdp")
    capacity = 2 * F_TOP * tok // experts
    slice_width = w_up.shape[2]
    shard = w_query.shape[0]
    slots = experts * capacity

    tail = jnp.concatenate([router, vectors.T], axis=1)
    tail = jnp.pad(tail, ((0, 0), (0, LANES - tail.shape[1])))
    pack = jnp.concatenate([w_query, w_out.T, w_kv, tail], axis=1)
    pack = lax.all_gather(pack, "dp", axis=0, tiled=False)
    pack = lax.all_gather(pack, "fsdp", axis=0, tiled=False)
    weights = pack.transpose(1, 0, 2, 3).reshape(D, PACK)
    whole_up = lax.all_gather(w_up[0], "dp", axis=0, tiled=False)
    whole_down = lax.all_gather(w_down[0], "dp", axis=0, tiled=False)

    meta = jnp.concatenate([attn_routes, ffn_routes, depths[:, None], depths[:, None]], axis=1)
    scal = jnp.stack([halt_in, cot_halt], axis=1)

    rank, rank_t, cot_slots = call(
        partial(slots_kernel, experts, capacity),
        "slots",
        (meta, cot_out),
        (
            whole((tok, LANES), F32),
            whole((LANES, tok), jnp.int32),
            whole((experts, capacity, D), BF),
        ),
    )

    slotq, kv, so, lse, gates, mixed, hidden, fgate, n2_slots = call(
        partial(attend_kernel, experts, capacity),
        "attend",
        (tokens, weights, meta, rank_t),
        (
            whole((2, tok, LANES), BF),
            whole((tok, LANES), BF),
            whole((2, tok, LANES), F32),
            whole((tok, LANES), F32),
            whole((tok, LANES), F32),
            whole((tok, WIDTH), BF),
            whole((tok, D), F32),
            whole((tok, LANES), F32),
            whole((experts, capacity, D), BF),
        ),
        (
            pltpu.VMEM((2, tok, LANES), BF),
            pltpu.VMEM((2, tok, LANES), BF),
            pltpu.VMEM((tok, D), BF),
        ),
    )

    def exchange(values):
        return lax.all_to_all(values, "fsdp", split_axis=0, concat_axis=0, tiled=True)

    owned_cot = exchange(cot_slots).reshape(slots, D)
    owned = exchange(n2_slots).reshape(slots, D)

    row_spec = pl.BlockSpec((capacity, D), lambda s: (s, 0))
    wide_spec = pl.BlockSpec((groups, capacity, slice_width), lambda s: (0, s, 0))
    up_spec = constant_spec((groups, D, slice_width))
    down_spec = constant_spec((groups, slice_width, D))
    params = pltpu.CompilerParams(vmem_limit_bytes=VMEM_LIMIT)
    wide = whole((groups, slots, slice_width), BF)
    owned_out, act, slope = pl.pallas_call(
        partial(expert_kernel, groups),
        name="expert",
        grid=(experts,),
        out_shape=(whole((slots, D), BF), wide, wide),
        in_specs=[row_spec, up_spec, down_spec],
        out_specs=[row_spec, wide_spec, wide_spec],
        compiler_params=params,
    )(owned, whole_up, whole_down)

    back = exchange(owned_out.reshape(experts, capacity, D))
    block_out, halt_wide, halt_slope, glf, halt_grad, ab = call(
        partial(combine_kernel, experts, capacity),
        "combine",
        (back, rank, rank_t, hidden, weights, meta, fgate, scal, cot_out),
        (
            whole((tok, D), BF),
            whole((tok, LANES), F32),
            whole((tok, LANES), F32),
            whole((tok, LANES), F32),
            whole((8, D), F32),
            whole((experts, 8, capacity), BF),
        ),
        (pltpu.VMEM((6, tok, LANES), BF),),
    )
    halt_out = halt_wide[:, 0]
    owned_ab = exchange(ab)

    gpre, gy, owned_rows = pl.pallas_call(
        partial(data_back_kernel, experts, groups),
        name="data_back",
        grid=(experts,),
        out_shape=(wide, whole((slots, D), BF), whole((slots, D), BF)),
        in_specs=[
            row_spec,
            pl.BlockSpec((1, 8, capacity), lambda s: (s, 0, 0)),
            pl.BlockSpec((D, LANES), lambda s: (0, RV_AT // LANES)),
            wide_spec,
            up_spec,
            down_spec,
        ],
        out_specs=[wide_spec, row_spec, row_spec],
        compiler_params=params,
    )(owned_cot, owned_ab, weights, slope, whole_up, whole_down)
    rows_back = exchange(owned_rows.reshape(experts, capacity, D))

    grad_up, grad_down = pl.pallas_call(
        partial(weight_back_kernel, groups),
        name="weight_back",
        grid=(experts,),
        out_shape=(whole((groups, D, slice_width), BF), whole((groups, slice_width, D), BF)),
        in_specs=[row_spec, row_spec, wide_spec, wide_spec],
        out_specs=[constant_spec((groups, D, slice_width)), constant_spec((groups, slice_width, D))],
        scratch_shapes=[
            pltpu.VMEM((groups, D, slice_width), F32),
            pltpu.VMEM((groups, D, slice_width), F32),
        ],
        compiler_params=params,
    )(owned, gy, gpre, act)
    part_up = lax.psum_scatter(grad_up, "dp", scatter_dimension=0, tiled=True).astype(F32)
    part_down = lax.psum_scatter(grad_down, "dp", scatter_dimension=0, tiled=True).astype(F32)

    grad_in, grads = call(
        partial(attend_back_kernel, experts, capacity),
        "attend_back",
        (
            rows_back,
            rank,
            hidden,
            tokens,
            weights,
            meta,
            cot_out,
            halt_slope,
            glf,
            halt_grad,
            mixed,
            so,
            lse,
            gates,
            slotq,
            kv,
        ),
        (whole((tok, D), BF), whole((D, PACK), BF)),
        (
            pltpu.VMEM((tok, D), F32),
            pltpu.VMEM((8, LANES), F32),
            pltpu.VMEM((2, 2, tok, LANES), F32),
            pltpu.VMEM((2, tok, LANES), BF),
            pltpu.VMEM((tok, LANES), F32),
            pltpu.VMEM((BLOCK, WIDTH), BF),
            pltpu.VMEM((D, WIDTH), F32),
            pltpu.VMEM((D, LANES), F32),
            pltpu.VMEM((LANES, D), F32),
            pltpu.VMEM((2, tok, LANES), BF),
            pltpu.VMEM((2, tok, LANES), BF),
            pltpu.VMEM((LANES, tok), F32),
            pltpu.VMEM((2, tok, LANES), F32),
        ),
    )

    sent = grads.reshape(groups, experts, shard, PACK).transpose(1, 0, 2, 3)
    came = exchange(sent)
    half = jnp.sum(came.astype(F32), axis=0).astype(BF)
    came = lax.all_to_all(half, "dp", split_axis=0, concat_axis=0, tiled=True)
    total = jnp.sum(came.astype(F32), axis=0)
    routers = A_EXP + experts
    return (
        block_out,
        halt_out,
        grad_in,
        total[:, :WIDTH],
        total[:, WIDTH:KV_AT].T,
        total[:, KV_AT:RV_AT],
        total[:, RV_AT : RV_AT + routers],
        total[:, RV_AT + routers : RV_AT + routers + 5].T,
        part_up,
        part_down,
    )


def solution(mesh):
    both = ("dp", "fsdp")
    placed = (
        P(both, None),
        P(both),
        P(both),
        P(both, None),
        P(both, None),
        P(both, None),
        P(None, both),
        P(both, None),
        P(both, None),
        P(None, both),
        P("fsdp", None, "dp"),
        P("fsdp", "dp", None),
        P(both, None),
        P(both),
    )
    return jax.shard_map(
        on_device,
        mesh=mesh,
        in_specs=placed,
        out_specs=(
            P(both, None),
            P(both),
            P(both, None),
            P(both, None),
            P(None, both),
            P(both, None),
            P(both, None),
            P(None, both),
            P("fsdp", None, "dp"),
            P("fsdp", "dp", None),
        ),
        check_vma=False,
    )
```

```python
from functools import partial

import jax
import jax.numpy as jnp
from jax import lax
from jax.experimental import pallas as pl
from jax.experimental.pallas import tpu as pltpu
from jax.sharding import PartitionSpec as P


D = 512
HEAD = 64
A_EXP = 24
A_TOP = 4
F_TOP = 2
STEP = 2
LANES = 128
BLOCK = 256
HALVES = 2
PAIRS = A_EXP // 2
WIDTH = A_EXP * HEAD
KV_AT = 2 * WIDTH
RV_AT = KV_AT + LANES
PACK = RV_AT + LANES
EPSILON = 1e-05
NEG = -1e30
BF = jnp.bfloat16
F32 = jnp.float32

NN = (((1,), (0,)), ((), ()))
NT = (((1,), (1,)), ((), ()))
TN = (((0,), (0,)), ((), ()))

TAIL_P = 0.3
TAIL = (
    0.11962930113077164,
    0.1207539290189743,
    0.09991367161273956,
    0.12856101989746094,
    -0.053682513535022736,
    0.20635227859020233,
    -0.15720237791538239,
    0.03567460551857948,
)


def dot(a, b, dims=NN):
    return lax.dot_general(a, b, dims, preferred_element_type=F32)


def lane_ids(rows):
    return lax.broadcasted_iota(jnp.int32, (rows, LANES), 1)


def norm_stats(values):
    center = values - jnp.mean(values, axis=-1, keepdims=True)
    inv_std = lax.rsqrt(jnp.mean(center * center, axis=-1, keepdims=True) + EPSILON)
    return center * inv_std, inv_std


def norm_back(grad_normed, normal_part, inv_std, gain_row):
    grad_hat = grad_normed * gain_row
    mean_one = jnp.mean(grad_hat, axis=-1, keepdims=True)
    mean_two = jnp.mean(grad_hat * normal_part, axis=-1, keepdims=True)
    return inv_std * (grad_hat - mean_one - normal_part * mean_two)


def transposed_tail(w_ref):
    return turned_tail(w_ref[:, RV_AT:PACK])


def turned_tail(tail):
    eye = (
        lax.broadcasted_iota(jnp.int32, (LANES, LANES), 0)
        == lax.broadcasted_iota(jnp.int32, (LANES, LANES), 1)
    )
    eye = jnp.where(eye, 1.0, 0.0).astype(BF)
    return dot(eye, tail, NT)


def vector_row(rows_t, first, index):
    return rows_t[first + index : first + index + 1, :]


def split_two(values):
    high = values.astype(BF)
    return high, (values - high.astype(F32)).astype(BF)


def slots_kernel(experts, capacity, meta_ref, cot_ref, rank_ref, rank_t_ref, *slots_refs):
    tok = cot_ref.shape[0]
    tri = lax.broadcasted_iota(jnp.int32, (BLOCK, BLOCK), 0) >= lax.broadcasted_iota(
        jnp.int32, (BLOCK, BLOCK), 1
    )
    tri = jnp.where(tri, 1.0, 0.0).astype(BF)
    carry = jnp.zeros((1, LANES), F32)
    lane = lane_ids(BLOCK)
    for b in range(tok // BLOCK):
        rows = slice(b * BLOCK, (b + 1) * BLOCK)
        meta = meta_ref[rows, :]
        pick = ((lane == meta[:, 4:5]) | (lane == meta[:, 5:6])) & (meta[:, 6:7] >= STEP)
        ones = jnp.where(pick, 1.0, 0.0)
        count = dot(tri, ones.astype(BF)) + carry
        carry = count[BLOCK - 1 :, :]
        rank_ref[rows, :] = jnp.where(pick, count - 1.0, -1.0)
    rank_t_ref[...] = jnp.transpose(rank_ref[...]).astype(jnp.int32)

    gather_slots(experts, capacity, rank_t_ref, cot_ref, slots_refs)


def gather_slots(experts, capacity, rank_t_ref, rows_ref, slots_refs):
    def gather(e, _):
        for h in range(HALVES):
            hot = one_hot(rank_t_ref, e, capacity, h)
            slots_refs[h][e] = dot(hot, rows_ref[...]).astype(BF)
        return 0

    lax.fori_loop(0, experts, gather, 0)


def one_hot(rank_t_ref, e, capacity, h):
    size = capacity // HALVES
    row = rank_t_ref[pl.ds(e, 1), :] - h * size
    place = lax.broadcasted_iota(jnp.int32, (size, row.shape[1]), 0)
    return jnp.where(place == row, 1.0, 0.0).astype(BF)


def select_heads(values, route, lane_half):
    shifted = route - lane_half
    acc = jnp.zeros((values.shape[0], LANES), F32)
    for p in range(PAIRS):
        acc = jnp.where(shifted == 2 * p, values[:, p * LANES : (p + 1) * LANES], acc)
    return acc + pltpu.roll(acc, HEAD, 1)


def spread_heads(pairs, meta, lane, lane_half, store):
    doubled, shifted = [], []
    for k in range(A_TOP):
        half = (lane >= HEAD) if k % 2 else (lane < HEAD)
        part = jnp.where(half, pairs[k // 2], 0.0)
        doubled.append(part + pltpu.roll(part, HEAD, 1))
        shifted.append(meta[:, k : k + 1] - lane_half)
    for p in range(PAIRS):
        acc = jnp.zeros(doubled[0].shape, F32)
        for k in range(A_TOP):
            acc = jnp.where(shifted[k] == 2 * p, doubled[k], acc)
        store(p, acc.astype(BF))


def place_pieces(shape, pieces, w_ref):
    groups, experts, shard = shape
    if len(pieces) == 1:
        w_ref[...] = pieces[0][...]
        return
    mine, group = lax.axis_index("fsdp"), lax.axis_index("dp")
    for m in range(experts):
        base = jnp.bitwise_xor(mine, m) * shard
        for g in range(groups):
            owner = lax.rem(group + g, groups)
            if m < 6:
                block = pieces[m][g]
            else:
                low, high = pieces[6 + 2 * (m - 6)], pieces[7 + 2 * (m - 6)]
                block = low[g] if g < groups // 2 else high[g - groups // 2]
            rows = pl.ds(pl.multiple_of(owner * experts * shard + base, shard), shard)
            w_ref[rows, :] = block


def attend_kernel(experts, capacity, shape, *refs):
    tok_ref, meta_ref, rank_t_ref = refs[:3]
    slots_refs, refs = refs[-3 - HALVES : -3], refs[3 : -3 - HALVES] + refs[-3:]
    pieces, refs = refs[:-12], refs[-12:]
    w_ref, slotq_ref, kv_ref, so_ref, lse_ref, gates_ref, mixed_ref, hidden_ref, fgate_ref = refs[:9]
    kx_ref, vx_ref, n2_ref = refs[9:]
    place_pieces(shape, pieces, w_ref)
    tok = tok_ref.shape[0]
    first = A_EXP + experts
    rows_t = transposed_tail(w_ref)
    gain_one, shift_one, gain_two, shift_two = (vector_row(rows_t, first, i) for i in range(4))
    lane = lane_ids(BLOCK)
    upper = lane >= HEAD
    lane_half = jnp.where(upper, 1, 0)

    def project(b, _):
        rows = pl.ds(b * BLOCK, BLOCK)
        meta = meta_ref[rows, :]
        hat, _ = norm_stats(tok_ref[rows, :].astype(F32))
        normed = (hat * gain_one + shift_one).astype(BF)
        queries = dot(normed, w_ref[:, :WIDTH])
        kv = dot(normed, w_ref[:, KV_AT:RV_AT])
        logits = dot(normed, w_ref[:, RV_AT:PACK])
        kv_ref[rows, :] = kv.astype(BF)
        swapped = pltpu.roll(kv, HEAD, 1)
        kx_ref[0, rows, :] = jnp.where(upper, 0.0, kv).astype(BF)
        kx_ref[1, rows, :] = jnp.where(upper, swapped, 0.0).astype(BF)
        vx_ref[0, rows, :] = jnp.where(upper, 0.0, swapped).astype(BF)
        vx_ref[1, rows, :] = jnp.where(upper, kv, 0.0).astype(BF)
        picked = [select_heads(queries, meta[:, k : k + 1], lane_half) for k in range(A_TOP)]
        for j in range(A_TOP // 2):
            slotq_ref[j, rows, :] = jnp.where(upper, picked[2 * j + 1], picked[2 * j]).astype(BF)
        chosen = [
            jnp.sum(jnp.where(lane == meta[:, k : k + 1], logits, 0.0), axis=1, keepdims=True)
            for k in range(A_TOP)
        ]
        top = jnp.maximum(jnp.maximum(chosen[0], chosen[1]), jnp.maximum(chosen[2], chosen[3]))
        raised = [jnp.exp(c - top) for c in chosen]
        scale = 1.0 / (raised[0] + raised[1] + raised[2] + raised[3])
        gates = jnp.zeros((BLOCK, LANES), F32)
        for k in range(A_TOP):
            gates = jnp.where(lane == k, raised[k] * scale, gates)
        gates_ref[rows, :] = gates
        return 0

    lax.fori_loop(0, tok // BLOCK, project, 0)

    below = lax.broadcasted_iota(jnp.int32, (BLOCK, BLOCK), 1) <= lax.broadcasted_iota(
        jnp.int32, (BLOCK, BLOCK), 0
    )
    for i in range(tok // BLOCK):
        rows = slice(i * BLOCK, (i + 1) * BLOCK)
        seen = (i + 1) * BLOCK
        lse_ref[rows, :] = jnp.zeros((BLOCK, LANES), F32)

        def pair(j, _, rows=rows, seen=seen, i=i):
            out = jnp.zeros((BLOCK, LANES), F32)
            query = slotq_ref[j, rows, :]
            logs = lse_ref[rows, :]
            for h in range(2):
                scores = dot(query, kx_ref[h, :seen, :], NT) * (HEAD**-0.5)
                last = jnp.where(below, scores[:, i * BLOCK :], NEG)
                scores = last if i == 0 else jnp.concatenate([scores[:, : i * BLOCK], last], axis=1)
                top = jnp.max(scores, axis=1, keepdims=True)
                raised = jnp.exp(scores - top)
                total = jnp.sum(raised, axis=1, keepdims=True)
                probs = (raised * (1.0 / total)).astype(BF)
                out = out + dot(probs, vx_ref[h, :seen, :])
                logs = jnp.where(lane == 2 * j + h, top + jnp.log(total), logs)
            so_ref[j, rows, :] = out
            lse_ref[rows, :] = logs
            return 0

        lax.fori_loop(0, A_TOP // 2, pair, 0)

    def finish(b, _):
        rows = pl.ds(b * BLOCK, BLOCK)
        meta = meta_ref[rows, :]
        gates = gates_ref[rows, :]
        active = jnp.where(meta[:, 6:7] >= STEP, 1.0, 0.0)
        pairs = [
            so_ref[j, rows, :]
            * jnp.where(upper, gates[:, 2 * j + 1 : 2 * j + 2], gates[:, 2 * j : 2 * j + 1])
            for j in range(A_TOP // 2)
        ]

        def store(p, block):
            mixed_ref[rows, p * LANES : (p + 1) * LANES] = block

        spread_heads(pairs, meta, lane, lane_half, store)
        branch = dot(mixed_ref[rows, :], w_ref[:, WIDTH:KV_AT], NT)
        hidden = tok_ref[rows, :].astype(F32) + active * branch
        hidden_ref[rows, :] = hidden
        hat, _ = norm_stats(hidden)
        normed = (hat * gain_two + shift_two).astype(BF)
        n2_ref[rows, :] = normed
        logits = pltpu.roll(dot(normed, w_ref[:, RV_AT:PACK]), LANES - A_EXP, 1)
        named = (lane == meta[:, 4:5]) | (lane == meta[:, 5:6])
        top = jnp.max(jnp.where(named, logits, NEG), axis=1, keepdims=True)
        raised = jnp.where(named, jnp.exp(jnp.where(named, logits, NEG) - top), 0.0)
        fgate_ref[rows, :] = raised * (1.0 / jnp.sum(raised, axis=1, keepdims=True))
        return 0

    lax.fori_loop(0, tok // BLOCK, finish, 0)
    gather_slots(experts, capacity, rank_t_ref, n2_ref, slots_refs)


def expert_kernel(parts, x_ref, up_ref, down_ref, out_ref, act_ref, slope_ref):
    rows = x_ref[...]

    def part(c, total):
        pre = dot(rows, up_ref[c])
        size = jnp.abs(pre)
        bell = jnp.exp(pre * pre * -0.5)
        inv = 1.0 / (1.0 + TAIL_P * size)
        tail = TAIL[-1] * inv
        for coef in TAIL[-2::-1]:
            tail = (tail + coef) * inv
        tail = tail * bell
        phi = jnp.where(pre >= 0.0, 1.0 - tail, tail)
        act = (pre * phi).astype(BF)
        act_ref[c] = act
        slope_ref[c] = (phi + pre * bell * 0.3989422804014327).astype(BF)
        return total + dot(act, down_ref[c])

    total = part(0, jnp.zeros(out_ref.shape, F32))
    for c in range(1, parts):
        total = part(c, total)
    out_ref[...] = total.astype(BF)


def combine_sums(experts, capacity, h, rank, back_ref, fgate, cot, halt_row, lane, sums):
    branch, with_cot, with_row = sums
    size = capacity // HALVES
    place = lax.broadcasted_iota(jnp.int32, (BLOCK, size), 1) + h * size
    for e in range(experts):
        hot = jnp.where(place == rank[:, e : e + 1], 1.0, 0.0).astype(BF)
        came = dot(hot, back_ref[e])
        branch = branch + fgate[:, e : e + 1] * came
        one = jnp.sum(came * cot, axis=1, keepdims=True)
        two = jnp.sum(came * halt_row, axis=1, keepdims=True)
        with_cot = with_cot + jnp.where(lane == e, one, 0.0)
        with_row = with_row + jnp.where(lane == e, two, 0.0)
    return branch, with_cot, with_row


def combine_first_kernel(
    experts, capacity, back_ref, rank_ref, tail_ref, fgate_ref, cot_ref, branch_ref, wcot_ref, wrow_ref
):
    halt_row = vector_row(turned_tail(tail_ref[...]), A_EXP + experts, 4)
    lane = lane_ids(BLOCK)

    def block(b, _):
        rows = pl.ds(b * BLOCK, BLOCK)
        rank = rank_ref[rows, :].astype(jnp.int32)
        cot = cot_ref[rows, :].astype(F32)
        zero = jnp.zeros((BLOCK, LANES), F32)
        sums = (jnp.zeros((BLOCK, D), F32), zero, zero)
        sums = combine_sums(
            experts, capacity, 0, rank, back_ref, fgate_ref[rows, :], cot, halt_row, lane, sums
        )
        branch_ref[rows, :], wcot_ref[rows, :], wrow_ref[rows, :] = sums
        return 0

    lax.fori_loop(0, branch_ref.shape[0] // BLOCK, block, 0)


def combine_kernel(
    experts,
    capacity,
    back_ref,
    branch_ref,
    wcot_ref,
    wrow_ref,
    rank_ref,
    rank_t_ref,
    hidden_ref,
    tail_ref,
    meta_ref,
    fgate_ref,
    scal_ref,
    cot_ref,
    out_ref,
    halt_ref,
    slope_ref,
    glf_ref,
    row_ref,
    *rest,
):
    ab_refs, cols_ref = rest[:HALVES], rest[HALVES]
    tok = hidden_ref.shape[0]
    halt_row = vector_row(turned_tail(tail_ref[...]), A_EXP + experts, 4)
    lane = lane_ids(BLOCK)
    row_ref[...] = jnp.zeros(row_ref.shape, F32)

    def block(b, _):
        rows = pl.ds(b * BLOCK, BLOCK)
        meta = meta_ref[rows, :]
        rank = rank_ref[rows, :].astype(jnp.int32)
        fgate = fgate_ref[rows, :]
        scal = scal_ref[rows, :]
        active = jnp.where(meta[:, 6:7] >= STEP, 1.0, 0.0)
        cot = cot_ref[rows, :].astype(F32)
        sums = (branch_ref[rows, :], wcot_ref[rows, :], wrow_ref[rows, :])
        branch, with_cot, with_row = combine_sums(
            experts, capacity, 1, rank, back_ref, fgate, cot, halt_row, lane, sums
        )
        z = hidden_ref[rows, :] + active * branch
        out_ref[rows, :] = z.astype(BF)
        prob = 1.0 / (1.0 + jnp.exp(-jnp.sum(z * halt_row, axis=1, keepdims=True)))
        halt_in, cot_halt = scal[:, 0:1], scal[:, 1:2]
        room = active * (1.0 - halt_in) * prob
        slope = cot_halt * room * (1.0 - prob)
        halt_ref[rows, :] = jnp.broadcast_to(halt_in + room, (BLOCK, LANES))
        slope_ref[rows, :] = jnp.broadcast_to(slope, (BLOCK, LANES))
        row_ref[0:1, :] += jnp.sum(slope * z, axis=0, keepdims=True)
        gfg = active * (with_cot + slope * with_row)
        inner = jnp.sum(fgate * gfg, axis=1, keepdims=True)
        glf_ref[rows, :] = pltpu.roll(fgate * (gfg - inner), A_EXP, 1)
        live = active * fgate
        bent = live * slope
        for index, part in enumerate((live, bent)):
            high = part.astype(BF)
            rest = part - high.astype(F32)
            middle = rest.astype(BF)
            cols_ref[3 * index, rows, :] = high
            cols_ref[3 * index + 1, rows, :] = middle
            cols_ref[3 * index + 2, rows, :] = (rest - middle.astype(F32)).astype(BF)
        return 0

    lax.fori_loop(0, tok // BLOCK, block, 0)
    turned = [jnp.transpose(cols_ref[i].astype(F32)) for i in range(6)]
    for e in range(experts):
        rows = jnp.concatenate(
            [t[e : e + 1, :] for t in turned] + [jnp.zeros((2, tok), F32)], axis=0
        ).astype(BF)
        for h in range(HALVES):
            ab_refs[h][e] = dot(rows, one_hot(rank_t_ref, e, capacity, h), NT).astype(BF)


def data_back_kernel(
    experts, parts, cot_ref, ab_ref, tail_ref, slope_ref, up_ref, down_ref, gpre_ref, gy_ref, rows_ref
):
    rows = cot_ref.shape[0]
    halt_row = vector_row(turned_tail(tail_ref[...]), A_EXP + experts, 4)
    cols = []
    for i in range(ab_ref.shape[0]):
        ab = ab_ref[i].astype(F32)
        live = ab[0:1, :] + ab[1:2, :] + ab[2:3, :]
        bent = ab[3:4, :] + ab[4:5, :] + ab[5:6, :]
        filler = jnp.zeros((LANES - 2, ab.shape[1]), F32)
        cols.append(jnp.transpose(jnp.concatenate([live, bent, filler], axis=0)))
    cols = jnp.concatenate(cols, axis=0)
    gy = (cols[:, 0:1] * cot_ref[...].astype(F32) + cols[:, 1:2] * halt_row).astype(BF)
    gy_ref[...] = gy
    total = jnp.zeros((rows, D), F32)
    for c in range(parts):
        gpre = (dot(gy, down_ref[c], NT) * slope_ref[c].astype(F32)).astype(BF)
        gpre_ref[c] = gpre
        total = total + dot(gpre, up_ref[c], NT)
    rows_ref[...] = total.astype(BF)


def weight_back_kernel(parts, steps, joined, *refs):
    up_acc, down_acc = refs[-2:]
    step = pl.program_id(0)

    @pl.when(step == 0)
    def _():
        up_acc[...] = jnp.zeros(up_acc.shape, F32)
        down_acc[...] = jnp.zeros(down_acc.shape, F32)

    for h in range(HALVES):
        x_ref, gy_ref, gpre_ref, act_ref = refs[4 * h : 4 * h + 4]

        @pl.when(step // steps == h)
        def _(x_ref=x_ref, gy_ref=gy_ref, gpre_ref=gpre_ref, act_ref=act_ref):
            for c in range(parts):
                up_acc[c] += dot(x_ref[...], gpre_ref[c], TN)
                down_acc[c] += dot(gy_ref[...], act_ref[c], TN)

    @pl.when(step == pl.num_programs(0) - 1)
    def _():
        for c in range(parts):
            if joined:
                refs[-3][c, :D] = up_acc[c].astype(BF)
                refs[-3][c, D:] = jnp.transpose(down_acc[c]).astype(BF)
            else:
                refs[-4][c] = up_acc[c].astype(BF)
                refs[-3][c] = jnp.transpose(down_acc[c]).astype(BF)


def hidden_back_kernel(
    experts,
    capacity,
    first_ref,
    second_ref,
    rank_ref,
    hidden_ref,
    w_ref,
    meta_ref,
    cot_ref,
    slope_ref,
    glf_ref,
    mixed_ref,
    so_ref,
    gates_ref,
    gout_ref,
    gh_ref,
    gslot_ref,
    gla_ref,
    rv_ref,
    vec_ref,
    acc_ref,
):
    tok = hidden_ref.shape[0]
    first = A_EXP + experts
    size = capacity // HALVES
    rows_t = transposed_tail(w_ref)
    low_t = rows_t.astype(BF)
    gain_two, shift_two, halt_row = (vector_row(rows_t, first, i) for i in (2, 3, 4))
    lane = lane_ids(BLOCK)
    upper = lane >= HEAD
    lane_half = jnp.where(upper, 1, 0)
    vec_ref[...] = jnp.zeros(vec_ref.shape, F32)
    acc_ref[...] = jnp.zeros(acc_ref.shape, F32)
    rv_ref[...] = jnp.zeros(rv_ref.shape, F32)

    def block(b, _):
        rows = pl.ds(b * BLOCK, BLOCK)
        meta = meta_ref[rows, :]
        rank = rank_ref[rows, :].astype(jnp.int32)
        active = jnp.where(meta[:, 6:7] >= STEP, 1.0, 0.0)
        place = lax.broadcasted_iota(jnp.int32, (BLOCK, size), 1)
        glf_high, glf_low = split_two(glf_ref[rows, :])
        grad = dot(glf_high, low_t) + dot(glf_low, low_t)
        for h, back_ref in enumerate((first_ref, second_ref)):
            for e in range(experts):
                hot = jnp.where(place + h * size == rank[:, e : e + 1], 1.0, 0.0).astype(BF)
                grad = grad + dot(hot, back_ref[e])
        hat, inv = norm_stats(hidden_ref[rows, :])
        normed = (hat * gain_two + shift_two).astype(BF)
        rv_ref[...] += dot(normed, glf_high, TN) + dot(normed, glf_low, TN)
        vec_ref[2:3, :] += jnp.sum(grad * hat, axis=0, keepdims=True)
        vec_ref[3:4, :] += jnp.sum(grad, axis=0, keepdims=True)
        gz = cot_ref[rows, :].astype(F32) + slope_ref[rows, 0:1] * halt_row
        gh = gz + norm_back(grad, hat, inv, gain_two)
        gh_ref[rows, :] = gh
        ga = (active * gh).astype(BF)
        acc_ref[...] += dot(ga, mixed_ref[rows, :], TN)
        gm = dot(ga, w_ref[:, WIDTH:KV_AT])
        gates = gates_ref[rows, :]
        weighted = jnp.zeros((BLOCK, 1), F32)
        grads = []
        picked = [select_heads(gm, meta[:, k : k + 1], lane_half) for k in range(A_TOP)]
        for j in range(A_TOP // 2):
            both = jnp.where(upper, picked[2 * j + 1], picked[2 * j])
            prod = both * so_ref[j, rows, :]
            scale = jnp.where(upper, gates[:, 2 * j + 1 : 2 * j + 2], gates[:, 2 * j : 2 * j + 1])
            gslot_ref[j, rows, :] = (both * scale).astype(BF)
            grads.append(jnp.sum(jnp.where(upper, 0.0, prod), axis=1, keepdims=True))
            grads.append(jnp.sum(jnp.where(upper, prod, 0.0), axis=1, keepdims=True))
        for k in range(A_TOP):
            weighted = weighted + gates[:, k : k + 1] * grads[k]
        gla = jnp.zeros((BLOCK, LANES), F32)
        for k in range(A_TOP):
            value = gates[:, k : k + 1] * (grads[k] - weighted)
            gla = jnp.where(lane == meta[:, k : k + 1], value, gla)
        gla_ref[rows, :] = gla
        return 0

    lax.fori_loop(0, tok // BLOCK, block, 0)
    gout_ref[...] = acc_ref[...].astype(BF)


def input_back_kernel(
    experts,
    tok_ref,
    w_ref,
    meta_ref,
    gh_ref,
    gslot_ref,
    gla_ref,
    rvin_ref,
    vecin_ref,
    halt_ref,
    lse_ref,
    slotq_ref,
    kv_ref,
    gin_ref,
    pack_ref,
    gx_ref,
    wide_ref,
    acc_ref,
    rv_ref,
    vec_ref,
    kx_ref,
    vx_ref,
    lset_ref,
    gq_ref,
):
    tok = tok_ref.shape[0]
    blocks = tok // BLOCK
    first = A_EXP + experts
    rows_t = transposed_tail(w_ref)
    low_t = rows_t.astype(BF)
    gain_one, shift_one = (vector_row(rows_t, first, i) for i in range(2))
    lane = lane_ids(BLOCK)
    upper = lane >= HEAD
    lane_half = jnp.where(upper, 1, 0)
    all_upper = lane_ids(tok) >= HEAD
    vec_ref[...] = jnp.zeros(vec_ref.shape, F32)
    vec_ref[2:4, :] = vecin_ref[2:4, :]
    vec_ref[4:5, :] = halt_ref[0:1, :]
    acc_ref[...] = jnp.zeros(acc_ref.shape, F32)
    rv_ref[...] = rvin_ref[...]
    kv = kv_ref[...].astype(F32)
    swapped = pltpu.roll(kv, HEAD, 1)
    kx_ref[0] = jnp.where(all_upper, 0.0, kv).astype(BF)
    kx_ref[1] = jnp.where(all_upper, swapped, 0.0).astype(BF)
    vx_ref[0] = jnp.where(all_upper, 0.0, swapped).astype(BF)
    vx_ref[1] = jnp.where(all_upper, kv, 0.0).astype(BF)
    lset_ref[...] = jnp.transpose(lse_ref[...])

    above = lax.broadcasted_iota(jnp.int32, (BLOCK, BLOCK), 0) <= lax.broadcasted_iota(
        jnp.int32, (BLOCK, BLOCK), 1
    )
    gx_ref[...] = jnp.zeros(gx_ref.shape, F32)
    for i in range(blocks):
        rows = slice(i * BLOCK, (i + 1) * BLOCK)
        seen = (i + 1) * BLOCK

        def pair(j, _, rows=rows, seen=seen, i=i):
            query = slotq_ref[j, rows, :]
            gslot = gslot_ref[j, rows, :]
            gq = jnp.zeros((BLOCK, LANES), F32)
            for h in range(2):
                keys = kx_ref[h, :seen, :]
                log = lset_ref[pl.ds(2 * j + h, 1), rows]
                scores = dot(keys, query, NT) * (HEAD**-0.5) - log
                last = jnp.where(above, scores[i * BLOCK :, :], NEG)
                scores = last if i == 0 else jnp.concatenate([scores[: i * BLOCK], last], axis=0)
                probs = jnp.exp(scores)
                gprob = dot(vx_ref[h, :seen, :], gslot, NT)
                inner = jnp.sum(probs * gprob, axis=0, keepdims=True)
                gs = (probs * (gprob - inner) * (HEAD**-0.5)).astype(BF)
                gq = gq + dot(gs, keys, TN)
                gx_ref[0, h, :seen, :] += dot(gs, query)
                gx_ref[1, h, :seen, :] += dot(probs.astype(BF), gslot)
            gq_ref[j, rows, :] = gq
            return 0

        lax.fori_loop(0, A_TOP // 2, pair, 0)

    def input_back(b, gkv_sum):
        rows = pl.ds(b * BLOCK, BLOCK)
        meta = meta_ref[rows, :]
        pairs = [gq_ref[j, rows, :] for j in range(A_TOP // 2)]

        def store(p, block):
            wide_ref[:, p * LANES : (p + 1) * LANES] = block

        spread_heads(pairs, meta, lane, lane_half, store)
        gkeys = gx_ref[0, 0, rows, :] + pltpu.roll(gx_ref[0, 1, rows, :], HEAD, 1)
        gvals = pltpu.roll(gx_ref[1, 0, rows, :], HEAD, 1) + gx_ref[1, 1, rows, :]
        gkv = jnp.where(upper, gvals, gkeys).astype(BF)
        gla_high, gla_low = split_two(gla_ref[rows, :])
        grad = dot(wide_ref[...], w_ref[:, :WIDTH], NT)
        grad = grad + dot(gkv, w_ref[:, KV_AT:RV_AT], NT)
        grad = grad + dot(gla_high, low_t) + dot(gla_low, low_t)
        hat, inv = norm_stats(tok_ref[rows, :].astype(F32))
        normed = (hat * gain_one + shift_one).astype(BF)
        acc_ref[...] += dot(normed, wide_ref[...], TN)
        rv_ref[...] += dot(normed, gla_high, TN) + dot(normed, gla_low, TN)
        vec_ref[0:1, :] += jnp.sum(grad * hat, axis=0, keepdims=True)
        vec_ref[1:2, :] += jnp.sum(grad, axis=0, keepdims=True)
        gin_ref[rows, :] = (gh_ref[rows, :] + norm_back(grad, hat, inv, gain_one)).astype(BF)
        return gkv_sum + dot(normed, gkv, TN)

    gkv_sum = lax.fori_loop(0, blocks, input_back, jnp.zeros((D, LANES), F32))
    pack_ref[:, :WIDTH] = acc_ref[...].astype(BF)
    pack_ref[:, WIDTH : WIDTH + LANES] = gkv_sum.astype(BF)
    turned = pltpu.roll(jnp.transpose(vec_ref[...]), first, 1)
    tail = jnp.where(lane_ids(D) < first, rv_ref[...], turned)
    pack_ref[:, WIDTH + LANES :] = tail.astype(BF)


VMEM_LIMIT = 60 * 1024 * 1024


def whole(shape, dtype):
    return jax.ShapeDtypeStruct(shape, dtype)


def in_vmem(count):
    return [pl.BlockSpec(memory_space=pltpu.VMEM)] * count


def call(kernel, inputs, outs, scratch=()):
    return pl.pallas_call(
        kernel,
        out_shape=outs,
        in_specs=in_vmem(len(inputs)),
        out_specs=in_vmem(len(outs)),
        scratch_shapes=list(scratch),
        compiler_params=pltpu.CompilerParams(vmem_limit_bytes=VMEM_LIMIT),
    )(*inputs)


def constant_spec(shape, middle=0):
    return pl.BlockSpec(shape, lambda s: (0, middle, 0), pipeline_mode=pl.Buffered(1))


def gather_pieces(pack, shape):
    groups, experts, _ = shape
    if experts != 8 or groups != 4:
        own = lax.all_gather(pack, "dp", axis=0, tiled=False)
        every = lax.all_gather(own, "fsdp", axis=0, tiled=False)
        return [every.transpose(1, 0, 2, 3).reshape(D, PACK)]

    own = [pack]
    for d in range(1, groups):
        pairs = [((i + d) % groups, i) for i in range(groups)]
        own.append(lax.ppermute(pack, "dp", pairs))
    own = jnp.stack(own)

    def swap(values, m):
        return lax.ppermute(values, "fsdp", [(i, i ^ m) for i in range(experts)])

    along, across = swap(own, 2), swap(own, 4)
    low = swap(along[: groups // 2], 4)
    high = swap(across[groups // 2 :], 2)
    return [
        own,
        swap(own, 1),
        along,
        swap(along, 1),
        across,
        swap(across, 1),
        low,
        high,
        swap(low, 1),
        swap(high, 1),
    ]


def on_device(
    tokens,
    halt_in,
    depths,
    attn_routes,
    ffn_routes,
    w_query,
    w_out,
    w_kv,
    router,
    vectors,
    w_up,
    w_down,
    cot_out,
    cot_halt,
):
    tok = tokens.shape[0]
    groups, experts = lax.axis_size("dp"), lax.axis_size("fsdp")
    capacity = 2 * F_TOP * tok // experts
    slice_width = w_up.shape[2]
    shard = w_query.shape[0]
    slots = experts * capacity

    tail = jnp.concatenate([router, vectors.T], axis=1)
    tail = jnp.pad(tail, ((0, 0), (0, LANES - tail.shape[1])))
    pack = jnp.concatenate([w_query, w_out.T, w_kv, tail], axis=1)
    shape = (groups, experts, shard)
    pieces = gather_pieces(pack, shape)
    joined = slice_width == D
    if joined:
        expert_pack = jnp.concatenate([w_up[0], w_down[0]], axis=0)
        whole_up = whole_down = lax.all_gather(expert_pack, "dp", axis=0, tiled=False)
    else:
        whole_up = lax.all_gather(w_up[0], "dp", axis=0, tiled=False)
        whole_down = lax.all_gather(w_down[0], "dp", axis=0, tiled=False)

    meta = jnp.concatenate([attn_routes, ffn_routes, depths[:, None], depths[:, None]], axis=1)
    scal = jnp.stack([halt_in, cot_halt], axis=1)
    half = capacity // HALVES
    half_slots = slots // HALVES
    slot_shape = whole((experts, half, D), BF)

    rank, rank_t, *cot_slots = call(
        partial(slots_kernel, experts, capacity),
        (meta, cot_out),
        (whole((tok, LANES), F32), whole((LANES, tok), jnp.int32)) + (slot_shape,) * HALVES,
    )

    def exchange(values):
        return lax.all_to_all(values, "fsdp", split_axis=0, concat_axis=0, tiled=True)

    *pieces, cot_first = lax.optimization_barrier((*pieces, cot_slots[0]))
    owned_cot = [exchange(cot_first)]

    weights, slotq, kv, so, lse, gates, mixed, hidden, fgate, *n2_slots = call(
        partial(attend_kernel, experts, capacity, shape),
        (tokens, meta, rank_t, *pieces),
        (
            whole((D, PACK), BF),
            whole((2, tok, LANES), BF),
            whole((tok, LANES), BF),
            whole((2, tok, LANES), F32),
            whole((tok, LANES), F32),
            whole((tok, LANES), F32),
            whole((tok, WIDTH), BF),
            whole((tok, D), F32),
            whole((tok, LANES), F32),
        )
        + (slot_shape,) * HALVES,
        (
            pltpu.VMEM((2, tok, LANES), BF),
            pltpu.VMEM((2, tok, LANES), BF),
            pltpu.VMEM((tok, D), BF),
        ),
    )
    n2_slots[0], owned_cot[0] = lax.optimization_barrier((n2_slots[0], owned_cot[0]))

    up_spec = constant_spec((groups, D, slice_width))
    down_spec = constant_spec((groups, slice_width, D), 1 if joined else 0)
    params = pltpu.CompilerParams(vmem_limit_bytes=VMEM_LIMIT)
    wide = whole((groups, half_slots, slice_width), BF)
    narrow = whole((half_slots, D), BF)
    step_rows = max(half, min(512, half_slots))
    step_spec = pl.BlockSpec((step_rows, D), lambda s: (s, 0))
    step_wide = pl.BlockSpec((groups, step_rows, slice_width), lambda s: (0, s, 0))

    owned = []
    for h in range(HALVES):
        owned.append(exchange(n2_slots[h]).reshape(half_slots, D))
        if h + 1 < HALVES:
            n2_slots[h + 1], owned[h] = lax.optimization_barrier((n2_slots[h + 1], owned[h]))
    outs, acts, slopes = [], [], []
    for h in range(HALVES):
        out, act, slope = pl.pallas_call(
            partial(expert_kernel, groups),
            grid=(half_slots // step_rows,),
            out_shape=(narrow, wide, wide),
            in_specs=[step_spec, up_spec, down_spec],
            out_specs=[step_spec, step_wide, step_wide],
            compiler_params=params,
        )(owned[h], whole_up, whole_down)
        outs.append(out)
        acts.append(act)
        slopes.append(slope)
    back = [exchange(out.reshape(experts, half, D)) for out in outs]

    tail_spec = pl.BlockSpec((D, LANES), lambda s: (0, RV_AT // LANES))
    full = pl.BlockSpec(memory_space=pltpu.VMEM)
    sums = pl.pallas_call(
        partial(combine_first_kernel, experts, capacity),
        name="combine_first",
        grid=(1,),
        out_shape=(whole((tok, D), F32), whole((tok, LANES), F32), whole((tok, LANES), F32)),
        in_specs=[full, full, tail_spec, full, full],
        out_specs=[full] * 3,
        compiler_params=params,
    )(back[0], rank, weights, fgate, cot_out)
    back[1], cot_second = lax.optimization_barrier((back[1], cot_slots[1]))
    owned_cot.append(exchange(cot_second))
    ab_shape = whole((experts, 8, half), BF)
    block_out, halt_wide, halt_slope, glf, halt_grad, *ab = pl.pallas_call(
        partial(combine_kernel, experts, capacity),
        name="combine",
        grid=(1,),
        out_shape=(
            whole((tok, D), BF),
            whole((tok, LANES), F32),
            whole((tok, LANES), F32),
            whole((tok, LANES), F32),
            whole((8, D), F32),
        )
        + (ab_shape,) * HALVES,
        in_specs=[full] * 7 + [tail_spec] + [full] * 4,
        out_specs=[full] * (5 + HALVES),
        scratch_shapes=[pltpu.VMEM((6, tok, LANES), BF)],
        compiler_params=params,
    )(back[1], *sums, rank, rank_t, hidden, weights, meta, fgate, scal, cot_out)
    halt_out = halt_wide[:, 0]
    owned_ab = exchange(jnp.concatenate(ab, axis=1))
    owned_ab = [owned_ab[:, 8 * h : 8 * h + 8] for h in range(HALVES)]

    together = step_rows // half if half % LANES == 0 else 1
    row_spec = pl.BlockSpec((together * half, D), lambda s: (s, 0))
    wide_spec = pl.BlockSpec((groups, together * half, slice_width), lambda s: (0, s, 0))
    gys, gpres, rows_back = [], [], []
    for h in range(HALVES):
        gpre, gy, owned_rows = pl.pallas_call(
            partial(data_back_kernel, experts, groups),
            grid=(experts // together,),
            out_shape=(wide, narrow, narrow),
            in_specs=[
                row_spec,
                pl.BlockSpec((together, 8, half), lambda s: (s, 0, 0)),
                tail_spec,
                wide_spec,
                up_spec,
                down_spec,
            ],
            out_specs=[wide_spec, row_spec, row_spec],
            compiler_params=params,
        )(owned_cot[h].reshape(half_slots, D), owned_ab[h], weights, slopes[h], whole_up, whole_down)
        gys.append(gy)
        gpres.append(gpre)
        rows_back.append(exchange(owned_rows.reshape(experts, half, D)))

    steps = half_slots // step_rows
    specs, inputs = [], []
    for h in range(HALVES):

        def at(s, h=h):
            return jnp.clip(s - h * steps, 0, steps - 1)

        narrow_at = pl.BlockSpec((step_rows, D), lambda s, at=at: (at(s), 0))
        wide_at = pl.BlockSpec((groups, step_rows, slice_width), lambda s, at=at: (0, at(s), 0))
        specs += [narrow_at, narrow_at, wide_at, wide_at]
        inputs += [owned[h], gys[h], gpres[h], acts[h]]
    if joined:
        grad_shapes = [(groups, 2 * D, D)]
    else:
        grad_shapes = [(groups, D, slice_width), (groups, slice_width, D)]
    expert_grads = pl.pallas_call(
        partial(weight_back_kernel, groups, steps, joined),
        name="weight_back",
        grid=(HALVES * steps,),
        out_shape=[whole(g, BF) for g in grad_shapes],
        in_specs=specs,
        out_specs=[constant_spec(g) for g in grad_shapes],
        scratch_shapes=[pltpu.VMEM((groups, D, slice_width), F32)] * 2,
        compiler_params=params,
    )(*inputs)
    expert_grads = [
        lax.psum_scatter(g, "dp", scatter_dimension=0, tiled=True).astype(F32) for g in expert_grads
    ]
    if joined:
        part_up, part_down = expert_grads[0][:, :D], expert_grads[0][:, D:]
    else:
        part_up, part_down = expert_grads

    grad_out, gh, gslot, gla, rv, vec = call(
        partial(hidden_back_kernel, experts, capacity),
        (
            *rows_back,
            rank,
            hidden,
            weights,
            meta,
            cot_out,
            halt_slope,
            glf,
            mixed,
            so,
            gates,
        ),
        (
            whole((D, WIDTH), BF),
            whole((tok, D), F32),
            whole((2, tok, LANES), BF),
            whole((tok, LANES), F32),
            whole((D, LANES), F32),
            whole((8, D), F32),
        ),
        (pltpu.VMEM((D, WIDTH), F32),),
    )

    def reduced(grads):
        sent = grads.reshape(groups, experts, shard, grads.shape[1]).transpose(1, 0, 2, 3)
        return jnp.sum(exchange(sent).astype(F32), axis=0).astype(BF)

    part_out = reduced(grad_out)
    grad_in, grads = call(
        partial(input_back_kernel, experts),
        (tokens, weights, meta, gh, gslot, gla, rv, vec, halt_grad, lse, slotq, kv),
        (whole((tok, D), BF), whole((D, WIDTH + 2 * LANES), BF)),
        (
            pltpu.VMEM((2, 2, tok, LANES), F32),
            pltpu.VMEM((BLOCK, WIDTH), BF),
            pltpu.VMEM((D, WIDTH), F32),
            pltpu.VMEM((D, LANES), F32),
            pltpu.VMEM((LANES, D), F32),
            pltpu.VMEM((2, tok, LANES), BF),
            pltpu.VMEM((2, tok, LANES), BF),
            pltpu.VMEM((LANES, tok), F32),
            pltpu.VMEM((2, tok, LANES), F32),
        ),
    )
    part = jnp.concatenate([reduced(grads), part_out], axis=2)
    came = lax.all_to_all(part, "dp", split_axis=0, concat_axis=0, tiled=True)
    total = jnp.sum(came.astype(F32), axis=0)
    kv_end = WIDTH + LANES
    router_end = kv_end + A_EXP + experts
    return (
        block_out,
        halt_out,
        grad_in,
        total[:, :WIDTH],
        total[:, WIDTH + 2 * LANES :].T,
        total[:, WIDTH:kv_end],
        total[:, kv_end:router_end],
        total[:, router_end : router_end + 5].T,
        part_up,
        part_down,
    )


def solution(mesh):
    both = ("dp", "fsdp")
    placed = (
        P(both, None),
        P(both),
        P(both),
        P(both, None),
        P(both, None),
        P(both, None),
        P(None, both),
        P(both, None),
        P(both, None),
        P(None, both),
        P("fsdp", None, "dp"),
        P("fsdp", "dp", None),
        P(both, None),
        P(both),
    )

    return jax.shard_map(
        on_device,
        mesh=mesh,
        in_specs=placed,
        out_specs=(
            P(both, None),
            P(both),
            P(both, None),
            P(both, None),
            P(None, both),
            P(both, None),
            P(both, None),
            P(None, both),
            P("fsdp", None, "dp"),
            P("fsdp", "dp", None),
        ),
        check_vma=False,
    )
```

```python
from functools import partial

import jax
import jax.numpy as jnp
from jax import lax
from jax.experimental import pallas as pl
from jax.experimental.pallas import tpu as pltpu
from jax.sharding import PartitionSpec as P


D = 512
HEAD = 64
A_EXP = 24
A_TOP = 4
F_TOP = 2
STEP = 2
LANES = 128
BLOCK = 256
HALVES = 2
PAIRS = A_EXP // 2
WIDTH = A_EXP * HEAD
KV_AT = 2 * WIDTH
RV_AT = KV_AT + LANES
PACK = RV_AT + LANES
EPSILON = 1e-05
NEG = -1e30
BF = jnp.bfloat16
F32 = jnp.float32

NN = (((1,), (0,)), ((), ()))
NT = (((1,), (1,)), ((), ()))
TN = (((0,), (0,)), ((), ()))

ROOT_MAX = 31.36
ROOT = (
    0.7978849411010742,
    0.03633308410644531,
    -3.259496588725597e-05,
    -5.530620546778664e-05,
    3.964748430007603e-06,
    -1.3226379280695255e-07,
    1.756186418511163e-09,
)
BELL = -0.7213475204444817
BELL_SCALE = 0.3989422804014327


def dot(a, b, dims=NN):
    return lax.dot_general(a, b, dims, preferred_element_type=F32)


def lane_ids(rows):
    return lax.broadcasted_iota(jnp.int32, (rows, LANES), 1)


def norm_stats(values):
    center = values - jnp.mean(values, axis=-1, keepdims=True)
    inv_std = lax.rsqrt(jnp.mean(center * center, axis=-1, keepdims=True) + EPSILON)
    return center * inv_std, inv_std


def norm_back(grad_normed, normal_part, inv_std, gain_row):
    grad_hat = grad_normed * gain_row
    mean_one = jnp.mean(grad_hat, axis=-1, keepdims=True)
    mean_two = jnp.mean(grad_hat * normal_part, axis=-1, keepdims=True)
    return inv_std * (grad_hat - mean_one - normal_part * mean_two)


def transposed_tail(w_ref):
    return turned_tail(w_ref[:, RV_AT:PACK])


def turned_tail(tail):
    eye = (
        lax.broadcasted_iota(jnp.int32, (LANES, LANES), 0)
        == lax.broadcasted_iota(jnp.int32, (LANES, LANES), 1)
    )
    eye = jnp.where(eye, 1.0, 0.0).astype(BF)
    return dot(eye, tail, NT)


def vector_row(rows_t, first, index):
    return rows_t[first + index : first + index + 1, :]


def split_two(values):
    high = values.astype(BF)
    return high, (values - high.astype(F32)).astype(BF)


def ranks_kernel(capacity, meta_ref, rank_ref, rank_t_ref, place_ref):
    tok = meta_ref.shape[0]
    size = capacity // HALVES
    tri = lax.broadcasted_iota(jnp.int32, (BLOCK, BLOCK), 0) >= lax.broadcasted_iota(
        jnp.int32, (BLOCK, BLOCK), 1
    )
    tri = jnp.where(tri, 1.0, 0.0).astype(BF)
    carry = jnp.zeros((1, LANES), F32)
    lane = lane_ids(BLOCK)
    for b in range(tok // BLOCK):
        rows = slice(b * BLOCK, (b + 1) * BLOCK)
        meta = meta_ref[rows, :]
        pick = ((lane == meta[:, 4:5]) | (lane == meta[:, 5:6])) & (meta[:, 6:7] >= STEP)
        ones = jnp.where(pick, 1.0, 0.0)
        count = dot(tri, ones.astype(BF)) + carry
        carry = count[BLOCK - 1 :, :]
        rank = jnp.where(pick, count - 1.0, -1.0)
        rank_ref[rows, :] = rank
        place = jnp.full((BLOCK, LANES), -1, jnp.int32)
        for k in range(F_TOP):
            route = meta[:, 4 + k : 5 + k]
            mine = jnp.sum(jnp.where(lane == route, rank, 0.0), axis=1, keepdims=True)
            mine = mine.astype(jnp.int32)
            for h in range(HALVES):
                within = mine - h * size
                dest = jnp.where((within >= 0) & (within < size), route * size + within, -1)
                place = jnp.where(lane == F_TOP * h + k, dest, place)
        place_ref[rows, :] = place
    rank_t_ref[...] = jnp.transpose(rank_ref[...])[: rank_t_ref.shape[0], :].astype(jnp.int32)


def gather_kernel(experts, starts, rank_t_ref, rows_ref, *slots_refs):
    tok = rows_ref.shape[0]

    def gather(pair, _):
        hots, targets = [], []
        for e in (2 * pair, 2 * pair + 1):
            row = rank_t_ref[pl.ds(e, 1), :]
            for start, slots_ref in zip(starts, slots_refs):
                size = slots_ref.shape[1]
                place = lax.broadcasted_iota(jnp.int32, (size, tok), 0) + start
                hots.append(jnp.where(place == row, 1.0, 0.0).astype(BF))
                targets.append((slots_ref, e, size))
        rows = dot(jnp.concatenate(hots, axis=0), rows_ref[...]).astype(BF)
        at = 0
        for slots_ref, e, size in targets:
            slots_ref[e] = rows[at : at + size]
            at += size
        return 0

    lax.fori_loop(0, experts // 2, gather, 0)


def one_hot(rank_t_ref, e, capacity):
    row = rank_t_ref[pl.ds(e, 1), :]
    place = lax.broadcasted_iota(jnp.int32, (capacity, row.shape[1]), 0)
    return jnp.where(place == row, 1.0, 0.0).astype(BF)


def select_heads(values, route, lane_half):
    shifted = route - lane_half
    acc = jnp.zeros((values.shape[0], LANES), F32)
    for p in range(PAIRS):
        acc = jnp.where(shifted == 2 * p, values[:, p * LANES : (p + 1) * LANES], acc)
    return acc + pltpu.roll(acc, HEAD, 1)


def spread_heads(pairs, meta, lane, lane_half, store):
    doubled, shifted = [], []
    for k in range(A_TOP):
        half = (lane >= HEAD) if k % 2 else (lane < HEAD)
        part = jnp.where(half, pairs[k // 2], 0.0)
        doubled.append(part + pltpu.roll(part, HEAD, 1))
        shifted.append(meta[:, k : k + 1] - lane_half)
    for p in range(PAIRS):
        acc = jnp.zeros(doubled[0].shape, F32)
        for k in range(A_TOP):
            acc = jnp.where(shifted[k] == 2 * p, doubled[k], acc)
        store(p, acc.astype(BF))


def place_pieces(shape, pieces, w_ref):
    groups, experts, shard = shape
    if len(pieces) == 1:
        w_ref[...] = pieces[0][...]
        return
    mine, group = lax.axis_index("fsdp"), lax.axis_index("dp")
    for m in range(experts):
        base = jnp.bitwise_xor(mine, m) * shard
        for g in range(groups):
            owner = lax.rem(group + g, groups)
            if m < 6:
                block = pieces[m][g]
            else:
                low, high = pieces[6 + 2 * (m - 6)], pieces[7 + 2 * (m - 6)]
                block = low[g] if g < groups // 2 else high[g - groups // 2]
            rows = pl.ds(pl.multiple_of(owner * experts * shard + base, shard), shard)
            w_ref[rows, :] = block


def attend_kernel(experts, shape, *refs):
    tok_ref, meta_ref = refs[:2]
    pieces, refs = refs[2:-12], refs[-12:]
    w_ref, slotq_ref, kv_ref, so_ref, lse_ref, gates_ref, mixed_ref, hidden_ref, fgate_ref = refs[:9]
    n2_ref, kx_ref, vx_ref = refs[9:]
    place_pieces(shape, pieces, w_ref)
    tok = tok_ref.shape[0]
    first = A_EXP + experts
    rows_t = transposed_tail(w_ref)
    gain_one, shift_one, gain_two, shift_two = (vector_row(rows_t, first, i) for i in range(4))
    lane = lane_ids(BLOCK)
    upper = lane >= HEAD
    lane_half = jnp.where(upper, 1, 0)

    def project(b, _):
        rows = pl.ds(b * BLOCK, BLOCK)
        meta = meta_ref[rows, :]
        hat, _ = norm_stats(tok_ref[rows, :].astype(F32))
        normed = (hat * gain_one + shift_one).astype(BF)
        queries = dot(normed, w_ref[:, :WIDTH])
        kv = dot(normed, w_ref[:, KV_AT:RV_AT])
        logits = dot(normed, w_ref[:, RV_AT:PACK])
        kv_ref[rows, :] = kv.astype(BF)
        swapped = pltpu.roll(kv, HEAD, 1)
        kx_ref[0, rows, :] = jnp.where(upper, 0.0, kv).astype(BF)
        kx_ref[1, rows, :] = jnp.where(upper, swapped, 0.0).astype(BF)
        vx_ref[0, rows, :] = jnp.where(upper, 0.0, swapped).astype(BF)
        vx_ref[1, rows, :] = jnp.where(upper, kv, 0.0).astype(BF)
        picked = [select_heads(queries, meta[:, k : k + 1], lane_half) for k in range(A_TOP)]
        for j in range(A_TOP // 2):
            slotq_ref[j, rows, :] = jnp.where(upper, picked[2 * j + 1], picked[2 * j]).astype(BF)
        chosen = [
            jnp.sum(jnp.where(lane == meta[:, k : k + 1], logits, 0.0), axis=1, keepdims=True)
            for k in range(A_TOP)
        ]
        top = jnp.maximum(jnp.maximum(chosen[0], chosen[1]), jnp.maximum(chosen[2], chosen[3]))
        raised = [jnp.exp(c - top) for c in chosen]
        scale = 1.0 / (raised[0] + raised[1] + raised[2] + raised[3])
        gates = jnp.zeros((BLOCK, LANES), F32)
        for k in range(A_TOP):
            gates = jnp.where(lane == k, raised[k] * scale, gates)
        gates_ref[rows, :] = gates
        return 0

    lax.fori_loop(0, tok // BLOCK, project, 0)

    below = lax.broadcasted_iota(jnp.int32, (BLOCK, BLOCK), 1) <= lax.broadcasted_iota(
        jnp.int32, (BLOCK, BLOCK), 0
    )
    for i in range(tok // BLOCK):
        rows = slice(i * BLOCK, (i + 1) * BLOCK)
        seen = (i + 1) * BLOCK
        lse_ref[rows, :] = jnp.zeros((BLOCK, LANES), F32)

        def pair(j, _, rows=rows, seen=seen, i=i):
            out = jnp.zeros((BLOCK, LANES), F32)
            query = slotq_ref[j, rows, :]
            logs = lse_ref[rows, :]
            for h in range(2):
                scores = dot(query, kx_ref[h, :seen, :], NT) * (HEAD**-0.5)
                last = jnp.where(below, scores[:, i * BLOCK :], NEG)
                scores = last if i == 0 else jnp.concatenate([scores[:, : i * BLOCK], last], axis=1)
                top = jnp.max(scores, axis=1, keepdims=True)
                raised = jnp.exp(scores - top)
                total = jnp.sum(raised, axis=1, keepdims=True)
                probs = (raised * (1.0 / total)).astype(BF)
                out = out + dot(probs, vx_ref[h, :seen, :])
                logs = jnp.where(lane == 2 * j + h, top + jnp.log(total), logs)
            so_ref[j, rows, :] = out
            lse_ref[rows, :] = logs
            return 0

        lax.fori_loop(0, A_TOP // 2, pair, 0)

    def finish(b, _):
        rows = pl.ds(b * BLOCK, BLOCK)
        meta = meta_ref[rows, :]
        gates = gates_ref[rows, :]
        active = jnp.where(meta[:, 6:7] >= STEP, 1.0, 0.0)
        pairs = [
            so_ref[j, rows, :]
            * jnp.where(upper, gates[:, 2 * j + 1 : 2 * j + 2], gates[:, 2 * j : 2 * j + 1])
            for j in range(A_TOP // 2)
        ]

        def store(p, block):
            mixed_ref[rows, p * LANES : (p + 1) * LANES] = block

        spread_heads(pairs, meta, lane, lane_half, store)
        branch = dot(mixed_ref[rows, :], w_ref[:, WIDTH:KV_AT], NT)
        hidden = tok_ref[rows, :].astype(F32) + active * branch
        hidden_ref[rows, :] = hidden
        hat, _ = norm_stats(hidden)
        normed = (hat * gain_two + shift_two).astype(BF)
        n2_ref[rows, :] = normed
        logits = dot(normed, w_ref[:, RV_AT:PACK])
        first_logit, second_logit = (
            jnp.sum(
                jnp.where(lane == meta[:, 4 + k : 5 + k] + A_EXP, logits, 0.0), axis=1, keepdims=True
            )
            for k in range(F_TOP)
        )
        top = jnp.maximum(first_logit, second_logit)
        first_raised, second_raised = jnp.exp(first_logit - top), jnp.exp(second_logit - top)
        scale = 1.0 / (first_raised + second_raised)
        fgate_ref[rows, :] = jnp.where(lane == 0, first_raised * scale, second_raised * scale)
        return 0

    lax.fori_loop(0, tok // BLOCK, finish, 0)


def expert_kernel(parts, x_ref, up_ref, down_ref, out_ref, act_ref, slope_ref, total_ref):
    total_ref[...] = jnp.zeros(total_ref.shape, F32)

    def part(c, _):
        pre = dot(x_ref[...], up_ref[c])
        square = pre * pre
        short = jnp.minimum(square, ROOT_MAX)
        root = ROOT[-1] * short
        for coef in ROOT[-2:0:-1]:
            root = (root + coef) * short
        phi = 0.5 + 0.5 * jnp.tanh(pre * (root + ROOT[0]))
        act = (pre * phi).astype(BF)
        act_ref[c] = act
        bell = jnp.exp2(square * BELL)
        slope_ref[c] = (phi + (pre * BELL_SCALE) * bell).astype(BF)
        total_ref[...] += dot(act, down_ref[c])
        return 0

    lax.fori_loop(0, parts, part, 0, unroll=2)
    out_ref[...] = total_ref[...].astype(BF)


def combine_sums(h, place, back_ref, fgate, cot, halt_row, lane, branch, cols):
    slot = lax.broadcasted_iota(jnp.int32, (BLOCK, back_ref.shape[0]), 1)
    for k in range(F_TOP):
        at = F_TOP * h + k
        hot = jnp.where(slot == place[:, at : at + 1], 1.0, 0.0).astype(BF)
        came = dot(hot, back_ref[...])
        branch = branch + fgate[:, k : k + 1] * came
        one = jnp.sum(came * cot, axis=1, keepdims=True)
        two = jnp.sum(came * halt_row, axis=1, keepdims=True)
        cols = cols + jnp.where(lane == k, one, jnp.where(lane == F_TOP + k, two, 0.0))
    return branch, cols


def split_three(values):
    high = values.astype(BF).astype(F32)
    middle = (values - high).astype(BF).astype(F32)
    return high, middle, values - high - middle


def combine_first_kernel(
    experts,
    back_ref,
    place_ref,
    tail_ref,
    meta_ref,
    fgate_ref,
    cot_ref,
    branch_ref,
    cols_ref,
    live_ref,
    dense_ref,
):
    halt_row = vector_row(turned_tail(tail_ref[...]), A_EXP + experts, 4)
    lane = lane_ids(BLOCK)

    def block(b, _):
        rows = pl.ds(b * BLOCK, BLOCK)
        meta = meta_ref[rows, :]
        fgate = fgate_ref[rows, :]
        branch, cols = combine_sums(
            0,
            place_ref[rows, :],
            back_ref,
            fgate,
            cot_ref[rows, :].astype(F32),
            halt_row,
            lane,
            jnp.zeros((BLOCK, D), F32),
            jnp.zeros((BLOCK, LANES), F32),
        )
        branch_ref[rows, :] = branch
        cols_ref[rows, :] = cols
        active = jnp.where(meta[:, 6:7] >= STEP, 1.0, 0.0)
        dense = jnp.zeros((BLOCK, LANES), F32)
        for k in range(F_TOP):
            named = lane == meta[:, 4 + k : 5 + k]
            dense = jnp.where(named, active * fgate[:, k : k + 1], dense)
        dense_ref[rows, :] = dense
        return 0

    lax.fori_loop(0, branch_ref.shape[0] // BLOCK, block, 0)
    turned = jnp.transpose(dense_ref[...])[: live_ref.shape[1], :]
    for index, part in enumerate(split_three(turned)):
        live_ref[index] = part.astype(BF)


def combine_kernel(
    experts,
    capacity,
    back_ref,
    branch_ref,
    cols_ref,
    live_ref,
    place_ref,
    rank_t_ref,
    hidden_ref,
    tail_ref,
    meta_ref,
    fgate_ref,
    scal_ref,
    cot_ref,
    out_ref,
    halt_ref,
    slope_ref,
    glf_ref,
    row_ref,
    ab_ref,
    kept_ref,
):
    step = pl.program_id(0)
    halt_row = vector_row(turned_tail(tail_ref[...]), A_EXP + experts, 4)
    lane = lane_ids(BLOCK)

    @pl.when(step == 0)
    def _():
        row_ref[...] = jnp.zeros(row_ref.shape, F32)

    meta = meta_ref[...]
    fgate = fgate_ref[...]
    scal = scal_ref[...]
    active = jnp.where(meta[:, 6:7] >= STEP, 1.0, 0.0)
    branch, cols = combine_sums(
        1,
        place_ref[...],
        back_ref,
        fgate,
        cot_ref[...].astype(F32),
        halt_row,
        lane,
        branch_ref[...],
        cols_ref[...],
    )
    z = hidden_ref[...] + active * branch
    out_ref[...] = z.astype(BF)
    prob = 1.0 / (1.0 + jnp.exp(-jnp.sum(z * halt_row, axis=1, keepdims=True)))
    halt_in, cot_halt = scal[:, 0:1], scal[:, 1:2]
    room = active * (1.0 - halt_in) * prob
    slope = cot_halt * room * (1.0 - prob)
    halt_ref[...] = jnp.broadcast_to(halt_in + room, (BLOCK, LANES))
    wide_slope = jnp.broadcast_to(slope, (BLOCK, LANES))
    slope_ref[...] = wide_slope
    kept_ref[pl.ds(step * BLOCK, BLOCK), :] = wide_slope
    row_ref[0:1, :] += jnp.sum(slope * z, axis=0, keepdims=True)
    gfg = [active * (cols[:, k : k + 1] + slope * cols[:, 2 + k : 3 + k]) for k in range(F_TOP)]
    inner = fgate[:, 0:1] * gfg[0] + fgate[:, 1:2] * gfg[1]
    glf = jnp.zeros((BLOCK, LANES), F32)
    for k in range(F_TOP):
        value = fgate[:, k : k + 1] * (gfg[k] - inner)
        glf = jnp.where(lane == meta[:, 4 + k : 5 + k] + A_EXP, value, glf)
    glf_ref[...] = glf

    @pl.when(step == pl.num_programs(0) - 1)
    def _():
        slopes = [part[:1, :] for part in split_three(jnp.transpose(kept_ref[...]))]
        low = [live_ref[i].astype(F32) for i in range(3)]
        tok = kept_ref.shape[0]
        for e in range(experts):
            rows = [part[e : e + 1, :] for part in low] + slopes + [jnp.zeros((2, tok), F32)]
            rows = jnp.concatenate(rows, axis=0).astype(BF)
            ab_ref[e] = dot(rows, one_hot(rank_t_ref, e, capacity), NT).astype(BF)


def data_back_kernel(experts, parts, h, *refs):
    cot_refs, refs = refs[:-8], refs[-8:]
    ab_ref, tail_ref, slope_ref, up_ref, down_ref, gpre_ref, gy_ref, rows_ref = refs
    size = ab_ref.shape[2] // HALVES
    count = ab_ref.shape[0]
    rows = count * size
    halt_row = vector_row(turned_tail(tail_ref[...]), A_EXP + experts, 4)
    cols = []
    cots = []
    for i in range(count):
        ab = ab_ref[i].astype(F32)[:, h * size : (h + 1) * size]
        live = ab[0:1, :] + ab[1:2, :] + ab[2:3, :]
        slope = ab[3:4, :] + ab[4:5, :] + ab[5:6, :]
        filler = jnp.zeros((LANES - 2, size), F32)
        cols.append(jnp.transpose(jnp.concatenate([live, slope, filler], axis=0)))
        for ref in cot_refs:
            part = ref.shape[0] // count
            cots.append(ref[i * part : (i + 1) * part, :].astype(F32))
    cols = jnp.concatenate(cols, axis=0)
    cots = jnp.concatenate(cots, axis=0)
    gy = (cols[:, 0:1] * (cots + cols[:, 1:2] * halt_row)).astype(BF)
    gy_ref[...] = gy
    total = jnp.zeros((rows, D), F32)
    for c in range(parts):
        gpre = (dot(gy, down_ref[c], NT) * slope_ref[c].astype(F32)).astype(BF)
        gpre_ref[c] = gpre
        total = total + dot(gpre, up_ref[c], NT)
    rows_ref[...] = total.astype(BF)


def weight_back_kernel(parts, steps, joined, *refs):
    up_acc, down_acc = refs[-2:]
    step = pl.program_id(0)

    @pl.when(step == 0)
    def _():
        up_acc[...] = jnp.zeros(up_acc.shape, F32)
        down_acc[...] = jnp.zeros(down_acc.shape, F32)

    for h in range(HALVES):
        x_ref, gy_ref, gpre_ref, act_ref = refs[4 * h : 4 * h + 4]

        @pl.when(step // steps == h)
        def _(x_ref=x_ref, gy_ref=gy_ref, gpre_ref=gpre_ref, act_ref=act_ref):
            for c in range(parts):
                up_acc[c] += dot(x_ref[...], gpre_ref[c], TN)
                down_acc[c] += dot(gy_ref[...], act_ref[c], TN)

    @pl.when(step == pl.num_programs(0) - 1)
    def _():
        for c in range(parts):
            if joined:
                refs[-3][c, :D] = up_acc[c].astype(BF)
                refs[-3][c, D:] = jnp.transpose(down_acc[c]).astype(BF)
            else:
                refs[-4][c] = up_acc[c].astype(BF)
                refs[-3][c] = jnp.transpose(down_acc[c]).astype(BF)


def store_grads(ref, values, start):
    columns = slice(start, start + values.shape[1])
    if len(ref.shape) == 2:
        ref[:, columns] = values
        return
    experts, groups, shard, _ = ref.shape
    for e in range(experts):
        for g in range(groups):
            at = (g * experts + e) * shard
            ref[e, g, :, columns] = values[at : at + shard]


def hidden_back_kernel(
    experts,
    capacity,
    first_ref,
    second_ref,
    rank_ref,
    hidden_ref,
    w_ref,
    tail_ref,
    meta_ref,
    cot_ref,
    slope_ref,
    glf_ref,
    mixed_ref,
    so_ref,
    gates_ref,
    gout_ref,
    gh_ref,
    gslot_ref,
    gla_ref,
    rv_ref,
    vec_ref,
    acc_ref,
):
    step = pl.program_id(0)
    first = A_EXP + experts
    size = capacity // HALVES
    rows_t = turned_tail(tail_ref[...])
    low_t = rows_t.astype(BF)
    gain_two, shift_two, halt_row = (vector_row(rows_t, first, i) for i in (2, 3, 4))
    lane = lane_ids(BLOCK)
    upper = lane >= HEAD
    lane_half = jnp.where(upper, 1, 0)

    @pl.when(step == 0)
    def _():
        vec_ref[...] = jnp.zeros(vec_ref.shape, F32)
        acc_ref[...] = jnp.zeros(acc_ref.shape, F32)
        rv_ref[...] = jnp.zeros(rv_ref.shape, F32)

    meta = meta_ref[...]
    rank = rank_ref[...].astype(jnp.int32)
    active = jnp.where(meta[:, 6:7] >= STEP, 1.0, 0.0)
    place = lax.broadcasted_iota(jnp.int32, (BLOCK, size), 1)
    glf_high, glf_low = split_two(glf_ref[...])
    grad = dot(glf_high, low_t) + dot(glf_low, low_t)
    for h, back_ref in enumerate((first_ref, second_ref)):
        for e in range(experts):
            hot = jnp.where(place + h * size == rank[:, e : e + 1], 1.0, 0.0).astype(BF)
            grad = grad + dot(hot, back_ref[e])
    hat, inv = norm_stats(hidden_ref[...])
    normed = (hat * gain_two + shift_two).astype(BF)
    rv_ref[...] += dot(normed, glf_high, TN) + dot(normed, glf_low, TN)
    vec_ref[2:3, :] += jnp.sum(grad * hat, axis=0, keepdims=True)
    vec_ref[3:4, :] += jnp.sum(grad, axis=0, keepdims=True)
    gz = cot_ref[...].astype(F32) + slope_ref[:, 0:1] * halt_row
    gh = gz + norm_back(grad, hat, inv, gain_two)
    gh_ref[...] = gh
    ga = (active * gh).astype(BF)
    acc_ref[...] += dot(ga, mixed_ref[...], TN)
    gm = dot(ga, w_ref[...])
    gates = gates_ref[...]
    weighted = jnp.zeros((BLOCK, 1), F32)
    grads = []
    picked = [select_heads(gm, meta[:, k : k + 1], lane_half) for k in range(A_TOP)]
    for j in range(A_TOP // 2):
        both = jnp.where(upper, picked[2 * j + 1], picked[2 * j])
        prod = both * so_ref[j]
        scale = jnp.where(upper, gates[:, 2 * j + 1 : 2 * j + 2], gates[:, 2 * j : 2 * j + 1])
        gslot_ref[j] = (both * scale).astype(BF)
        grads.append(jnp.sum(jnp.where(upper, 0.0, prod), axis=1, keepdims=True))
        grads.append(jnp.sum(jnp.where(upper, prod, 0.0), axis=1, keepdims=True))
    for k in range(A_TOP):
        weighted = weighted + gates[:, k : k + 1] * grads[k]
    gla = jnp.zeros((BLOCK, LANES), F32)
    for k in range(A_TOP):
        value = gates[:, k : k + 1] * (grads[k] - weighted)
        gla = jnp.where(lane == meta[:, k : k + 1], value, gla)
    gla_ref[...] = gla

    @pl.when(step == pl.num_programs(0) - 1)
    def _():
        store_grads(gout_ref, acc_ref[...].astype(BF), 0)


def input_back_kernel(
    experts,
    tok_ref,
    w_ref,
    meta_ref,
    gh_ref,
    gslot_ref,
    gla_ref,
    rvin_ref,
    vecin_ref,
    halt_ref,
    lse_ref,
    slotq_ref,
    kv_ref,
    gin_ref,
    pack_ref,
    gx_ref,
    wide_ref,
    acc_ref,
    rv_ref,
    vec_ref,
    kx_ref,
    vx_ref,
    lset_ref,
    gq_ref,
):
    tok = tok_ref.shape[0]
    blocks = tok // BLOCK
    first = A_EXP + experts
    rows_t = transposed_tail(w_ref)
    low_t = rows_t.astype(BF)
    gain_one, shift_one = (vector_row(rows_t, first, i) for i in range(2))
    lane = lane_ids(BLOCK)
    upper = lane >= HEAD
    lane_half = jnp.where(upper, 1, 0)
    all_upper = lane_ids(tok) >= HEAD
    vec_ref[...] = jnp.zeros(vec_ref.shape, F32)
    vec_ref[2:4, :] = vecin_ref[2:4, :]
    vec_ref[4:5, :] = halt_ref[0:1, :]
    acc_ref[...] = jnp.zeros(acc_ref.shape, F32)
    rv_ref[...] = rvin_ref[...]
    kv = kv_ref[...].astype(F32)
    swapped = pltpu.roll(kv, HEAD, 1)
    kx_ref[0] = jnp.where(all_upper, 0.0, kv).astype(BF)
    kx_ref[1] = jnp.where(all_upper, swapped, 0.0).astype(BF)
    vx_ref[0] = jnp.where(all_upper, 0.0, swapped).astype(BF)
    vx_ref[1] = jnp.where(all_upper, kv, 0.0).astype(BF)
    lset_ref[...] = jnp.transpose(lse_ref[...])

    above = lax.broadcasted_iota(jnp.int32, (BLOCK, BLOCK), 0) <= lax.broadcasted_iota(
        jnp.int32, (BLOCK, BLOCK), 1
    )
    gx_ref[...] = jnp.zeros(gx_ref.shape, F32)
    for i in range(blocks):
        rows = slice(i * BLOCK, (i + 1) * BLOCK)
        seen = (i + 1) * BLOCK

        def pair(j, _, rows=rows, seen=seen, i=i):
            query = slotq_ref[j, rows, :]
            gslot = gslot_ref[j, rows, :]
            gq = jnp.zeros((BLOCK, LANES), F32)
            for h in range(2):
                keys = kx_ref[h, :seen, :]
                log = lset_ref[pl.ds(2 * j + h, 1), rows]
                scores = dot(keys, query, NT) * (HEAD**-0.5) - log
                last = jnp.where(above, scores[i * BLOCK :, :], NEG)
                scores = last if i == 0 else jnp.concatenate([scores[: i * BLOCK], last], axis=0)
                probs = jnp.exp(scores)
                gprob = dot(vx_ref[h, :seen, :], gslot, NT)
                inner = jnp.sum(probs * gprob, axis=0, keepdims=True)
                gs = (probs * (gprob - inner) * (HEAD**-0.5)).astype(BF)
                gq = gq + dot(gs, keys, TN)
                gx_ref[0, h, :seen, :] += dot(gs, query)
                gx_ref[1, h, :seen, :] += dot(probs.astype(BF), gslot)
            gq_ref[j, rows, :] = gq
            return 0

        lax.fori_loop(0, A_TOP // 2, pair, 0)

    def input_back(b, gkv_sum):
        rows = pl.ds(b * BLOCK, BLOCK)
        meta = meta_ref[rows, :]
        pairs = [gq_ref[j, rows, :] for j in range(A_TOP // 2)]

        def store(p, block):
            wide_ref[:, p * LANES : (p + 1) * LANES] = block

        spread_heads(pairs, meta, lane, lane_half, store)
        gkeys = gx_ref[0, 0, rows, :] + pltpu.roll(gx_ref[0, 1, rows, :], HEAD, 1)
        gvals = pltpu.roll(gx_ref[1, 0, rows, :], HEAD, 1) + gx_ref[1, 1, rows, :]
        gkv = jnp.where(upper, gvals, gkeys).astype(BF)
        gla_high, gla_low = split_two(gla_ref[rows, :])
        grad = dot(wide_ref[...], w_ref[:, :WIDTH], NT)
        grad = grad + dot(gkv, w_ref[:, KV_AT:RV_AT], NT)
        grad = grad + dot(gla_high, low_t) + dot(gla_low, low_t)
        hat, inv = norm_stats(tok_ref[rows, :].astype(F32))
        normed = (hat * gain_one + shift_one).astype(BF)
        acc_ref[...] += dot(normed, wide_ref[...], TN)
        rv_ref[...] += dot(normed, gla_high, TN) + dot(normed, gla_low, TN)
        vec_ref[0:1, :] += jnp.sum(grad * hat, axis=0, keepdims=True)
        vec_ref[1:2, :] += jnp.sum(grad, axis=0, keepdims=True)
        gin_ref[rows, :] = (gh_ref[rows, :] + norm_back(grad, hat, inv, gain_one)).astype(BF)
        return gkv_sum + dot(normed, gkv, TN)

    gkv_sum = lax.fori_loop(0, blocks, input_back, jnp.zeros((D, LANES), F32))
    store_grads(pack_ref, acc_ref[...].astype(BF), 0)
    store_grads(pack_ref, gkv_sum.astype(BF), WIDTH)
    turned = pltpu.roll(jnp.transpose(vec_ref[...]), first, 1)
    tail = jnp.where(lane_ids(D) < first, rv_ref[...], turned)
    store_grads(pack_ref, tail.astype(BF), WIDTH + LANES)


VMEM_LIMIT = 60 * 1024 * 1024


def whole(shape, dtype):
    return jax.ShapeDtypeStruct(shape, dtype)


def in_vmem(count):
    return [pl.BlockSpec(memory_space=pltpu.VMEM)] * count


def call(kernel, inputs, outs, scratch=()):
    return pl.pallas_call(
        kernel,
        out_shape=outs,
        in_specs=in_vmem(len(inputs)),
        out_specs=in_vmem(len(outs)),
        scratch_shapes=list(scratch),
        compiler_params=pltpu.CompilerParams(vmem_limit_bytes=VMEM_LIMIT),
    )(*inputs)


def constant_spec(shape, middle=0):
    return pl.BlockSpec(shape, lambda s: (0, middle, 0), pipeline_mode=pl.Buffered(1))


def gather_pieces(pack, shape):
    groups, experts, _ = shape
    if experts != 8 or groups != 4:
        own = lax.all_gather(pack, "dp", axis=0, tiled=False)
        every = lax.all_gather(own, "fsdp", axis=0, tiled=False)
        return [every.transpose(1, 0, 2, 3).reshape(D, PACK)]

    own = [pack]
    for d in range(1, groups):
        pairs = [((i + d) % groups, i) for i in range(groups)]
        own.append(lax.ppermute(pack, "dp", pairs))
    own = jnp.stack(own)

    def swap(values, m):
        return lax.ppermute(values, "fsdp", [(i, i ^ m) for i in range(experts)])

    along = swap(own, 2)
    across = swap(own, 4)
    low = swap(along[: groups // 2], 4)
    high = swap(across[groups // 2 :], 2)
    return [
        own,
        swap(own, 1),
        along,
        swap(along, 1),
        across,
        swap(across, 1),
        low,
        high,
        swap(low, 1),
        swap(high, 1),
    ]


def on_device(
    tokens,
    halt_in,
    depths,
    attn_routes,
    ffn_routes,
    w_query,
    w_out,
    w_kv,
    router,
    vectors,
    w_up,
    w_down,
    cot_out,
    cot_halt,
):
    tok = tokens.shape[0]
    groups, experts = lax.axis_size("dp"), lax.axis_size("fsdp")
    capacity = 2 * F_TOP * tok // experts
    slice_width = w_up.shape[2]
    shard = w_query.shape[0]
    slots = experts * capacity

    tail = jnp.concatenate([router, vectors.T], axis=1)
    tail = jnp.pad(tail, ((0, 0), (0, LANES - tail.shape[1])))
    pack = jnp.concatenate([w_query, w_out.T, w_kv, tail], axis=1)
    shape = (groups, experts, shard)
    pieces = gather_pieces(pack, shape)
    joined = slice_width == D
    if joined:
        expert_pack = jnp.concatenate([w_up[0], w_down[0]], axis=0)
        whole_up = whole_down = lax.all_gather(expert_pack, "dp", axis=0, tiled=False)
    else:
        whole_up = lax.all_gather(w_up[0], "dp", axis=0, tiled=False)
        whole_down = lax.all_gather(w_down[0], "dp", axis=0, tiled=False)

    meta = jnp.concatenate([attn_routes, ffn_routes, depths[:, None], depths[:, None]], axis=1)
    scal = jnp.stack([halt_in, cot_halt], axis=1)
    half = capacity // HALVES
    half_slots = slots // HALVES

    rank, rank_t, place = call(
        partial(ranks_kernel, capacity),
        (meta,),
        (whole((tok, LANES), F32), whole((experts, tok), jnp.int32), whole((tok, LANES), jnp.int32)),
    )

    def gather_rows(rows, starts):
        ends = starts[1:] + (capacity if len(starts) > 1 else starts[0] + half,)
        shapes = [whole((experts, end - start, D), BF) for start, end in zip(starts, ends)]
        return call(partial(gather_kernel, experts, starts), (rank_t, rows), shapes)

    cot_slots = gather_rows(cot_out, (0, half, half + half // 2))

    def exchange(values):
        came = lax.all_to_all(values, "fsdp", split_axis=0, concat_axis=0, tiled=True)
        return came

    *pieces, cot_first, scal = lax.optimization_barrier((*pieces, cot_slots[0], scal))
    owned_cot = [exchange(cot_first)]

    weights, slotq, kv, so, lse, gates, mixed, hidden, fgate, normed_two = call(
        partial(attend_kernel, experts, shape),
        (tokens, meta, *pieces),
        (
            whole((D, PACK), BF),
            whole((2, tok, LANES), BF),
            whole((tok, LANES), BF),
            whole((2, tok, LANES), F32),
            whole((tok, LANES), F32),
            whole((tok, LANES), F32),
            whole((tok, WIDTH), BF),
            whole((tok, D), F32),
            whole((tok, LANES), F32),
            whole((tok, D), BF),
        ),
        (pltpu.VMEM((2, tok, LANES), BF), pltpu.VMEM((2, tok, LANES), BF)),
    )
    n2_slots = [gather_rows(normed_two, (h * half,))[0] for h in range(HALVES)]
    n2_slots[0], owned_cot[0] = lax.optimization_barrier((n2_slots[0], owned_cot[0]))

    up_spec = constant_spec((groups, D, slice_width))
    down_spec = constant_spec((groups, slice_width, D), 1 if joined else 0)
    params = pltpu.CompilerParams(vmem_limit_bytes=VMEM_LIMIT)
    wide = whole((groups, half_slots, slice_width), BF)
    narrow = whole((half_slots, D), BF)
    step_rows = max(half, min(512, half_slots))
    step_spec = pl.BlockSpec((step_rows, D), lambda s: (s, 0))
    step_wide = pl.BlockSpec((groups, step_rows, slice_width), lambda s: (0, s, 0))

    owned = []
    for h in range(HALVES):
        owned.append(exchange(n2_slots[h]).reshape(half_slots, D))
        if h + 1 < HALVES:
            n2_slots[h + 1], owned[h] = lax.optimization_barrier((n2_slots[h + 1], owned[h]))
    outs, acts, slopes = [], [], []
    for h in range(HALVES):
        out, act, slope = pl.pallas_call(
            partial(expert_kernel, groups),
            grid=(half_slots // step_rows,),
            out_shape=(narrow, wide, wide),
            in_specs=[step_spec, up_spec, down_spec],
            out_specs=[step_spec, step_wide, step_wide],
            scratch_shapes=[pltpu.VMEM((step_rows, D), F32)],
            compiler_params=params,
        )(owned[h], whole_up, whole_down)
        outs.append(out)
        acts.append(act)
        slopes.append(slope)
    back = []
    for h in range(HALVES):
        back.append(exchange(outs[h].reshape(experts, half, D)).reshape(half_slots, D))

    tail_spec = pl.BlockSpec((D, LANES), lambda s: (0, RV_AT // LANES))
    full = pl.BlockSpec(memory_space=pltpu.VMEM)
    sums = pl.pallas_call(
        partial(combine_first_kernel, experts),
        name="combine_first",
        grid=(1,),
        out_shape=(
            whole((tok, D), F32),
            whole((tok, LANES), F32),
            whole((3, max(16, experts), tok), BF),
        ),
        in_specs=[full, full, tail_spec, full, full, full],
        out_specs=[full] * 3,
        scratch_shapes=[pltpu.VMEM((tok, LANES), F32)],
        compiler_params=params,
    )(back[0], place, weights, meta, fgate, cot_out)
    back[1], cot_second = lax.optimization_barrier((back[1], cot_slots[1]))
    owned_cot.append(exchange(cot_second))

    def tokens_of(width):
        return pl.BlockSpec((BLOCK, width), lambda b: (b, 0))

    block_out, halt_wide, halt_slope, glf, halt_grad, ab = pl.pallas_call(
        partial(combine_kernel, experts, capacity),
        name="combine",
        grid=(tok // BLOCK,),
        out_shape=(
            whole((tok, D), BF),
            whole((tok, LANES), F32),
            whole((tok, LANES), F32),
            whole((tok, LANES), F32),
            whole((8, D), F32),
            whole((experts, 8, capacity), BF),
        ),
        in_specs=[
            full,
            tokens_of(D),
            tokens_of(LANES),
            full,
            tokens_of(LANES),
            full,
            tokens_of(D),
            tail_spec,
            tokens_of(meta.shape[1]),
            tokens_of(LANES),
            tokens_of(2),
            tokens_of(D),
        ],
        out_specs=[tokens_of(D)] + [tokens_of(LANES)] * 3 + [full] * 2,
        scratch_shapes=[pltpu.VMEM((tok, LANES), F32)],
        compiler_params=params,
    )(back[1], *sums, place, rank_t, hidden, weights, meta, fgate, scal, cot_out)
    halt_out = halt_wide[:, 0]
    ab, owned_cot[1] = lax.optimization_barrier((ab, owned_cot[1]))
    owned_ab = exchange(ab)
    owned_ab, cot_third = lax.optimization_barrier((owned_ab, cot_slots[2]))
    owned_cot.append(exchange(cot_third))
    cot_parts = [owned_cot[:1], owned_cot[1:]]

    together = step_rows // half if half % LANES == 0 else 1
    row_spec = pl.BlockSpec((together * half, D), lambda s: (s, 0))
    wide_spec = pl.BlockSpec((groups, together * half, slice_width), lambda s: (0, s, 0))
    gys, gpres, rows_back = [], [], []
    for h in range(HALVES):
        gpre, gy, owned_rows = pl.pallas_call(
            partial(data_back_kernel, experts, groups, h),
            grid=(experts // together,),
            out_shape=(wide, narrow, narrow),
            in_specs=[
                *(pl.BlockSpec((together * part.shape[1], D), lambda s: (s, 0)) for part in cot_parts[h]),
                pl.BlockSpec((together, 8, capacity), lambda s: (s, 0, 0)),
                tail_spec,
                wide_spec,
                up_spec,
                down_spec,
            ],
            out_specs=[wide_spec, row_spec, row_spec],
            compiler_params=params,
        )(
            *(part.reshape(-1, D) for part in cot_parts[h]),
            owned_ab,
            weights,
            slopes[h],
            whole_up,
            whole_down,
        )
        gys.append(gy)
        gpres.append(gpre)
        rows_back.append(exchange(owned_rows.reshape(experts, half, D)))

    steps = half_slots // step_rows
    specs, inputs = [], []
    for h in range(HALVES):

        def at(s, h=h):
            return jnp.clip(s - h * steps, 0, steps - 1)

        narrow_at = pl.BlockSpec((step_rows, D), lambda s, at=at: (at(s), 0))
        wide_at = pl.BlockSpec((groups, step_rows, slice_width), lambda s, at=at: (0, at(s), 0))
        specs += [narrow_at, narrow_at, wide_at, wide_at]
        inputs += [owned[h], gys[h], gpres[h], acts[h]]
    if joined:
        grad_shapes = [(groups, 2 * D, D)]
    else:
        grad_shapes = [(groups, D, slice_width), (groups, slice_width, D)]
    expert_grads = pl.pallas_call(
        partial(weight_back_kernel, groups, steps, joined),
        name="weight_back",
        grid=(HALVES * steps,),
        out_shape=[whole(g, BF) for g in grad_shapes],
        in_specs=specs,
        out_specs=[constant_spec(g) for g in grad_shapes],
        scratch_shapes=[pltpu.VMEM((groups, D, slice_width), F32)] * 2,
        compiler_params=params,
    )(*inputs)
    expert_grads = [
        lax.psum_scatter(g, "dp", scatter_dimension=0, tiled=True).astype(F32) for g in expert_grads
    ]
    if joined:
        part_up, part_down = expert_grads[0][:, :D], expert_grads[0][:, D:]
    else:
        part_up, part_down = expert_grads

    ordered = shard % 16 == 0

    def grads_shape(width):
        return whole((experts, groups, shard, width) if ordered else (D, width), BF)

    pair_spec = pl.BlockSpec((2, BLOCK, LANES), lambda b: (0, b, 0))
    grad_out, gh, gslot, gla, rv, vec = pl.pallas_call(
        partial(hidden_back_kernel, experts, capacity),
        name="hidden_back",
        grid=(tok // BLOCK,),
        out_shape=(
            grads_shape(WIDTH),
            whole((tok, D), F32),
            whole((2, tok, LANES), BF),
            whole((tok, LANES), F32),
            whole((D, LANES), F32),
            whole((8, D), F32),
        ),
        in_specs=[
            full,
            full,
            tokens_of(LANES),
            tokens_of(D),
            pl.BlockSpec((D, WIDTH), lambda b: (0, 1), pipeline_mode=pl.Buffered(1)),
            tail_spec,
            tokens_of(meta.shape[1]),
            tokens_of(D),
            tokens_of(LANES),
            tokens_of(LANES),
            tokens_of(WIDTH),
            pair_spec,
            tokens_of(LANES),
        ],
        out_specs=[full, tokens_of(D), pair_spec, tokens_of(LANES), full, full],
        scratch_shapes=[pltpu.VMEM((D, WIDTH), F32)],
        compiler_params=params,
    )(
        *rows_back,
        rank,
        hidden,
        weights,
        weights,
        meta,
        cot_out,
        halt_slope,
        glf,
        mixed,
        so,
        gates,
    )

    def reduced(sent):
        if not ordered:
            sent = sent.reshape(groups, experts, shard, sent.shape[1]).transpose(1, 0, 2, 3)
        return jnp.sum(exchange(sent).astype(F32), axis=0).astype(BF)

    part_out = reduced(grad_out)
    grad_in, grads = call(
        partial(input_back_kernel, experts),
        (tokens, weights, meta, gh, gslot, gla, rv, vec, halt_grad, lse, slotq, kv),
        (whole((tok, D), BF), grads_shape(WIDTH + 2 * LANES)),
        (
            pltpu.VMEM((2, 2, tok, LANES), F32),
            pltpu.VMEM((BLOCK, WIDTH), BF),
            pltpu.VMEM((D, WIDTH), F32),
            pltpu.VMEM((D, LANES), F32),
            pltpu.VMEM((LANES, D), F32),
            pltpu.VMEM((2, tok, LANES), BF),
            pltpu.VMEM((2, tok, LANES), BF),
            pltpu.VMEM((LANES, tok), F32),
            pltpu.VMEM((2, tok, LANES), F32),
        ),
    )
    part = jnp.concatenate([reduced(grads), part_out], axis=2)
    came = lax.all_to_all(part, "dp", split_axis=0, concat_axis=0, tiled=True)
    total = jnp.sum(came.astype(F32), axis=0)
    kv_end = WIDTH + LANES
    router_end = kv_end + A_EXP + experts
    return (
        block_out,
        halt_out,
        grad_in,
        total[:, :WIDTH],
        total[:, WIDTH + 2 * LANES :].T,
        total[:, WIDTH:kv_end],
        total[:, kv_end:router_end],
        total[:, router_end : router_end + 5].T,
        part_up,
        part_down,
    )


def solution(mesh):
    both = ("dp", "fsdp")
    placed = (
        P(both, None),
        P(both),
        P(both),
        P(both, None),
        P(both, None),
        P(both, None),
        P(None, both),
        P(both, None),
        P(both, None),
        P(None, both),
        P("fsdp", None, "dp"),
        P("fsdp", "dp", None),
        P(both, None),
        P(both),
    )

    return jax.shard_map(
        on_device,
        mesh=mesh,
        in_specs=placed,
        out_specs=(
            P(both, None),
            P(both),
            P(both, None),
            P(both, None),
            P(None, both),
            P(both, None),
            P(both, None),
            P(None, both),
            P("fsdp", None, "dp"),
            P("fsdp", "dp", None),
        ),
        check_vma=False,
    )
```

```python
from functools import partial

import jax
import jax.numpy as jnp
from jax import lax
from jax.experimental import pallas as pl
from jax.experimental.pallas import tpu as pltpu
from jax.sharding import PartitionSpec as P


D = 512
HEAD = 64
A_EXP = 24
A_TOP = 4
F_TOP = 2
STEP = 2
LANES = 128
BLOCK = 256
HALVES = 2
PAIRS = A_EXP // 2
WIDTH = A_EXP * HEAD
KV_AT = 2 * WIDTH
RV_AT = KV_AT + LANES
PACK = RV_AT + LANES
EPSILON = 1e-05
NEG = -1e30
BF = jnp.bfloat16
F32 = jnp.float32

NN = (((1,), (0,)), ((), ()))
NT = (((1,), (1,)), ((), ()))
TN = (((0,), (0,)), ((), ()))

ROOT_MAX = 31.36
ROOT = (
    0.7978849411010742,
    0.03633308410644531,
    -3.259496588725597e-05,
    -5.530620546778664e-05,
    3.964748430007603e-06,
    -1.3226379280695255e-07,
    1.756186418511163e-09,
)
BELL = -0.7213475204444817
BELL_SCALE = 0.3989422804014327


def dot(a, b, dims=NN):
    return lax.dot_general(a, b, dims, preferred_element_type=F32)


def lane_ids(rows):
    return lax.broadcasted_iota(jnp.int32, (rows, LANES), 1)


def norm_stats(values):
    center = values - jnp.mean(values, axis=-1, keepdims=True)
    inv_std = lax.rsqrt(jnp.mean(center * center, axis=-1, keepdims=True) + EPSILON)
    return center * inv_std, inv_std


def norm_back(grad_normed, normal_part, inv_std, gain_row):
    grad_hat = grad_normed * gain_row
    mean_one = jnp.mean(grad_hat, axis=-1, keepdims=True)
    mean_two = jnp.mean(grad_hat * normal_part, axis=-1, keepdims=True)
    return inv_std * (grad_hat - mean_one - normal_part * mean_two)


def transposed_tail(w_ref):
    return turned_tail(w_ref[:, RV_AT:PACK])


def turned_tail(tail):
    eye = (
        lax.broadcasted_iota(jnp.int32, (LANES, LANES), 0)
        == lax.broadcasted_iota(jnp.int32, (LANES, LANES), 1)
    )
    eye = jnp.where(eye, 1.0, 0.0).astype(BF)
    return dot(eye, tail, NT)


def vector_row(rows_t, first, index):
    return rows_t[first + index : first + index + 1, :]


def split_two(values):
    high = values.astype(BF)
    return high, (values - high.astype(F32)).astype(BF)


def ranks_kernel(capacity, meta_ref, pair_ref, rank_ref, rank_t_ref, place_ref, scal_ref):
    tok = meta_ref.shape[0]
    size = capacity // HALVES
    tri = lax.broadcasted_iota(jnp.int32, (BLOCK, BLOCK), 0) >= lax.broadcasted_iota(
        jnp.int32, (BLOCK, BLOCK), 1
    )
    tri = jnp.where(tri, 1.0, 0.0).astype(BF)
    lane = lane_ids(BLOCK)

    def block(b, carry):
        rows = pl.ds(b * BLOCK, BLOCK)
        meta = meta_ref[rows, :]
        pair = pair_ref[rows, :]
        scal_ref[rows, :] = jnp.where(lane == 0, pair[:, 0:1], pair[:, 1:2])
        pick = ((lane == meta[:, 4:5]) | (lane == meta[:, 5:6])) & (meta[:, 6:7] >= STEP)
        ones = jnp.where(pick, 1.0, 0.0)
        count = dot(tri, ones.astype(BF)) + carry
        rank = jnp.where(pick, count - 1.0, -1.0)
        rank_ref[rows, :] = rank
        place = jnp.full((BLOCK, LANES), -1, jnp.int32)
        for k in range(F_TOP):
            route = meta[:, 4 + k : 5 + k]
            mine = jnp.sum(jnp.where(lane == route, rank, 0.0), axis=1, keepdims=True)
            mine = mine.astype(jnp.int32)
            for h in range(HALVES):
                within = mine - h * size
                dest = jnp.where((within >= 0) & (within < size), route * size + within, -1)
                place = jnp.where(lane == F_TOP * h + k, dest, place)
        place_ref[rows, :] = place
        return count[BLOCK - 1 :, :]

    lax.fori_loop(0, tok // BLOCK, block, jnp.zeros((1, LANES), F32))
    rank_t_ref[...] = jnp.transpose(rank_ref[...])[: rank_t_ref.shape[0], :].astype(jnp.int32)


def gather_pair(rank_t_ref, rows_ref, starts, slots_refs, pair):
    hots, targets = [], []
    for e in (2 * pair, 2 * pair + 1):
        row = rank_t_ref[pl.ds(e, 1), :]
        for start, slots_ref in zip(starts, slots_refs):
            size = slots_ref.shape[1]
            place = lax.broadcasted_iota(jnp.int32, (size, row.shape[1]), 0) + start
            hots.append(jnp.where(place == row, 1.0, 0.0).astype(BF))
            targets.append((slots_ref, e, size))
    rows = dot(jnp.concatenate(hots, axis=0), rows_ref[...]).astype(BF)
    at = 0
    for slots_ref, e, size in targets:
        slots_ref[e] = rows[at : at + size]
        at += size


def gather_kernel(experts, starts, rank_t_ref, rows_ref, *slots_refs):
    def gather(pair, _):
        gather_pair(rank_t_ref, rows_ref, starts, slots_refs, pair)
        return 0

    lax.fori_loop(0, experts // 2, gather, 0)


def one_hot(rank_t_ref, e, capacity):
    row = rank_t_ref[pl.ds(e, 1), :]
    place = lax.broadcasted_iota(jnp.int32, (capacity, row.shape[1]), 0)
    return jnp.where(place == row, 1.0, 0.0).astype(BF)


def select_heads(values, route, lane_half):
    shifted = route - lane_half
    acc = jnp.zeros((values.shape[0], LANES), F32)
    for p in range(PAIRS):
        acc = jnp.where(shifted == 2 * p, values[:, p * LANES : (p + 1) * LANES], acc)
    return acc + pltpu.roll(acc, HEAD, 1)


def spread_heads(pairs, meta, lane, lane_half, store):
    doubled, shifted = [], []
    for k in range(A_TOP):
        half = (lane >= HEAD) if k % 2 else (lane < HEAD)
        part = jnp.where(half, pairs[k // 2], 0.0)
        doubled.append(part + pltpu.roll(part, HEAD, 1))
        shifted.append(meta[:, k : k + 1] - lane_half)
    for p in range(PAIRS):
        acc = jnp.zeros(doubled[0].shape, F32)
        for k in range(A_TOP):
            acc = jnp.where(shifted[k] == 2 * p, doubled[k], acc)
        store(p, acc.astype(BF))


def place_pieces(shape, pieces, w_ref):
    groups, experts, shard = shape
    if len(pieces) == 1:
        w_ref[...] = pieces[0][...]
        return
    mine, group = lax.axis_index("fsdp"), lax.axis_index("dp")
    for m in range(experts):
        base = jnp.bitwise_xor(mine, m) * shard
        for g in range(groups):
            owner = lax.rem(group + g, groups)
            if m < 6:
                block = pieces[m][g]
            else:
                low, high = pieces[6 + 2 * (m - 6)], pieces[7 + 2 * (m - 6)]
                block = low[g] if g < groups // 2 else high[g - groups // 2]
            rows = pl.ds(pl.multiple_of(owner * experts * shard + base, shard), shard)
            w_ref[rows, :] = block


def attend_kernel(experts, shape, *refs):
    tok_ref, meta_ref, rank_t_ref = refs[:3]
    pieces, outs, refs = refs[3:-25], refs[-25:-14], refs[-14:]
    w_ref, slotq_ref, kv_ref, so_ref, lse_ref, gates_ref, mixed_ref, hidden_ref, fgate_ref = refs[:9]
    n2_ref, slots_ref, kx_ref, vx_ref, sems = refs[9:]
    place_pieces(shape, pieces, w_ref)
    tok = tok_ref.shape[0]
    whole_copies = {
        i: pltpu.make_async_copy(refs[i], outs[i], sems.at[i, 0]) for i in (0, 1, 2, 3, 4, 5)
    }
    whole_copies[0].start()

    def row_copies(b, rows):
        return [
            pltpu.make_async_copy(refs[i].at[rows], outs[i].at[rows], sems.at[i, b])
            for i in (6, 7, 8, 9)
        ]

    first = A_EXP + experts
    rows_t = transposed_tail(w_ref)
    gain_one, shift_one, gain_two, shift_two = (vector_row(rows_t, first, i) for i in range(4))
    lane = lane_ids(BLOCK)
    upper = lane >= HEAD
    lane_half = jnp.where(upper, 1, 0)

    def project(b, _):
        rows = pl.ds(b * BLOCK, BLOCK)
        meta = meta_ref[rows, :]
        hat, _ = norm_stats(tok_ref[rows, :].astype(F32))
        normed = (hat * gain_one + shift_one).astype(BF)
        queries = dot(normed, w_ref[:, :WIDTH])
        kv = dot(normed, w_ref[:, KV_AT:RV_AT])
        logits = dot(normed, w_ref[:, RV_AT:PACK])
        kv_ref[rows, :] = kv.astype(BF)
        swapped = pltpu.roll(kv, HEAD, 1)
        kx_ref[0, rows, :] = jnp.where(upper, 0.0, kv).astype(BF)
        kx_ref[1, rows, :] = jnp.where(upper, swapped, 0.0).astype(BF)
        vx_ref[0, rows, :] = jnp.where(upper, 0.0, swapped).astype(BF)
        vx_ref[1, rows, :] = jnp.where(upper, kv, 0.0).astype(BF)
        picked = [select_heads(queries, meta[:, k : k + 1], lane_half) for k in range(A_TOP)]
        for j in range(A_TOP // 2):
            slotq_ref[j, rows, :] = jnp.where(upper, picked[2 * j + 1], picked[2 * j]).astype(BF)
        chosen = [
            jnp.sum(jnp.where(lane == meta[:, k : k + 1], logits, 0.0), axis=1, keepdims=True)
            for k in range(A_TOP)
        ]
        top = jnp.maximum(jnp.maximum(chosen[0], chosen[1]), jnp.maximum(chosen[2], chosen[3]))
        raised = [jnp.exp(c - top) for c in chosen]
        scale = 1.0 / (raised[0] + raised[1] + raised[2] + raised[3])
        gates = jnp.zeros((BLOCK, LANES), F32)
        for k in range(A_TOP):
            gates = jnp.where(lane == k, raised[k] * scale, gates)
        gates_ref[rows, :] = gates
        return 0

    lax.fori_loop(0, tok // BLOCK, project, 0)
    for i in (1, 2, 5):
        whole_copies[i].start()

    below = lax.broadcasted_iota(jnp.int32, (BLOCK, BLOCK), 1) <= lax.broadcasted_iota(
        jnp.int32, (BLOCK, BLOCK), 0
    )
    for i in range(tok // BLOCK):
        rows = slice(i * BLOCK, (i + 1) * BLOCK)
        seen = (i + 1) * BLOCK
        lse_ref[rows, :] = jnp.zeros((BLOCK, LANES), F32)

        def pair(j, _, rows=rows, seen=seen, i=i):
            out = jnp.zeros((BLOCK, LANES), F32)
            query = slotq_ref[j, rows, :]
            logs = lse_ref[rows, :]
            for h in range(2):
                scores = dot(query, kx_ref[h, :seen, :], NT) * (HEAD**-0.5)
                last = jnp.where(below, scores[:, i * BLOCK :], NEG)
                scores = last if i == 0 else jnp.concatenate([scores[:, : i * BLOCK], last], axis=1)
                top = jnp.max(scores, axis=1, keepdims=True)
                raised = jnp.exp(scores - top)
                total = jnp.sum(raised, axis=1, keepdims=True)
                probs = (raised * (1.0 / total)).astype(BF)
                out = out + dot(probs, vx_ref[h, :seen, :])
                logs = jnp.where(lane == 2 * j + h, top + jnp.log(total), logs)
            so_ref[j, rows, :] = out
            lse_ref[rows, :] = logs
            return 0

        lax.fori_loop(0, A_TOP // 2, pair, 0)

    for i in (3, 4):
        whole_copies[i].start()

    def finish(b, _):
        rows = pl.ds(b * BLOCK, BLOCK)
        meta = meta_ref[rows, :]
        gates = gates_ref[rows, :]
        active = jnp.where(meta[:, 6:7] >= STEP, 1.0, 0.0)
        pairs = [
            so_ref[j, rows, :]
            * jnp.where(upper, gates[:, 2 * j + 1 : 2 * j + 2], gates[:, 2 * j : 2 * j + 1])
            for j in range(A_TOP // 2)
        ]

        def store(p, block):
            mixed_ref[rows, p * LANES : (p + 1) * LANES] = block

        spread_heads(pairs, meta, lane, lane_half, store)
        branch = dot(mixed_ref[rows, :], w_ref[:, WIDTH:KV_AT], NT)
        hidden = tok_ref[rows, :].astype(F32) + active * branch
        hidden_ref[rows, :] = hidden
        hat, _ = norm_stats(hidden)
        normed = (hat * gain_two + shift_two).astype(BF)
        n2_ref[rows, :] = normed
        logits = dot(normed, w_ref[:, RV_AT:PACK])
        first_logit, second_logit = (
            jnp.sum(
                jnp.where(lane == meta[:, 4 + k : 5 + k] + A_EXP, logits, 0.0), axis=1, keepdims=True
            )
            for k in range(F_TOP)
        )
        top = jnp.maximum(first_logit, second_logit)
        first_raised, second_raised = jnp.exp(first_logit - top), jnp.exp(second_logit - top)
        scale = 1.0 / (first_raised + second_raised)
        fgate_ref[rows, :] = jnp.where(lane == 0, first_raised * scale, second_raised * scale)
        for copy in row_copies(b, rows):
            copy.start()
        return 0

    lax.fori_loop(0, tok // BLOCK, finish, 0)

    def slots_copy(pair):
        both = pl.ds(2 * pair, 2)
        return pltpu.make_async_copy(slots_ref.at[both], outs[10].at[both], sems.at[10, pair])

    def gather(pair, _):
        gather_pair(rank_t_ref, n2_ref, (0,), (slots_ref,), pair)
        slots_copy(pair).start()
        return 0

    lax.fori_loop(0, experts // 2, gather, 0)
    for pair in range(experts // 2):
        slots_copy(pair).wait()
    for copy in whole_copies.values():
        copy.wait()
    for b in range(tok // BLOCK):
        for copy in row_copies(b, pl.ds(b * BLOCK, BLOCK)):
            copy.wait()


def expert_kernel(parts, x_ref, up_ref, down_ref, out_ref, act_ref, slope_ref, total_ref):
    total_ref[...] = jnp.zeros(total_ref.shape, F32)

    def part(c, _):
        pre = dot(x_ref[...], up_ref[c])
        square = pre * pre
        short = jnp.minimum(square, ROOT_MAX)
        root = ROOT[-1] * short
        for coef in ROOT[-2:0:-1]:
            root = (root + coef) * short
        phi = 0.5 + 0.5 * jnp.tanh(pre * (root + ROOT[0]))
        act = (pre * phi).astype(BF)
        act_ref[c] = act
        bell = jnp.exp2(square * BELL)
        slope_ref[c] = (phi + (pre * BELL_SCALE) * bell).astype(BF)
        total_ref[...] += dot(act, down_ref[c])
        return 0

    lax.fori_loop(0, parts, part, 0, unroll=2)
    out_ref[...] = total_ref[...].astype(BF)


def combine_sums(h, place, back_ref, fgate, cot, halt_row, lane, branch, cols):
    slot = lax.broadcasted_iota(jnp.int32, (BLOCK, back_ref.shape[0]), 1)
    for k in range(F_TOP):
        at = F_TOP * h + k
        hot = jnp.where(slot == place[:, at : at + 1], 1.0, 0.0).astype(BF)
        came = dot(hot, back_ref[...])
        branch = branch + fgate[:, k : k + 1] * came
        one = jnp.sum(came * cot, axis=1, keepdims=True)
        two = jnp.sum(came * halt_row, axis=1, keepdims=True)
        cols = cols + jnp.where(lane == k, one, jnp.where(lane == F_TOP + k, two, 0.0))
    return branch, cols


def split_three(values):
    high = values.astype(BF).astype(F32)
    middle = (values - high).astype(BF).astype(F32)
    return high, middle, values - high - middle


def combine_first_kernel(
    experts,
    back_ref,
    place_ref,
    tail_ref,
    meta_ref,
    fgate_ref,
    cot_ref,
    branch_ref,
    cols_ref,
    live_ref,
    dense_ref,
):
    halt_row = vector_row(turned_tail(tail_ref[...]), A_EXP + experts, 4)
    lane = lane_ids(BLOCK)

    def block(b, _):
        rows = pl.ds(b * BLOCK, BLOCK)
        meta = meta_ref[rows, :]
        fgate = fgate_ref[rows, :]
        branch, cols = combine_sums(
            0,
            place_ref[rows, :],
            back_ref,
            fgate,
            cot_ref[rows, :].astype(F32),
            halt_row,
            lane,
            jnp.zeros((BLOCK, D), F32),
            jnp.zeros((BLOCK, LANES), F32),
        )
        branch_ref[rows, :] = branch
        cols_ref[rows, :] = cols
        active = jnp.where(meta[:, 6:7] >= STEP, 1.0, 0.0)
        dense = jnp.zeros((BLOCK, LANES), F32)
        for k in range(F_TOP):
            named = lane == meta[:, 4 + k : 5 + k]
            dense = jnp.where(named, active * fgate[:, k : k + 1], dense)
        dense_ref[rows, :] = dense
        return 0

    lax.fori_loop(0, branch_ref.shape[0] // BLOCK, block, 0)
    turned = jnp.transpose(dense_ref[...])[: live_ref.shape[1], :]
    for index, part in enumerate(split_three(turned)):
        live_ref[index] = part.astype(BF)


def combine_kernel(
    experts,
    capacity,
    back_ref,
    branch_ref,
    cols_ref,
    live_ref,
    place_ref,
    rank_t_ref,
    hidden_ref,
    tail_ref,
    meta_ref,
    fgate_ref,
    scal_ref,
    cot_ref,
    out_ref,
    halt_ref,
    slope_ref,
    glf_ref,
    row_ref,
    ab_ref,
    kept_ref,
):
    step = pl.program_id(0)
    halt_row = vector_row(turned_tail(tail_ref[...]), A_EXP + experts, 4)
    lane = lane_ids(BLOCK)

    @pl.when(step == 0)
    def _():
        row_ref[...] = jnp.zeros(row_ref.shape, F32)

    meta = meta_ref[...]
    fgate = fgate_ref[...]
    scal = scal_ref[...]
    active = jnp.where(meta[:, 6:7] >= STEP, 1.0, 0.0)
    branch, cols = combine_sums(
        1,
        place_ref[...],
        back_ref,
        fgate,
        cot_ref[...].astype(F32),
        halt_row,
        lane,
        branch_ref[...],
        cols_ref[...],
    )
    z = hidden_ref[...] + active * branch
    out_ref[...] = z.astype(BF)
    prob = 1.0 / (1.0 + jnp.exp(-jnp.sum(z * halt_row, axis=1, keepdims=True)))
    halt_in, cot_halt = scal[:, 0:1], scal[:, 1:2]
    room = active * (1.0 - halt_in) * prob
    slope = cot_halt * room * (1.0 - prob)
    halt_ref[...] = jnp.broadcast_to(halt_in + room, (BLOCK, LANES))
    wide_slope = jnp.broadcast_to(slope, (BLOCK, LANES))
    slope_ref[...] = wide_slope
    kept_ref[pl.ds(step * BLOCK, BLOCK), :] = wide_slope
    row_ref[0:1, :] += jnp.sum(slope * z, axis=0, keepdims=True)
    gfg = [active * (cols[:, k : k + 1] + slope * cols[:, 2 + k : 3 + k]) for k in range(F_TOP)]
    inner = fgate[:, 0:1] * gfg[0] + fgate[:, 1:2] * gfg[1]
    glf = jnp.zeros((BLOCK, LANES), F32)
    for k in range(F_TOP):
        value = fgate[:, k : k + 1] * (gfg[k] - inner)
        glf = jnp.where(lane == meta[:, 4 + k : 5 + k] + A_EXP, value, glf)
    glf_ref[...] = glf

    @pl.when(step == pl.num_programs(0) - 1)
    def _():
        slopes = [part[:1, :] for part in split_three(jnp.transpose(kept_ref[...]))]
        low = [live_ref[i].astype(F32) for i in range(3)]
        tok = kept_ref.shape[0]
        for e in range(experts):
            rows = [part[e : e + 1, :] for part in low] + slopes + [jnp.zeros((2, tok), F32)]
            rows = jnp.concatenate(rows, axis=0).astype(BF)
            ab_ref[e] = dot(rows, one_hot(rank_t_ref, e, capacity), NT).astype(BF)


def data_back_kernel(experts, parts, h, *refs):
    cot_refs, refs = refs[:-8], refs[-8:]
    ab_ref, tail_ref, slope_ref, up_ref, down_ref, gpre_ref, gy_ref, rows_ref = refs
    size = ab_ref.shape[2] // HALVES
    count = ab_ref.shape[0]
    rows = count * size
    halt_row = vector_row(turned_tail(tail_ref[...]), A_EXP + experts, 4)
    cols = []
    cots = []
    for i in range(count):
        ab = ab_ref[i].astype(F32)[:, h * size : (h + 1) * size]
        live = ab[0:1, :] + ab[1:2, :] + ab[2:3, :]
        slope = ab[3:4, :] + ab[4:5, :] + ab[5:6, :]
        filler = jnp.zeros((LANES - 2, size), F32)
        cols.append(jnp.transpose(jnp.concatenate([live, slope, filler], axis=0)))
        for ref in cot_refs:
            part = ref.shape[0] // count
            cots.append(ref[i * part : (i + 1) * part, :].astype(F32))
    cols = jnp.concatenate(cols, axis=0)
    cots = jnp.concatenate(cots, axis=0)
    gy = (cols[:, 0:1] * (cots + cols[:, 1:2] * halt_row)).astype(BF)
    gy_ref[...] = gy
    total = jnp.zeros((rows, D), F32)
    for c in range(parts):
        gpre = (dot(gy, down_ref[c], NT) * slope_ref[c].astype(F32)).astype(BF)
        gpre_ref[c] = gpre
        total = total + dot(gpre, up_ref[c], NT)
    rows_ref[...] = total.astype(BF)


def weight_back_kernel(parts, steps, joined, *refs):
    up_acc, down_acc = refs[-2:]
    step = pl.program_id(0)

    @pl.when(step == 0)
    def _():
        up_acc[...] = jnp.zeros(up_acc.shape, F32)
        down_acc[...] = jnp.zeros(down_acc.shape, F32)

    for h in range(HALVES):
        x_ref, gy_ref, gpre_ref, act_ref = refs[4 * h : 4 * h + 4]

        @pl.when(step // steps == h)
        def _(x_ref=x_ref, gy_ref=gy_ref, gpre_ref=gpre_ref, act_ref=act_ref):
            for c in range(parts):
                up_acc[c] += dot(x_ref[...], gpre_ref[c], TN)
                down_acc[c] += dot(gy_ref[...], act_ref[c], TN)

    @pl.when(step == pl.num_programs(0) - 1)
    def _():
        for c in range(parts):
            if joined:
                refs[-3][c, :D] = up_acc[c].astype(BF)
                refs[-3][c, D:] = jnp.transpose(down_acc[c]).astype(BF)
            else:
                refs[-4][c] = up_acc[c].astype(BF)
                refs[-3][c] = jnp.transpose(down_acc[c]).astype(BF)


def store_grads(ref, values, start):
    columns = slice(start, start + values.shape[1])
    if len(ref.shape) == 2:
        ref[:, columns] = values
        return
    if len(ref.shape) == 5:
        _, chips, groups, shard, _ = ref.shape
        core = jnp.bitwise_and(lax.axis_index("fsdp"), 1)
        for e in range(2 * chips):
            for g in range(groups):
                at = (g * 2 * chips + e) * shard
                side = jnp.bitwise_xor(core, e % 2)
                ref[side, e // 2, g, :, columns] = values[at : at + shard]
        return
    experts, groups, shard, _ = ref.shape
    for e in range(experts):
        for g in range(groups):
            at = (g * experts + e) * shard
            ref[e, g, :, columns] = values[at : at + shard]


def hidden_back_kernel(
    experts,
    capacity,
    first_ref,
    second_ref,
    rank_ref,
    hidden_ref,
    w_ref,
    tail_ref,
    meta_ref,
    cot_ref,
    slope_ref,
    glf_ref,
    mixed_ref,
    so_ref,
    gates_ref,
    lse_ref,
    gout_ref,
    gh_ref,
    gslot_ref,
    gla_ref,
    logs_ref,
    rv_ref,
    vec_ref,
    acc_ref,
):
    step = pl.program_id(0)
    count = hidden_ref.shape[0]
    first = A_EXP + experts
    size = capacity // HALVES
    rows_t = turned_tail(tail_ref[...])
    low_t = rows_t.astype(BF)
    gain_two, shift_two, halt_row = (vector_row(rows_t, first, i) for i in (2, 3, 4))
    lane = lane_ids(count)
    upper = lane >= HEAD
    lane_half = jnp.where(upper, 1, 0)

    @pl.when(step == 0)
    def _():
        vec_ref[...] = jnp.zeros(vec_ref.shape, F32)
        acc_ref[...] = jnp.zeros(acc_ref.shape, F32)
        rv_ref[...] = jnp.zeros(rv_ref.shape, F32)

    meta = meta_ref[...]
    rank = rank_ref[...].astype(jnp.int32)
    active = jnp.where(meta[:, 6:7] >= STEP, 1.0, 0.0)
    place = lax.broadcasted_iota(jnp.int32, (count, size), 1)
    glf_high, glf_low = split_two(glf_ref[...])
    grad = dot(glf_high, low_t) + dot(glf_low, low_t)
    for h, back_ref in enumerate((first_ref, second_ref)):
        for e in range(experts):
            hot = jnp.where(place + h * size == rank[:, e : e + 1], 1.0, 0.0).astype(BF)
            grad = grad + dot(hot, back_ref[e])
    hat, inv = norm_stats(hidden_ref[...])
    normed = (hat * gain_two + shift_two).astype(BF)
    rv_ref[...] += dot(normed, glf_high, TN) + dot(normed, glf_low, TN)
    vec_ref[2:3, :] += jnp.sum(grad * hat, axis=0, keepdims=True)
    vec_ref[3:4, :] += jnp.sum(grad, axis=0, keepdims=True)
    gz = cot_ref[...].astype(F32) + slope_ref[:, 0:1] * halt_row
    gh = gz + norm_back(grad, hat, inv, gain_two)
    gh_ref[...] = gh
    ga = (active * gh).astype(BF)
    acc_ref[...] += dot(ga, mixed_ref[...], TN)
    gm = dot(ga, w_ref[...])
    gates = gates_ref[...]
    weighted = jnp.zeros((count, 1), F32)
    grads = []
    picked = [select_heads(gm, meta[:, k : k + 1], lane_half) for k in range(A_TOP)]
    for j in range(A_TOP // 2):
        both = jnp.where(upper, picked[2 * j + 1], picked[2 * j])
        prod = both * so_ref[j]
        scale = jnp.where(upper, gates[:, 2 * j + 1 : 2 * j + 2], gates[:, 2 * j : 2 * j + 1])
        gslot_ref[j] = (both * scale).astype(BF)
        grads.append(jnp.sum(jnp.where(upper, 0.0, prod), axis=1, keepdims=True))
        grads.append(jnp.sum(jnp.where(upper, prod, 0.0), axis=1, keepdims=True))
    logs = lse_ref[...]
    for k in range(A_TOP):
        inner = gates[:, k : k + 1] * grads[k]
        weighted = weighted + inner
        logs = jnp.where(lane == A_TOP + k, inner, logs)
    logs_ref[...] = logs
    gla = jnp.zeros((count, LANES), F32)
    for k in range(A_TOP):
        value = gates[:, k : k + 1] * (grads[k] - weighted)
        gla = jnp.where(lane == meta[:, k : k + 1], value, gla)
    gla_ref[...] = gla

    @pl.when(step == pl.num_programs(0) - 1)
    def _():
        store_grads(gout_ref, acc_ref[...].astype(BF), 0)


def input_back_kernel(
    experts,
    tok_ref,
    w_ref,
    meta_ref,
    gh_ref,
    gslot_ref,
    gla_ref,
    rvin_ref,
    vecin_ref,
    halt_ref,
    lse_ref,
    slotq_ref,
    kv_ref,
    gin_ref,
    pack_ref,
    gx_ref,
    wide_ref,
    acc_ref,
    rv_ref,
    vec_ref,
    kx_ref,
    vx_ref,
    lset_ref,
    gq_ref,
):
    tok = tok_ref.shape[0]
    blocks = tok // BLOCK
    first = A_EXP + experts
    rows_t = transposed_tail(w_ref)
    low_t = rows_t.astype(BF)
    gain_one, shift_one = (vector_row(rows_t, first, i) for i in range(2))
    lane = lane_ids(BLOCK)
    upper = lane >= HEAD
    lane_half = jnp.where(upper, 1, 0)
    all_upper = lane_ids(tok) >= HEAD
    vec_ref[...] = jnp.zeros(vec_ref.shape, F32)
    vec_ref[2:4, :] = vecin_ref[2:4, :]
    vec_ref[4:5, :] = halt_ref[0:1, :]
    acc_ref[...] = jnp.zeros(acc_ref.shape, F32)
    rv_ref[...] = rvin_ref[...]
    kv = kv_ref[...].astype(F32)
    swapped = pltpu.roll(kv, HEAD, 1)
    kx_ref[0] = jnp.where(all_upper, 0.0, kv).astype(BF)
    kx_ref[1] = jnp.where(all_upper, swapped, 0.0).astype(BF)
    vx_ref[0] = jnp.where(all_upper, 0.0, swapped).astype(BF)
    vx_ref[1] = jnp.where(all_upper, kv, 0.0).astype(BF)
    lset_ref[...] = jnp.transpose(lse_ref[...])

    above = lax.broadcasted_iota(jnp.int32, (BLOCK, BLOCK), 0) <= lax.broadcasted_iota(
        jnp.int32, (BLOCK, BLOCK), 1
    )
    gx_ref[...] = jnp.zeros(gx_ref.shape, F32)
    for i in range(blocks):
        rows = slice(i * BLOCK, (i + 1) * BLOCK)
        seen = (i + 1) * BLOCK

        def pair(j, _, rows=rows, seen=seen, i=i):
            query = (slotq_ref[j, rows, :].astype(F32) * (HEAD**-0.5)).astype(BF)
            gslot = gslot_ref[j, rows, :]
            gq = jnp.zeros((BLOCK, LANES), F32)
            for h in range(2):
                keys = kx_ref[h, :seen, :]
                log = lset_ref[pl.ds(2 * j + h, 1), rows]
                scores = dot(keys, query, NT) - log
                last = jnp.where(above, scores[i * BLOCK :, :], NEG)
                scores = last if i == 0 else jnp.concatenate([scores[: i * BLOCK], last], axis=0)
                probs = jnp.exp(scores)
                gprob = dot(vx_ref[h, :seen, :], gslot, NT)
                inner = lset_ref[pl.ds(A_TOP + 2 * j + h, 1), rows]
                gs = (probs * (gprob - inner)).astype(BF)
                gq = gq + dot(gs, keys, TN)
                gx_ref[0, h, :seen, :] += dot(gs, query)
                gx_ref[1, h, :seen, :] += dot(probs.astype(BF), gslot)
            gq_ref[j, rows, :] = gq * (HEAD**-0.5)
            return 0

        lax.fori_loop(0, A_TOP // 2, pair, 0)

    def input_back(b, gkv_sum):
        rows = pl.ds(b * BLOCK, BLOCK)
        meta = meta_ref[rows, :]
        pairs = [gq_ref[j, rows, :] for j in range(A_TOP // 2)]

        def store(p, block):
            wide_ref[:, p * LANES : (p + 1) * LANES] = block

        spread_heads(pairs, meta, lane, lane_half, store)
        gkeys = gx_ref[0, 0, rows, :] + pltpu.roll(gx_ref[0, 1, rows, :], HEAD, 1)
        gvals = pltpu.roll(gx_ref[1, 0, rows, :], HEAD, 1) + gx_ref[1, 1, rows, :]
        gkv = jnp.where(upper, gvals, gkeys).astype(BF)
        gla_high, gla_low = split_two(gla_ref[rows, :])
        grad = dot(wide_ref[...], w_ref[:, :WIDTH], NT)
        grad = grad + dot(gkv, w_ref[:, KV_AT:RV_AT], NT)
        grad = grad + dot(gla_high, low_t) + dot(gla_low, low_t)
        hat, inv = norm_stats(tok_ref[rows, :].astype(F32))
        normed = (hat * gain_one + shift_one).astype(BF)
        acc_ref[...] += dot(normed, wide_ref[...], TN)
        rv_ref[...] += dot(normed, gla_high, TN) + dot(normed, gla_low, TN)
        vec_ref[0:1, :] += jnp.sum(grad * hat, axis=0, keepdims=True)
        vec_ref[1:2, :] += jnp.sum(grad, axis=0, keepdims=True)
        gin_ref[rows, :] = (gh_ref[rows, :] + norm_back(grad, hat, inv, gain_one)).astype(BF)
        return gkv_sum + dot(normed, gkv, TN)

    gkv_sum = lax.fori_loop(0, blocks, input_back, jnp.zeros((D, LANES), F32))
    store_grads(pack_ref, acc_ref[...].astype(BF), 0)
    store_grads(pack_ref, gkv_sum.astype(BF), WIDTH)
    turned = pltpu.roll(jnp.transpose(vec_ref[...]), first, 1)
    tail = jnp.where(lane_ids(D) < first, rv_ref[...], turned)
    store_grads(pack_ref, tail.astype(BF), WIDTH + LANES)


VMEM_LIMIT = 60 * 1024 * 1024
VMEM_ALL = 67043328


def whole(shape, dtype):
    return jax.ShapeDtypeStruct(shape, dtype)


def in_vmem(count):
    return [pl.BlockSpec(memory_space=pltpu.VMEM)] * count


def call(kernel, inputs, outs, scratch=(), limit=VMEM_LIMIT):
    return pl.pallas_call(
        kernel,
        out_shape=outs,
        in_specs=in_vmem(len(inputs)),
        out_specs=in_vmem(len(outs)),
        scratch_shapes=list(scratch),
        compiler_params=pltpu.CompilerParams(vmem_limit_bytes=limit),
    )(*inputs)


def constant_spec(shape, middle=0):
    return pl.BlockSpec(shape, lambda s: (0, middle, 0), pipeline_mode=pl.Buffered(1))


def gather_pieces(pack, shape):
    groups, experts, _ = shape
    if experts != 8 or groups != 4:
        own = lax.all_gather(pack, "dp", axis=0, tiled=False)
        every = lax.all_gather(own, "fsdp", axis=0, tiled=False)
        return [every.transpose(1, 0, 2, 3).reshape(D, PACK)]

    own = [pack]
    for d in range(1, groups):
        pairs = [((i + d) % groups, i) for i in range(groups)]
        own.append(lax.ppermute(pack, "dp", pairs))
    own = jnp.stack(own)

    def swap(values, m):
        return lax.ppermute(values, "fsdp", [(i, i ^ m) for i in range(experts)])

    along = swap(own, 2)
    across = swap(own, 4)
    low = swap(along[: groups // 2], 4)
    high = swap(across[groups // 2 :], 2)
    return [
        own,
        swap(own, 1),
        along,
        swap(along, 1),
        across,
        swap(across, 1),
        low,
        high,
        swap(low, 1),
        swap(high, 1),
    ]


def on_device(
    tokens,
    halt_in,
    depths,
    attn_routes,
    ffn_routes,
    w_query,
    w_out,
    w_kv,
    router,
    vectors,
    w_up,
    w_down,
    cot_out,
    cot_halt,
):
    tok = tokens.shape[0]
    groups, experts = lax.axis_size("dp"), lax.axis_size("fsdp")
    capacity = 2 * F_TOP * tok // experts
    slice_width = w_up.shape[2]
    shard = w_query.shape[0]
    slots = experts * capacity

    tail = jnp.concatenate([router, vectors.T], axis=1)
    tail = jnp.pad(tail, ((0, 0), (0, LANES - tail.shape[1])))
    pack = jnp.concatenate([w_query, w_out.T, w_kv, tail], axis=1)
    shape = (groups, experts, shard)
    pieces = gather_pieces(pack, shape)
    joined = slice_width == D
    if joined:
        expert_pack = jnp.concatenate([w_up[0], w_down[0]], axis=0)
        whole_up = whole_down = lax.all_gather(expert_pack, "dp", axis=0, tiled=False)
    else:
        whole_up = lax.all_gather(w_up[0], "dp", axis=0, tiled=False)
        whole_down = lax.all_gather(w_down[0], "dp", axis=0, tiled=False)

    meta = jnp.concatenate([attn_routes, ffn_routes, depths[:, None], depths[:, None]], axis=1)
    scal = jnp.stack([halt_in, cot_halt], axis=1)
    half = capacity // HALVES
    half_slots = slots // HALVES

    rank, rank_t, place, scal = call(
        partial(ranks_kernel, capacity),
        (meta, scal),
        (
            whole((tok, LANES), F32),
            whole((experts, tok), jnp.int32),
            whole((tok, LANES), jnp.int32),
            whole((tok, LANES), F32),
        ),
    )

    def gather_rows(rows, name, starts):
        ends = starts[1:] + (starts[0] + half,)
        shapes = [whole((experts, end - start, D), BF) for start, end in zip(starts, ends)]
        limit = VMEM_LIMIT if name == "cot_slots" else VMEM_ALL
        return call(partial(gather_kernel, experts, starts), (rank_t, rows), shapes, limit=limit)

    cot_slots = gather_rows(cot_out, "cot_slots", (0,))

    def exchange(values):
        came = lax.all_to_all(values, "fsdp", split_axis=0, concat_axis=0, tiled=True)
        return came

    *pieces, cot_first = lax.optimization_barrier((*pieces, cot_slots[0]))
    owned_cot = [exchange(cot_first)]

    attend_outs = (
        whole((D, PACK), BF),
        whole((2, tok, LANES), BF),
        whole((tok, LANES), BF),
        whole((2, tok, LANES), F32),
        whole((tok, LANES), F32),
        whole((tok, LANES), F32),
        whole((tok, WIDTH), BF),
        whole((tok, D), F32),
        whole((tok, LANES), F32),
        whole((tok, D), BF),
        whole((experts, half, D), BF),
    )
    weights, slotq, kv, so, lse, gates, mixed, hidden, fgate, normed_two, sent = pl.pallas_call(
        partial(attend_kernel, experts, shape),
        name="attend",
        out_shape=attend_outs,
        in_specs=in_vmem(3 + len(pieces)),
        out_specs=[pl.BlockSpec(memory_space=pl.ANY)] * len(attend_outs),
        scratch_shapes=[pltpu.VMEM(out.shape, out.dtype) for out in attend_outs]
        + [
            pltpu.VMEM((2, tok, LANES), BF),
            pltpu.VMEM((2, tok, LANES), BF),
            pltpu.SemaphoreType.DMA((len(attend_outs), max(tok // BLOCK, experts // 2))),
        ],
        compiler_params=pltpu.CompilerParams(vmem_limit_bytes=VMEM_ALL),
    )(tokens, meta, rank_t, *pieces)
    n2_slots = [sent, *gather_rows(normed_two, "dispatch_1", (half,))]
    n2_slots[0], owned_cot[0] = lax.optimization_barrier((n2_slots[0], owned_cot[0]))
    cot_slots += gather_rows(cot_out, "cot_late", (half, half + half // 2))

    up_spec = constant_spec((groups, D, slice_width))
    down_spec = constant_spec((groups, slice_width, D), 1 if joined else 0)
    params = pltpu.CompilerParams(vmem_limit_bytes=VMEM_ALL)
    wide = whole((groups, half_slots, slice_width), BF)
    narrow = whole((half_slots, D), BF)
    step_rows = max(half, min(512, half_slots))
    step_spec = pl.BlockSpec((step_rows, D), lambda s: (s, 0))
    step_wide = pl.BlockSpec((groups, step_rows, slice_width), lambda s: (0, s, 0))

    owned = []
    for h in range(HALVES):
        owned.append(exchange(n2_slots[h]).reshape(half_slots, D))
        if h + 1 < HALVES:
            n2_slots[h + 1], owned[h] = lax.optimization_barrier((n2_slots[h + 1], owned[h]))
    outs, acts, slopes = [], [], []
    for h in range(HALVES):
        out, act, slope = pl.pallas_call(
            partial(expert_kernel, groups),
            grid=(half_slots // step_rows,),
            out_shape=(narrow, wide, wide),
            in_specs=[step_spec, up_spec, down_spec],
            out_specs=[step_spec, step_wide, step_wide],
            scratch_shapes=[pltpu.VMEM((step_rows, D), F32)],
            compiler_params=params,
        )(owned[h], whole_up, whole_down)
        outs.append(out)
        acts.append(act)
        slopes.append(slope)
    back = []
    for h in range(HALVES):
        back.append(exchange(outs[h].reshape(experts, half, D)).reshape(half_slots, D))

    tail_spec = pl.BlockSpec((D, LANES), lambda s: (0, RV_AT // LANES))
    full = pl.BlockSpec(memory_space=pltpu.VMEM)
    sums = pl.pallas_call(
        partial(combine_first_kernel, experts),
        name="combine_first",
        grid=(1,),
        out_shape=(
            whole((tok, D), F32),
            whole((tok, LANES), F32),
            whole((3, max(16, experts), tok), BF),
        ),
        in_specs=[full, full, tail_spec, full, full, full],
        out_specs=[full] * 3,
        scratch_shapes=[pltpu.VMEM((tok, LANES), F32)],
        compiler_params=params,
    )(back[0], place, weights, meta, fgate, cot_out)
    back[1], cot_second = lax.optimization_barrier((back[1], cot_slots[1]))
    owned_cot.append(exchange(cot_second))

    def tokens_of(width, count=BLOCK):
        return pl.BlockSpec((count, width), lambda b: (b, 0))

    block_out, halt_wide, halt_slope, glf, halt_grad, ab = pl.pallas_call(
        partial(combine_kernel, experts, capacity),
        name="combine",
        grid=(tok // BLOCK,),
        out_shape=(
            whole((tok, D), BF),
            whole((tok, LANES), F32),
            whole((tok, LANES), F32),
            whole((tok, LANES), F32),
            whole((8, D), F32),
            whole((experts, 8, capacity), BF),
        ),
        in_specs=[
            full,
            tokens_of(D),
            tokens_of(LANES),
            full,
            tokens_of(LANES),
            full,
            tokens_of(D),
            tail_spec,
            tokens_of(meta.shape[1]),
            tokens_of(LANES),
            tokens_of(LANES),
            tokens_of(D),
        ],
        out_specs=[tokens_of(D)] + [tokens_of(LANES)] * 3 + [full] * 2,
        scratch_shapes=[pltpu.VMEM((tok, LANES), F32)],
        compiler_params=params,
    )(back[1], *sums, place, rank_t, hidden, weights, meta, fgate, scal, cot_out)
    halt_out = halt_wide[:, 0]
    ab, owned_cot[1] = lax.optimization_barrier((ab, owned_cot[1]))
    owned_ab = exchange(ab)
    owned_ab, cot_third = lax.optimization_barrier((owned_ab, cot_slots[2]))
    owned_cot.append(exchange(cot_third))
    cot_parts = [owned_cot[:1], owned_cot[1:]]

    together = step_rows // half if half % LANES == 0 else 1
    row_spec = pl.BlockSpec((together * half, D), lambda s: (s, 0))
    wide_spec = pl.BlockSpec((groups, together * half, slice_width), lambda s: (0, s, 0))
    gys, gpres, rows_back = [], [], []
    for h in range(HALVES):
        gpre, gy, owned_rows = pl.pallas_call(
            partial(data_back_kernel, experts, groups, h),
            grid=(experts // together,),
            out_shape=(wide, narrow, narrow),
            in_specs=[
                *(pl.BlockSpec((together * part.shape[1], D), lambda s: (s, 0)) for part in cot_parts[h]),
                pl.BlockSpec((together, 8, capacity), lambda s: (s, 0, 0)),
                tail_spec,
                wide_spec,
                up_spec,
                down_spec,
            ],
            out_specs=[wide_spec, row_spec, row_spec],
            compiler_params=params,
        )(
            *(part.reshape(-1, D) for part in cot_parts[h]),
            owned_ab,
            weights,
            slopes[h],
            whole_up,
            whole_down,
        )
        gys.append(gy)
        gpres.append(gpre)
        rows_back.append(exchange(owned_rows.reshape(experts, half, D)))

    steps = half_slots // step_rows
    specs, inputs = [], []
    for h in range(HALVES):

        def at(s, h=h):
            return jnp.clip(s - h * steps, 0, steps - 1)

        narrow_at = pl.BlockSpec((step_rows, D), lambda s, at=at: (at(s), 0))
        wide_at = pl.BlockSpec((groups, step_rows, slice_width), lambda s, at=at: (0, at(s), 0))
        specs += [narrow_at, narrow_at, wide_at, wide_at]
        inputs += [owned[h], gys[h], gpres[h], acts[h]]
    if joined:
        grad_shapes = [(groups, 2 * D, D)]
    else:
        grad_shapes = [(groups, D, slice_width), (groups, slice_width, D)]
    expert_grads = pl.pallas_call(
        partial(weight_back_kernel, groups, steps, joined),
        name="weight_back",
        grid=(HALVES * steps,),
        out_shape=[whole(g, BF) for g in grad_shapes],
        in_specs=specs,
        out_specs=[constant_spec(g) for g in grad_shapes],
        scratch_shapes=[pltpu.VMEM((groups, D, slice_width), F32)] * 2,
        compiler_params=params,
    )(*inputs)
    expert_grads = [
        lax.psum_scatter(g, "dp", scatter_dimension=0, tiled=True) for g in expert_grads
    ]
    expert_grads = [g.astype(F32) for g in expert_grads]
    if joined:
        part_up, part_down = expert_grads[0][:, :D], expert_grads[0][:, D:]
    else:
        part_up, part_down = expert_grads

    ordered = shard % 16 == 0

    def grads_shape(width):
        return whole((experts, groups, shard, width) if ordered else (D, width), BF)

    wide_block = BLOCK
    pair_spec = pl.BlockSpec((2, wide_block, LANES), lambda b: (0, b, 0))
    lanes_spec = tokens_of(LANES, wide_block)
    grad_out, gh, gslot, gla, logs, rv, vec = pl.pallas_call(
        partial(hidden_back_kernel, experts, capacity),
        name="hidden_back",
        grid=(tok // wide_block,),
        out_shape=(
            grads_shape(WIDTH),
            whole((tok, D), F32),
            whole((2, tok, LANES), BF),
            whole((tok, LANES), F32),
            whole((tok, LANES), F32),
            whole((D, LANES), F32),
            whole((8, D), F32),
        ),
        in_specs=[
            full,
            full,
            lanes_spec,
            tokens_of(D, wide_block),
            pl.BlockSpec((D, WIDTH), lambda b: (0, 1), pipeline_mode=pl.Buffered(1)),
            tail_spec,
            tokens_of(meta.shape[1], wide_block),
            tokens_of(D, wide_block),
            lanes_spec,
            lanes_spec,
            tokens_of(WIDTH, wide_block),
            pair_spec,
            lanes_spec,
            lanes_spec,
        ],
        out_specs=[full, tokens_of(D, wide_block), pair_spec, lanes_spec, lanes_spec, full, full],
        scratch_shapes=[pltpu.VMEM((D, WIDTH), F32)],
        compiler_params=pltpu.CompilerParams(vmem_limit_bytes=VMEM_LIMIT),
    )(
        *rows_back,
        rank,
        hidden,
        weights,
        weights,
        meta,
        cot_out,
        halt_slope,
        glf,
        mixed,
        so,
        gates,
        lse,
    )

    def reduced(sent):
        if not ordered:
            sent = sent.reshape(groups, experts, shard, sent.shape[1]).transpose(1, 0, 2, 3)
        return jnp.sum(exchange(sent).astype(F32), axis=0).astype(BF)

    part_out = reduced(grad_out)
    paired = ordered and experts == 8
    last_shape = grads_shape(WIDTH + 2 * LANES)
    if paired:
        last_shape = whole((2, experts // 2, groups, shard, WIDTH + 2 * LANES), BF)

    def reduced_last(grads):
        if not paired:
            return reduced(grads)
        other = lax.ppermute(grads, "fsdp", [(i, i ^ 1) for i in range(experts)])
        chip = (grads[0].astype(F32) + other[1].astype(F32)).astype(BF)
        same = [list(range(c, experts, 2)) for c in range(2)]
        came = lax.all_to_all(
            chip, "fsdp", split_axis=0, concat_axis=0, tiled=True, axis_index_groups=same
        )
        return jnp.sum(came.astype(F32), axis=0).astype(BF)

    grad_in, grads = call(
        partial(input_back_kernel, experts),
        (tokens, weights, meta, gh, gslot, gla, rv, vec, halt_grad, logs, slotq, kv),
        (whole((tok, D), BF), last_shape),
        (
            pltpu.VMEM((2, 2, tok, LANES), F32),
            pltpu.VMEM((BLOCK, WIDTH), BF),
            pltpu.VMEM((D, WIDTH), F32),
            pltpu.VMEM((D, LANES), F32),
            pltpu.VMEM((LANES, D), F32),
            pltpu.VMEM((2, tok, LANES), BF),
            pltpu.VMEM((2, tok, LANES), BF),
            pltpu.VMEM((LANES, tok), F32),
            pltpu.VMEM((2, tok, LANES), F32),
        ),
    )
    part = jnp.concatenate([reduced_last(grads), part_out], axis=2)
    came = lax.all_to_all(part, "dp", split_axis=0, concat_axis=0, tiled=True)
    total = jnp.sum(came.astype(F32), axis=0)
    kv_end = WIDTH + LANES
    router_end = kv_end + A_EXP + experts
    return (
        block_out,
        halt_out,
        grad_in,
        total[:, :WIDTH],
        total[:, WIDTH + 2 * LANES :].T,
        total[:, WIDTH:kv_end],
        total[:, kv_end:router_end],
        total[:, router_end : router_end + 5].T,
        part_up,
        part_down,
    )


def solution(mesh):
    both = ("dp", "fsdp")
    placed = (
        P(both, None),
        P(both),
        P(both),
        P(both, None),
        P(both, None),
        P(both, None),
        P(None, both),
        P(both, None),
        P(both, None),
        P(None, both),
        P("fsdp", None, "dp"),
        P("fsdp", "dp", None),
        P(both, None),
        P(both),
    )

    return jax.shard_map(
        on_device,
        mesh=mesh,
        in_specs=placed,
        out_specs=(
            P(both, None),
            P(both),
            P(both, None),
            P(both, None),
            P(None, both),
            P(both, None),
            P(both, None),
            P(None, both),
            P("fsdp", None, "dp"),
            P("fsdp", "dp", None),
        ),
        check_vma=False,
    )
```

```python
from functools import partial

import jax
import jax.numpy as jnp
from jax import lax
from jax.experimental import pallas as pl
from jax.experimental.pallas import tpu as pltpu
from jax.sharding import PartitionSpec as P


D = 512
HEAD = 64
A_EXP = 24
A_TOP = 4
F_TOP = 2
STEP = 2
LANES = 128
BLOCK = 256
HALVES = 2
PAIRS = A_EXP // 2
WIDTH = A_EXP * HEAD
KV_AT = 2 * WIDTH
RV_AT = KV_AT + LANES
PACK = RV_AT + LANES
EPSILON = 1e-05
NEG = -1e30
BF = jnp.bfloat16
F32 = jnp.float32

NN = (((1,), (0,)), ((), ()))
NT = (((1,), (1,)), ((), ()))
TN = (((0,), (0,)), ((), ()))

ROOT_MAX = 31.36
ROOT = (
    0.7978849411010742,
    0.03633308410644531,
    -3.259496588725597e-05,
    -5.530620546778664e-05,
    3.964748430007603e-06,
    -1.3226379280695255e-07,
    1.756186418511163e-09,
)
BELL = -0.7213475204444817
BELL_SCALE = 0.3989422804014327


def dot(a, b, dims=NN):
    return lax.dot_general(a, b, dims, preferred_element_type=F32)


def lane_ids(rows):
    return lax.broadcasted_iota(jnp.int32, (rows, LANES), 1)


def norm_stats(values):
    center = values - jnp.mean(values, axis=-1, keepdims=True)
    inv_std = lax.rsqrt(jnp.mean(center * center, axis=-1, keepdims=True) + EPSILON)
    return center * inv_std, inv_std


def norm_back(grad_normed, normal_part, inv_std, gain_row):
    grad_hat = grad_normed * gain_row
    mean_one = jnp.mean(grad_hat, axis=-1, keepdims=True)
    mean_two = jnp.mean(grad_hat * normal_part, axis=-1, keepdims=True)
    return inv_std * (grad_hat - mean_one - normal_part * mean_two)


def transposed_tail(w_ref):
    return turned_tail(w_ref[:, RV_AT:PACK])


def turned_tail(tail):
    eye = (
        lax.broadcasted_iota(jnp.int32, (LANES, LANES), 0)
        == lax.broadcasted_iota(jnp.int32, (LANES, LANES), 1)
    )
    eye = jnp.where(eye, 1.0, 0.0).astype(BF)
    return dot(eye, tail, NT)


def vector_row(rows_t, first, index):
    return rows_t[first + index : first + index + 1, :]


def split_two(values):
    high = values.astype(BF)
    return high, (values - high.astype(F32)).astype(BF)


def ranks_kernel(meta_ref, rank_ref, rank_t_ref):
    tok = meta_ref.shape[0]
    tri = lax.broadcasted_iota(jnp.int32, (BLOCK, BLOCK), 0) >= lax.broadcasted_iota(
        jnp.int32, (BLOCK, BLOCK), 1
    )
    tri = jnp.where(tri, 1.0, 0.0).astype(BF)
    lane = lane_ids(BLOCK)

    def block(b, carry):
        rows = pl.ds(b * BLOCK, BLOCK)
        meta = meta_ref[rows, :]
        pick = ((lane == meta[:, 4:5]) | (lane == meta[:, 5:6])) & (meta[:, 6:7] >= STEP)
        count = dot(tri, jnp.where(pick, 1.0, 0.0).astype(BF)) + carry
        rank_ref[rows, :] = jnp.where(pick, count - 1.0, -1.0)
        return count[BLOCK - 1 :, :]

    lax.fori_loop(0, tok // BLOCK, block, jnp.zeros((1, LANES), F32))
    rank_t_ref[...] = jnp.transpose(rank_ref[...])[: rank_t_ref.shape[0], :].astype(jnp.int32)


def slot_places(capacity, meta, rank, lane):
    size = capacity // HALVES
    place = jnp.full(rank.shape, -1, jnp.int32)
    for k in range(F_TOP):
        route = meta[:, 4 + k : 5 + k]
        mine = jnp.sum(jnp.where(lane == route, rank, 0.0), axis=1, keepdims=True)
        mine = mine.astype(jnp.int32)
        for h in range(HALVES):
            within = mine - h * size
            dest = jnp.where((within >= 0) & (within < size), route * size + within, -1)
            place = jnp.where(lane == F_TOP * h + k, dest, place)
    return place


def gather_pair(rank_t_ref, rows_ref, starts, slots_refs, pair):
    hots, targets = [], []
    for e in (2 * pair, 2 * pair + 1):
        row = rank_t_ref[pl.ds(e, 1), :]
        for start, slots_ref in zip(starts, slots_refs):
            size = slots_ref.shape[1]
            place = lax.broadcasted_iota(jnp.int32, (size, row.shape[1]), 0) + start
            hots.append(jnp.where(place == row, 1.0, 0.0).astype(BF))
            targets.append((slots_ref, e, size))
    rows = dot(jnp.concatenate(hots, axis=0), rows_ref[...]).astype(BF)
    at = 0
    for slots_ref, e, size in targets:
        slots_ref[e] = rows[at : at + size]
        at += size


def gather_kernel(experts, starts, rank_t_ref, rows_ref, *slots_refs):
    def gather(pair, _):
        gather_pair(rank_t_ref, rows_ref, starts, slots_refs, pair)
        return 0

    lax.fori_loop(0, experts // 2, gather, 0)


def one_hot(rank_t_ref, e, capacity):
    row = rank_t_ref[pl.ds(e, 1), :]
    place = lax.broadcasted_iota(jnp.int32, (capacity, row.shape[1]), 0)
    return jnp.where(place == row, 1.0, 0.0).astype(BF)


def select_heads(values, route, lane_half):
    shifted = route - lane_half
    acc = jnp.zeros((values.shape[0], LANES), F32)
    for p in range(PAIRS):
        acc = jnp.where(shifted == 2 * p, values[:, p * LANES : (p + 1) * LANES], acc)
    return acc + pltpu.roll(acc, HEAD, 1)


def spread_heads(pairs, meta, lane, lane_half, store):
    doubled, shifted = [], []
    for k in range(A_TOP):
        half = (lane >= HEAD) if k % 2 else (lane < HEAD)
        part = jnp.where(half, pairs[k // 2], 0.0)
        doubled.append(part + pltpu.roll(part, HEAD, 1))
        shifted.append(meta[:, k : k + 1] - lane_half)
    for p in range(PAIRS):
        acc = jnp.zeros(doubled[0].shape, F32)
        for k in range(A_TOP):
            acc = jnp.where(shifted[k] == 2 * p, doubled[k], acc)
        store(p, acc.astype(BF))


def place_pieces(shape, pieces, w_ref):
    groups, experts, shard = shape
    if len(pieces) == 1:
        w_ref[...] = pieces[0][...]
        return
    mine, group = lax.axis_index("fsdp"), lax.axis_index("dp")
    for m in range(experts):
        base = jnp.bitwise_xor(mine, m) * shard
        for g in range(groups):
            owner = lax.rem(group + g, groups)
            if m < 6:
                block = pieces[m][g]
            else:
                low, high = pieces[6 + 2 * (m - 6)], pieces[7 + 2 * (m - 6)]
                block = low[g] if g < groups // 2 else high[g - groups // 2]
            rows = pl.ds(pl.multiple_of(owner * experts * shard + base, shard), shard)
            w_ref[rows, :] = block


def attend_kernel(experts, shape, *refs):
    tok_ref, meta_ref, rank_t_ref = refs[:3]
    pieces, outs, refs = refs[3:-25], refs[-25:-14], refs[-14:]
    w_ref, slotq_ref, kv_ref, so_ref, lse_ref, gates_ref, mixed_ref, hidden_ref, fgate_ref = refs[:9]
    n2_ref, slots_ref, kx_ref, vx_ref, sems = refs[9:]
    place_pieces(shape, pieces, w_ref)
    tok = tok_ref.shape[0]
    whole_copies = {
        i: pltpu.make_async_copy(refs[i], outs[i], sems.at[i, 0]) for i in (0, 1, 2, 3, 4, 5)
    }
    whole_copies[0].start()

    def row_copies(b, rows):
        return [
            pltpu.make_async_copy(refs[i].at[rows], outs[i].at[rows], sems.at[i, b])
            for i in (6, 7, 8, 9)
        ]

    first = A_EXP + experts
    rows_t = transposed_tail(w_ref)
    gain_one, shift_one, gain_two, shift_two = (vector_row(rows_t, first, i) for i in range(4))
    lane = lane_ids(BLOCK)
    upper = lane >= HEAD
    lane_half = jnp.where(upper, 1, 0)

    def project(b, _):
        rows = pl.ds(b * BLOCK, BLOCK)
        meta = meta_ref[rows, :]
        hat, _ = norm_stats(tok_ref[rows, :].astype(F32))
        normed = (hat * gain_one + shift_one).astype(BF)
        queries = dot(normed, w_ref[:, :WIDTH])
        kv = dot(normed, w_ref[:, KV_AT:RV_AT])
        logits = dot(normed, w_ref[:, RV_AT:PACK])
        kv_ref[rows, :] = kv.astype(BF)
        swapped = pltpu.roll(kv, HEAD, 1)
        kx_ref[0, rows, :] = jnp.where(upper, 0.0, kv).astype(BF)
        kx_ref[1, rows, :] = jnp.where(upper, swapped, 0.0).astype(BF)
        vx_ref[0, rows, :] = jnp.where(upper, 0.0, swapped).astype(BF)
        vx_ref[1, rows, :] = jnp.where(upper, kv, 0.0).astype(BF)
        picked = [select_heads(queries, meta[:, k : k + 1], lane_half) for k in range(A_TOP)]
        for j in range(A_TOP // 2):
            slotq_ref[j, rows, :] = jnp.where(upper, picked[2 * j + 1], picked[2 * j]).astype(BF)
        chosen = [
            jnp.sum(jnp.where(lane == meta[:, k : k + 1], logits, 0.0), axis=1, keepdims=True)
            for k in range(A_TOP)
        ]
        top = jnp.maximum(jnp.maximum(chosen[0], chosen[1]), jnp.maximum(chosen[2], chosen[3]))
        raised = [jnp.exp(c - top) for c in chosen]
        scale = 1.0 / (raised[0] + raised[1] + raised[2] + raised[3])
        gates = jnp.zeros((BLOCK, LANES), F32)
        for k in range(A_TOP):
            gates = jnp.where(lane == k, raised[k] * scale, gates)
        gates_ref[rows, :] = gates
        return 0

    lax.fori_loop(0, tok // BLOCK, project, 0)
    for i in (1, 2, 5):
        whole_copies[i].start()

    below = lax.broadcasted_iota(jnp.int32, (BLOCK, BLOCK), 1) <= lax.broadcasted_iota(
        jnp.int32, (BLOCK, BLOCK), 0
    )
    for i in range(tok // BLOCK):
        rows = slice(i * BLOCK, (i + 1) * BLOCK)
        seen = (i + 1) * BLOCK
        lse_ref[rows, :] = jnp.zeros((BLOCK, LANES), F32)

        def pair(j, _, rows=rows, seen=seen, i=i):
            out = jnp.zeros((BLOCK, LANES), F32)
            query = slotq_ref[j, rows, :]
            logs = lse_ref[rows, :]
            for h in range(2):
                scores = dot(query, kx_ref[h, :seen, :], NT) * (HEAD**-0.5)
                last = jnp.where(below, scores[:, i * BLOCK :], NEG)
                scores = last if i == 0 else jnp.concatenate([scores[:, : i * BLOCK], last], axis=1)
                top = jnp.max(scores, axis=1, keepdims=True)
                raised = jnp.exp(scores - top)
                total = jnp.sum(raised, axis=1, keepdims=True)
                probs = (raised * (1.0 / total)).astype(BF)
                out = out + dot(probs, vx_ref[h, :seen, :])
                logs = jnp.where(lane == 2 * j + h, top + jnp.log(total), logs)
            so_ref[j, rows, :] = out
            lse_ref[rows, :] = logs
            return 0

        lax.fori_loop(0, A_TOP // 2, pair, 0)

    for i in (3, 4):
        whole_copies[i].start()

    def finish(b, _):
        rows = pl.ds(b * BLOCK, BLOCK)
        meta = meta_ref[rows, :]
        gates = gates_ref[rows, :]
        active = jnp.where(meta[:, 6:7] >= STEP, 1.0, 0.0)
        pairs = [
            so_ref[j, rows, :]
            * jnp.where(upper, gates[:, 2 * j + 1 : 2 * j + 2], gates[:, 2 * j : 2 * j + 1])
            for j in range(A_TOP // 2)
        ]

        def store(p, block):
            mixed_ref[rows, p * LANES : (p + 1) * LANES] = block

        spread_heads(pairs, meta, lane, lane_half, store)
        branch = dot(mixed_ref[rows, :], w_ref[:, WIDTH:KV_AT], NT)
        hidden = tok_ref[rows, :].astype(F32) + active * branch
        hidden_ref[rows, :] = hidden
        hat, _ = norm_stats(hidden)
        normed = (hat * gain_two + shift_two).astype(BF)
        n2_ref[rows, :] = normed
        logits = dot(normed, w_ref[:, RV_AT:PACK])
        first_logit, second_logit = (
            jnp.sum(
                jnp.where(lane == meta[:, 4 + k : 5 + k] + A_EXP, logits, 0.0), axis=1, keepdims=True
            )
            for k in range(F_TOP)
        )
        top = jnp.maximum(first_logit, second_logit)
        first_raised, second_raised = jnp.exp(first_logit - top), jnp.exp(second_logit - top)
        scale = 1.0 / (first_raised + second_raised)
        fgate_ref[rows, :] = jnp.where(lane == 0, first_raised * scale, second_raised * scale)
        for copy in row_copies(b, rows):
            copy.start()
        return 0

    lax.fori_loop(0, tok // BLOCK, finish, 0)

    def slots_copy(pair):
        both = pl.ds(2 * pair, 2)
        return pltpu.make_async_copy(slots_ref.at[both], outs[10].at[both], sems.at[10, pair])

    def gather(pair, _):
        gather_pair(rank_t_ref, n2_ref, (0,), (slots_ref,), pair)
        slots_copy(pair).start()
        return 0

    lax.fori_loop(0, experts // 2, gather, 0)
    for pair in range(experts // 2):
        slots_copy(pair).wait()
    for copy in whole_copies.values():
        copy.wait()
    for b in range(tok // BLOCK):
        for copy in row_copies(b, pl.ds(b * BLOCK, BLOCK)):
            copy.wait()


def expert_kernel(parts, x_ref, up_ref, down_ref, out_ref, act_ref, slope_ref, total_ref):
    total_ref[...] = jnp.zeros(total_ref.shape, F32)

    def part(c, _):
        pre = dot(x_ref[...], up_ref[c])
        square = pre * pre
        short = jnp.minimum(square, ROOT_MAX)
        root = ROOT[-1] * short
        for coef in ROOT[-2:0:-1]:
            root = (root + coef) * short
        phi = 0.5 + 0.5 * jnp.tanh(pre * (root + ROOT[0]))
        act = (pre * phi).astype(BF)
        act_ref[c] = act
        bell = jnp.exp2(square * BELL)
        slope_ref[c] = (phi + (pre * BELL_SCALE) * bell).astype(BF)
        total_ref[...] += dot(act, down_ref[c])
        return 0

    lax.fori_loop(0, parts, part, 0, unroll=2)
    out_ref[...] = total_ref[...].astype(BF)


def combine_sums(h, place, back_ref, fgate, cot, halt_row, lane, branch, cols):
    slot = lax.broadcasted_iota(jnp.int32, (BLOCK, back_ref.shape[0]), 1)
    for k in range(F_TOP):
        at = F_TOP * h + k
        hot = jnp.where(slot == place[:, at : at + 1], 1.0, 0.0).astype(BF)
        came = dot(hot, back_ref[...])
        branch = branch + fgate[:, k : k + 1] * came
        one = jnp.sum(came * cot, axis=1, keepdims=True)
        two = jnp.sum(came * halt_row, axis=1, keepdims=True)
        cols = cols + jnp.where(lane == k, one, jnp.where(lane == F_TOP + k, two, 0.0))
    return branch, cols


def split_three(values):
    high = values.astype(BF).astype(F32)
    middle = (values - high).astype(BF).astype(F32)
    return high, middle, values - high - middle


def combine_first_kernel(
    experts,
    capacity,
    back_ref,
    rank_ref,
    tail_ref,
    meta_ref,
    fgate_ref,
    cot_ref,
    pair_ref,
    branch_ref,
    cols_ref,
    live_ref,
    place_ref,
    scal_ref,
    dense_ref,
):
    halt_row = vector_row(turned_tail(tail_ref[...]), A_EXP + experts, 4)
    lane = lane_ids(BLOCK)

    def block(b, _):
        rows = pl.ds(b * BLOCK, BLOCK)
        meta = meta_ref[rows, :]
        fgate = fgate_ref[rows, :]
        pair = pair_ref[rows, :]
        scal_ref[rows, :] = jnp.where(lane == 0, pair[:, 0:1], pair[:, 1:2])
        place = slot_places(capacity, meta, rank_ref[rows, :], lane)
        place_ref[rows, :] = place
        branch, cols = combine_sums(
            0,
            place,
            back_ref,
            fgate,
            cot_ref[rows, :].astype(F32),
            halt_row,
            lane,
            jnp.zeros((BLOCK, D), F32),
            jnp.zeros((BLOCK, LANES), F32),
        )
        branch_ref[rows, :] = branch
        cols_ref[rows, :] = cols
        active = jnp.where(meta[:, 6:7] >= STEP, 1.0, 0.0)
        dense = jnp.zeros((BLOCK, LANES), F32)
        for k in range(F_TOP):
            named = lane == meta[:, 4 + k : 5 + k]
            dense = jnp.where(named, active * fgate[:, k : k + 1], dense)
        dense_ref[rows, :] = dense
        return 0

    lax.fori_loop(0, branch_ref.shape[0] // BLOCK, block, 0)
    turned = jnp.transpose(dense_ref[...])[: live_ref.shape[1], :]
    for index, part in enumerate(split_three(turned)):
        live_ref[index] = part.astype(BF)


def combine_kernel(
    experts,
    capacity,
    back_ref,
    branch_ref,
    cols_ref,
    live_ref,
    place_ref,
    rank_t_ref,
    hidden_ref,
    tail_ref,
    meta_ref,
    fgate_ref,
    scal_ref,
    cot_ref,
    out_ref,
    halt_ref,
    slope_ref,
    glf_ref,
    row_ref,
    ab_ref,
    kept_ref,
):
    step = pl.program_id(0)
    halt_row = vector_row(turned_tail(tail_ref[...]), A_EXP + experts, 4)
    lane = lane_ids(BLOCK)

    @pl.when(step == 0)
    def _():
        row_ref[...] = jnp.zeros(row_ref.shape, F32)

    meta = meta_ref[...]
    fgate = fgate_ref[...]
    scal = scal_ref[...]
    active = jnp.where(meta[:, 6:7] >= STEP, 1.0, 0.0)
    branch, cols = combine_sums(
        1,
        place_ref[...],
        back_ref,
        fgate,
        cot_ref[...].astype(F32),
        halt_row,
        lane,
        branch_ref[...],
        cols_ref[...],
    )
    z = hidden_ref[...] + active * branch
    out_ref[...] = z.astype(BF)
    prob = 1.0 / (1.0 + jnp.exp(-jnp.sum(z * halt_row, axis=1, keepdims=True)))
    halt_in, cot_halt = scal[:, 0:1], scal[:, 1:2]
    room = active * (1.0 - halt_in) * prob
    slope = cot_halt * room * (1.0 - prob)
    halt_ref[...] = jnp.broadcast_to(halt_in + room, (BLOCK, LANES))
    wide_slope = jnp.broadcast_to(slope, (BLOCK, LANES))
    slope_ref[...] = wide_slope
    kept_ref[pl.ds(step * BLOCK, BLOCK), :] = wide_slope
    row_ref[0:1, :] += jnp.sum(slope * z, axis=0, keepdims=True)
    gfg = [active * (cols[:, k : k + 1] + slope * cols[:, 2 + k : 3 + k]) for k in range(F_TOP)]
    inner = fgate[:, 0:1] * gfg[0] + fgate[:, 1:2] * gfg[1]
    glf = jnp.zeros((BLOCK, LANES), F32)
    for k in range(F_TOP):
        value = fgate[:, k : k + 1] * (gfg[k] - inner)
        glf = jnp.where(lane == meta[:, 4 + k : 5 + k] + A_EXP, value, glf)
    glf_ref[...] = glf

    @pl.when(step == pl.num_programs(0) - 1)
    def _():
        slopes = [part[:1, :] for part in split_three(jnp.transpose(kept_ref[...]))]
        low = [live_ref[i].astype(F32) for i in range(3)]
        tok = kept_ref.shape[0]
        for e in range(experts):
            rows = [part[e : e + 1, :] for part in low] + slopes + [jnp.zeros((2, tok), F32)]
            rows = jnp.concatenate(rows, axis=0).astype(BF)
            ab_ref[e] = dot(rows, one_hot(rank_t_ref, e, capacity), NT).astype(BF)


def data_back_kernel(experts, parts, h, *refs):
    cot_refs, refs = refs[:-8], refs[-8:]
    ab_ref, tail_ref, slope_ref, up_ref, down_ref, gpre_ref, gy_ref, rows_ref = refs
    size = ab_ref.shape[2] // HALVES
    count = ab_ref.shape[0]
    rows = count * size
    halt_row = vector_row(turned_tail(tail_ref[...]), A_EXP + experts, 4)
    cols = []
    cots = []
    for i in range(count):
        ab = ab_ref[i].astype(F32)[:, h * size : (h + 1) * size]
        live = ab[0:1, :] + ab[1:2, :] + ab[2:3, :]
        slope = ab[3:4, :] + ab[4:5, :] + ab[5:6, :]
        filler = jnp.zeros((LANES - 2, size), F32)
        cols.append(jnp.transpose(jnp.concatenate([live, slope, filler], axis=0)))
        for ref in cot_refs:
            part = ref.shape[0] // count
            cots.append(ref[i * part : (i + 1) * part, :].astype(F32))
    cols = jnp.concatenate(cols, axis=0)
    cots = jnp.concatenate(cots, axis=0)
    gy = (cols[:, 0:1] * (cots + cols[:, 1:2] * halt_row)).astype(BF)
    gy_ref[...] = gy
    total = jnp.zeros((rows, D), F32)
    for c in range(parts):
        gpre = (dot(gy, down_ref[c], NT) * slope_ref[c].astype(F32)).astype(BF)
        gpre_ref[c] = gpre
        total = total + dot(gpre, up_ref[c], NT)
    rows_ref[...] = total.astype(BF)


def weight_back_kernel(parts, steps, joined, *refs):
    up_acc, down_acc = refs[-2:]
    step = pl.program_id(0)

    @pl.when(step == 0)
    def _():
        up_acc[...] = jnp.zeros(up_acc.shape, F32)
        down_acc[...] = jnp.zeros(down_acc.shape, F32)

    for h in range(HALVES):
        x_ref, gy_ref, gpre_ref, act_ref = refs[4 * h : 4 * h + 4]

        @pl.when(step // steps == h)
        def _(x_ref=x_ref, gy_ref=gy_ref, gpre_ref=gpre_ref, act_ref=act_ref):
            for c in range(parts):
                up_acc[c] += dot(x_ref[...], gpre_ref[c], TN)
                down_acc[c] += dot(gy_ref[...], act_ref[c], TN)

    @pl.when(step == pl.num_programs(0) - 1)
    def _():
        for c in range(parts):
            if joined:
                refs[-3][c, :D] = up_acc[c].astype(BF)
                refs[-3][c, D:] = jnp.transpose(down_acc[c]).astype(BF)
            else:
                refs[-4][c] = up_acc[c].astype(BF)
                refs[-3][c] = jnp.transpose(down_acc[c]).astype(BF)


def store_grads(ref, values, start):
    columns = slice(start, start + values.shape[1])
    if len(ref.shape) == 2:
        ref[:, columns] = values
        return
    if len(ref.shape) == 5:
        _, chips, groups, shard, _ = ref.shape
        core = jnp.bitwise_and(lax.axis_index("fsdp"), 1)
        for e in range(2 * chips):
            for g in range(groups):
                at = (g * 2 * chips + e) * shard
                side = jnp.bitwise_xor(core, e % 2)
                ref[side, e // 2, g, :, columns] = values[at : at + shard]
        return
    experts, groups, shard, _ = ref.shape
    for e in range(experts):
        for g in range(groups):
            at = (g * experts + e) * shard
            ref[e, g, :, columns] = values[at : at + shard]


def hidden_back_kernel(
    experts,
    capacity,
    first_ref,
    second_ref,
    rank_ref,
    hidden_ref,
    w_ref,
    tail_ref,
    meta_ref,
    cot_ref,
    slope_ref,
    glf_ref,
    mixed_ref,
    so_ref,
    gates_ref,
    lse_ref,
    gout_ref,
    gh_ref,
    gslot_ref,
    gla_ref,
    logs_ref,
    rv_ref,
    vec_ref,
    acc_ref,
):
    step = pl.program_id(0)
    count = hidden_ref.shape[0]
    first = A_EXP + experts
    size = capacity // HALVES
    rows_t = turned_tail(tail_ref[...])
    low_t = rows_t.astype(BF)
    gain_two, shift_two, halt_row = (vector_row(rows_t, first, i) for i in (2, 3, 4))
    lane = lane_ids(count)
    upper = lane >= HEAD
    lane_half = jnp.where(upper, 1, 0)

    @pl.when(step == 0)
    def _():
        vec_ref[...] = jnp.zeros(vec_ref.shape, F32)
        acc_ref[...] = jnp.zeros(acc_ref.shape, F32)
        rv_ref[...] = jnp.zeros(rv_ref.shape, F32)

    meta = meta_ref[...]
    rank = rank_ref[...].astype(jnp.int32)
    active = jnp.where(meta[:, 6:7] >= STEP, 1.0, 0.0)
    place = lax.broadcasted_iota(jnp.int32, (count, size), 1)
    glf_high, glf_low = split_two(glf_ref[...])
    grad = dot(glf_high, low_t) + dot(glf_low, low_t)
    for h, back_ref in enumerate((first_ref, second_ref)):
        for e in range(experts):
            hot = jnp.where(place + h * size == rank[:, e : e + 1], 1.0, 0.0).astype(BF)
            grad = grad + dot(hot, back_ref[e])
    hat, inv = norm_stats(hidden_ref[...])
    normed = (hat * gain_two + shift_two).astype(BF)
    rv_ref[...] += dot(normed, glf_high, TN) + dot(normed, glf_low, TN)
    vec_ref[2:3, :] += jnp.sum(grad * hat, axis=0, keepdims=True)
    vec_ref[3:4, :] += jnp.sum(grad, axis=0, keepdims=True)
    gz = cot_ref[...].astype(F32) + slope_ref[:, 0:1] * halt_row
    gh = gz + norm_back(grad, hat, inv, gain_two)
    gh_ref[...] = gh
    ga = (active * gh).astype(BF)
    acc_ref[...] += dot(ga, mixed_ref[...], TN)
    gm = dot(ga, w_ref[...])
    gates = gates_ref[...]
    weighted = jnp.zeros((count, 1), F32)
    grads = []
    picked = [select_heads(gm, meta[:, k : k + 1], lane_half) for k in range(A_TOP)]
    for j in range(A_TOP // 2):
        both = jnp.where(upper, picked[2 * j + 1], picked[2 * j])
        prod = both * so_ref[j]
        scale = jnp.where(upper, gates[:, 2 * j + 1 : 2 * j + 2], gates[:, 2 * j : 2 * j + 1])
        gslot_ref[j] = (both * scale).astype(BF)
        grads.append(jnp.sum(jnp.where(upper, 0.0, prod), axis=1, keepdims=True))
        grads.append(jnp.sum(jnp.where(upper, prod, 0.0), axis=1, keepdims=True))
    logs = lse_ref[...]
    for k in range(A_TOP):
        inner = gates[:, k : k + 1] * grads[k]
        weighted = weighted + inner
        logs = jnp.where(lane == A_TOP + k, inner, logs)
    logs_ref[...] = logs
    gla = jnp.zeros((count, LANES), F32)
    for k in range(A_TOP):
        value = gates[:, k : k + 1] * (grads[k] - weighted)
        gla = jnp.where(lane == meta[:, k : k + 1], value, gla)
    gla_ref[...] = gla

    @pl.when(step == pl.num_programs(0) - 1)
    def _():
        store_grads(gout_ref, acc_ref[...].astype(BF), 0)


def input_back_kernel(
    experts,
    tok_hbm,
    w_hbm,
    meta_hbm,
    gh_hbm,
    gla_hbm,
    gslot_ref,
    rvin_ref,
    vecin_ref,
    halt_ref,
    lse_ref,
    slotq_ref,
    kv_ref,
    gin_hbm,
    pack_ref,
    tok_ref,
    w_ref,
    meta_ref,
    gh_ref,
    gla_ref,
    gin_ref,
    gx_ref,
    wide_ref,
    acc_ref,
    rv_ref,
    vec_ref,
    kx_ref,
    vx_ref,
    lset_ref,
    gq_ref,
    load_sems,
    store_sems,
):
    loads = [
        pltpu.make_async_copy(source, target, load_sems.at[i])
        for i, (source, target) in enumerate(
            (
                (tok_hbm, tok_ref),
                (w_hbm, w_ref),
                (meta_hbm, meta_ref),
                (gh_hbm, gh_ref),
                (gla_hbm, gla_ref),
            )
        )
    ]
    for load in loads:
        load.start()
    tok = tok_ref.shape[0]
    blocks = tok // BLOCK
    first = A_EXP + experts
    lane = lane_ids(BLOCK)
    upper = lane >= HEAD
    lane_half = jnp.where(upper, 1, 0)
    all_upper = lane_ids(tok) >= HEAD
    vec_ref[...] = jnp.zeros(vec_ref.shape, F32)
    vec_ref[2:4, :] = vecin_ref[2:4, :]
    vec_ref[4:5, :] = halt_ref[0:1, :]
    acc_ref[...] = jnp.zeros(acc_ref.shape, F32)
    rv_ref[...] = rvin_ref[...]
    kv = kv_ref[...].astype(F32)
    swapped = pltpu.roll(kv, HEAD, 1)
    kx_ref[0] = jnp.where(all_upper, 0.0, kv).astype(BF)
    kx_ref[1] = jnp.where(all_upper, swapped, 0.0).astype(BF)
    vx_ref[0] = jnp.where(all_upper, 0.0, swapped).astype(BF)
    vx_ref[1] = jnp.where(all_upper, kv, 0.0).astype(BF)
    lset_ref[...] = jnp.transpose(lse_ref[...])

    above = lax.broadcasted_iota(jnp.int32, (BLOCK, BLOCK), 0) <= lax.broadcasted_iota(
        jnp.int32, (BLOCK, BLOCK), 1
    )
    gx_ref[...] = jnp.zeros(gx_ref.shape, F32)
    for i in range(blocks):
        rows = slice(i * BLOCK, (i + 1) * BLOCK)
        seen = (i + 1) * BLOCK

        def pair(j, _, rows=rows, seen=seen, i=i):
            query = (slotq_ref[j, rows, :].astype(F32) * (HEAD**-0.5)).astype(BF)
            gslot = gslot_ref[j, rows, :]
            gq = jnp.zeros((BLOCK, LANES), F32)
            for h in range(2):
                keys = kx_ref[h, :seen, :]
                log = lset_ref[pl.ds(2 * j + h, 1), rows]
                scores = dot(keys, query, NT) - log
                last = jnp.where(above, scores[i * BLOCK :, :], NEG)
                scores = last if i == 0 else jnp.concatenate([scores[: i * BLOCK], last], axis=0)
                probs = jnp.exp(scores)
                gprob = dot(vx_ref[h, :seen, :], gslot, NT)
                inner = lset_ref[pl.ds(A_TOP + 2 * j + h, 1), rows]
                gs = (probs * (gprob - inner)).astype(BF)
                gq = gq + dot(gs, keys, TN)
                gx_ref[0, h, :seen, :] += dot(gs, query)
                gx_ref[1, h, :seen, :] += dot(probs.astype(BF), gslot)
            gq_ref[j, rows, :] = gq * (HEAD**-0.5)
            return 0

        lax.fori_loop(0, A_TOP // 2, pair, 0)

    for load in loads:
        load.wait()
    rows_t = transposed_tail(w_ref)
    low_t = rows_t.astype(BF)
    gain_one, shift_one = (vector_row(rows_t, first, i) for i in range(2))

    def stored(b):
        rows = pl.ds(b * BLOCK, BLOCK)
        return pltpu.make_async_copy(gin_ref.at[rows], gin_hbm.at[rows], store_sems.at[b])

    def input_back(b, gkv_sum):
        rows = pl.ds(b * BLOCK, BLOCK)
        meta = meta_ref[rows, :]
        pairs = [gq_ref[j, rows, :] for j in range(A_TOP // 2)]

        def store(p, block):
            wide_ref[:, p * LANES : (p + 1) * LANES] = block

        spread_heads(pairs, meta, lane, lane_half, store)
        gkeys = gx_ref[0, 0, rows, :] + pltpu.roll(gx_ref[0, 1, rows, :], HEAD, 1)
        gvals = pltpu.roll(gx_ref[1, 0, rows, :], HEAD, 1) + gx_ref[1, 1, rows, :]
        gkv = jnp.where(upper, gvals, gkeys).astype(BF)
        gla_high, gla_low = split_two(gla_ref[rows, :])
        grad = dot(wide_ref[...], w_ref[:, :WIDTH], NT)
        grad = grad + dot(gkv, w_ref[:, KV_AT:RV_AT], NT)
        grad = grad + dot(gla_high, low_t) + dot(gla_low, low_t)
        hat, inv = norm_stats(tok_ref[rows, :].astype(F32))
        normed = (hat * gain_one + shift_one).astype(BF)
        acc_ref[...] += dot(normed, wide_ref[...], TN)
        rv_ref[...] += dot(normed, gla_high, TN) + dot(normed, gla_low, TN)
        vec_ref[0:1, :] += jnp.sum(grad * hat, axis=0, keepdims=True)
        vec_ref[1:2, :] += jnp.sum(grad, axis=0, keepdims=True)
        gin_ref[rows, :] = (gh_ref[rows, :] + norm_back(grad, hat, inv, gain_one)).astype(BF)
        stored(b).start()
        return gkv_sum + dot(normed, gkv, TN)

    gkv_sum = lax.fori_loop(0, blocks, input_back, jnp.zeros((D, LANES), F32))
    store_grads(pack_ref, acc_ref[...].astype(BF), 0)
    store_grads(pack_ref, gkv_sum.astype(BF), WIDTH)
    turned = pltpu.roll(jnp.transpose(vec_ref[...]), first, 1)
    tail = jnp.where(lane_ids(D) < first, rv_ref[...], turned)
    store_grads(pack_ref, tail.astype(BF), WIDTH + LANES)
    for b in range(blocks):
        stored(b).wait()


VMEM_LIMIT = 60 * 1024 * 1024
VMEM_ALL = 67043328


def whole(shape, dtype):
    return jax.ShapeDtypeStruct(shape, dtype)


def in_vmem(count):
    return [pl.BlockSpec(memory_space=pltpu.VMEM)] * count


def call(kernel, inputs, outs, scratch=(), limit=VMEM_LIMIT):
    return pl.pallas_call(
        kernel,
        out_shape=outs,
        in_specs=in_vmem(len(inputs)),
        out_specs=in_vmem(len(outs)),
        scratch_shapes=list(scratch),
        compiler_params=pltpu.CompilerParams(vmem_limit_bytes=limit),
    )(*inputs)


def constant_spec(shape, middle=0):
    return pl.BlockSpec(shape, lambda s: (0, middle, 0), pipeline_mode=pl.Buffered(1))


def gather_pieces(pack, shape):
    groups, experts, _ = shape
    if experts != 8 or groups != 4:
        own = lax.all_gather(pack, "dp", axis=0, tiled=False)
        every = lax.all_gather(own, "fsdp", axis=0, tiled=False)
        return [every.transpose(1, 0, 2, 3).reshape(D, PACK)]

    own = [pack]
    for d in range(1, groups):
        pairs = [((i + d) % groups, i) for i in range(groups)]
        own.append(lax.ppermute(pack, "dp", pairs))
    own = jnp.stack(own)

    def swap(values, m):
        return lax.ppermute(values, "fsdp", [(i, i ^ m) for i in range(experts)])

    along = swap(own, 2)
    across = swap(own, 4)
    low = swap(along[: groups // 2], 4)
    high = swap(across[groups // 2 :], 2)
    return [
        own,
        swap(own, 1),
        along,
        swap(along, 1),
        across,
        swap(across, 1),
        low,
        high,
        swap(low, 1),
        swap(high, 1),
    ]


def on_device(
    tokens,
    halt_in,
    depths,
    attn_routes,
    ffn_routes,
    w_query,
    w_out,
    w_kv,
    router,
    vectors,
    w_up,
    w_down,
    cot_out,
    cot_halt,
):
    tok = tokens.shape[0]
    groups, experts = lax.axis_size("dp"), lax.axis_size("fsdp")
    capacity = 2 * F_TOP * tok // experts
    slice_width = w_up.shape[2]
    shard = w_query.shape[0]
    slots = experts * capacity

    tail = jnp.concatenate([router, vectors.T], axis=1)
    tail = jnp.pad(tail, ((0, 0), (0, LANES - tail.shape[1])))
    pack = jnp.concatenate([w_query, w_out.T, w_kv, tail], axis=1)
    shape = (groups, experts, shard)
    pieces = gather_pieces(pack, shape)
    joined = slice_width == D
    if joined:
        expert_pack = jnp.concatenate([w_up[0], w_down[0]], axis=0)
        whole_up = whole_down = lax.all_gather(expert_pack, "dp", axis=0, tiled=False)
    else:
        whole_up = lax.all_gather(w_up[0], "dp", axis=0, tiled=False)
        whole_down = lax.all_gather(w_down[0], "dp", axis=0, tiled=False)

    meta = jnp.concatenate([attn_routes, ffn_routes, depths[:, None], depths[:, None]], axis=1)
    scal = jnp.stack([halt_in, cot_halt], axis=1)
    half = capacity // HALVES
    half_slots = slots // HALVES

    rank, rank_t = call(
        ranks_kernel, (meta,), (whole((tok, LANES), F32), whole((experts, tok), jnp.int32))
    )

    def gather_rows(rows, name, starts):
        ends = starts[1:] + (starts[0] + half,)
        shapes = [whole((experts, end - start, D), BF) for start, end in zip(starts, ends)]
        limit = VMEM_LIMIT if name == "cot_slots" else VMEM_ALL
        return call(partial(gather_kernel, experts, starts), (rank_t, rows), shapes, limit=limit)

    cot_slots = gather_rows(cot_out, "cot_slots", (0,))

    def exchange(values):
        came = lax.all_to_all(values, "fsdp", split_axis=0, concat_axis=0, tiled=True)
        return came

    *pieces, cot_first = lax.optimization_barrier((*pieces, cot_slots[0]))
    owned_cot = [exchange(cot_first)]

    attend_outs = (
        whole((D, PACK), BF),
        whole((2, tok, LANES), BF),
        whole((tok, LANES), BF),
        whole((2, tok, LANES), F32),
        whole((tok, LANES), F32),
        whole((tok, LANES), F32),
        whole((tok, WIDTH), BF),
        whole((tok, D), F32),
        whole((tok, LANES), F32),
        whole((tok, D), BF),
        whole((experts, half, D), BF),
    )
    weights, slotq, kv, so, lse, gates, mixed, hidden, fgate, normed_two, sent = pl.pallas_call(
        partial(attend_kernel, experts, shape),
        name="attend",
        out_shape=attend_outs,
        in_specs=in_vmem(3 + len(pieces)),
        out_specs=[pl.BlockSpec(memory_space=pl.ANY)] * len(attend_outs),
        scratch_shapes=[pltpu.VMEM(out.shape, out.dtype) for out in attend_outs]
        + [
            pltpu.VMEM((2, tok, LANES), BF),
            pltpu.VMEM((2, tok, LANES), BF),
            pltpu.SemaphoreType.DMA((len(attend_outs), max(tok // BLOCK, experts // 2))),
        ],
        compiler_params=pltpu.CompilerParams(vmem_limit_bytes=VMEM_ALL),
    )(tokens, meta, rank_t, *pieces)
    n2_slots = [sent, *gather_rows(normed_two, "dispatch_1", (half,))]
    n2_slots[0], owned_cot[0] = lax.optimization_barrier((n2_slots[0], owned_cot[0]))
    cot_slots += gather_rows(cot_out, "cot_late", (half, half + half // 2))

    up_spec = constant_spec((groups, D, slice_width))
    down_spec = constant_spec((groups, slice_width, D), 1 if joined else 0)
    params = pltpu.CompilerParams(vmem_limit_bytes=VMEM_ALL)
    wide = whole((groups, half_slots, slice_width), BF)
    narrow = whole((half_slots, D), BF)
    step_rows = max(half, min(512, half_slots))
    step_spec = pl.BlockSpec((step_rows, D), lambda s: (s, 0))
    step_wide = pl.BlockSpec((groups, step_rows, slice_width), lambda s: (0, s, 0))

    owned = []
    for h in range(HALVES):
        owned.append(exchange(n2_slots[h]).reshape(half_slots, D))
        if h + 1 < HALVES:
            n2_slots[h + 1], owned[h] = lax.optimization_barrier((n2_slots[h + 1], owned[h]))
    outs, acts, slopes = [], [], []
    for h in range(HALVES):
        out, act, slope = pl.pallas_call(
            partial(expert_kernel, groups),
            grid=(half_slots // step_rows,),
            out_shape=(narrow, wide, wide),
            in_specs=[step_spec, up_spec, down_spec],
            out_specs=[step_spec, step_wide, step_wide],
            scratch_shapes=[pltpu.VMEM((step_rows, D), F32)],
            compiler_params=params,
        )(owned[h], whole_up, whole_down)
        outs.append(out)
        acts.append(act)
        slopes.append(slope)
    back = []
    for h in range(HALVES):
        back.append(exchange(outs[h].reshape(experts, half, D)).reshape(half_slots, D))

    tail_spec = pl.BlockSpec((D, LANES), lambda s: (0, RV_AT // LANES))
    full = pl.BlockSpec(memory_space=pltpu.VMEM)
    *sums, place, scal = pl.pallas_call(
        partial(combine_first_kernel, experts, capacity),
        name="combine_first",
        grid=(1,),
        out_shape=(
            whole((tok, D), F32),
            whole((tok, LANES), F32),
            whole((3, max(16, experts), tok), BF),
            whole((tok, LANES), jnp.int32),
            whole((tok, LANES), F32),
        ),
        in_specs=[full, full, tail_spec, full, full, full, full],
        out_specs=[full] * 5,
        scratch_shapes=[pltpu.VMEM((tok, LANES), F32)],
        compiler_params=params,
    )(back[0], rank, weights, meta, fgate, cot_out, scal)
    back[1], cot_second = lax.optimization_barrier((back[1], cot_slots[1]))
    owned_cot.append(exchange(cot_second))

    def tokens_of(width, count=BLOCK):
        return pl.BlockSpec((count, width), lambda b: (b, 0))

    block_out, halt_wide, halt_slope, glf, halt_grad, ab = pl.pallas_call(
        partial(combine_kernel, experts, capacity),
        name="combine",
        grid=(tok // BLOCK,),
        out_shape=(
            whole((tok, D), BF),
            whole((tok, LANES), F32),
            whole((tok, LANES), F32),
            whole((tok, LANES), F32),
            whole((8, D), F32),
            whole((experts, 8, capacity), BF),
        ),
        in_specs=[
            full,
            tokens_of(D),
            tokens_of(LANES),
            full,
            tokens_of(LANES),
            full,
            tokens_of(D),
            tail_spec,
            tokens_of(meta.shape[1]),
            tokens_of(LANES),
            tokens_of(LANES),
            tokens_of(D),
        ],
        out_specs=[tokens_of(D)] + [tokens_of(LANES)] * 3 + [full] * 2,
        scratch_shapes=[pltpu.VMEM((tok, LANES), F32)],
        compiler_params=params,
    )(back[1], *sums, place, rank_t, hidden, weights, meta, fgate, scal, cot_out)
    halt_out = halt_wide[:, 0]
    ab, owned_cot[1] = lax.optimization_barrier((ab, owned_cot[1]))
    owned_ab = exchange(ab)
    owned_ab, cot_third = lax.optimization_barrier((owned_ab, cot_slots[2]))
    owned_cot.append(exchange(cot_third))
    cot_parts = [owned_cot[:1], owned_cot[1:]]

    together = step_rows // half if half % LANES == 0 else 1
    row_spec = pl.BlockSpec((together * half, D), lambda s: (s, 0))
    wide_spec = pl.BlockSpec((groups, together * half, slice_width), lambda s: (0, s, 0))
    gys, gpres, rows_back = [], [], []
    for h in range(HALVES):
        gpre, gy, owned_rows = pl.pallas_call(
            partial(data_back_kernel, experts, groups, h),
            grid=(experts // together,),
            out_shape=(wide, narrow, narrow),
            in_specs=[
                *(pl.BlockSpec((together * part.shape[1], D), lambda s: (s, 0)) for part in cot_parts[h]),
                pl.BlockSpec((together, 8, capacity), lambda s: (s, 0, 0)),
                tail_spec,
                wide_spec,
                up_spec,
                down_spec,
            ],
            out_specs=[wide_spec, row_spec, row_spec],
            compiler_params=params,
        )(
            *(part.reshape(-1, D) for part in cot_parts[h]),
            owned_ab,
            weights,
            slopes[h],
            whole_up,
            whole_down,
        )
        gys.append(gy)
        gpres.append(gpre)
        rows_back.append(exchange(owned_rows.reshape(experts, half, D)))

    steps = half_slots // step_rows
    specs, inputs = [], []
    for h in range(HALVES):

        def at(s, h=h):
            return jnp.clip(s - h * steps, 0, steps - 1)

        narrow_at = pl.BlockSpec((step_rows, D), lambda s, at=at: (at(s), 0))
        wide_at = pl.BlockSpec((groups, step_rows, slice_width), lambda s, at=at: (0, at(s), 0))
        specs += [narrow_at, narrow_at, wide_at, wide_at]
        inputs += [owned[h], gys[h], gpres[h], acts[h]]
    if joined:
        grad_shapes = [(groups, 2 * D, D)]
    else:
        grad_shapes = [(groups, D, slice_width), (groups, slice_width, D)]
    expert_grads = pl.pallas_call(
        partial(weight_back_kernel, groups, steps, joined),
        name="weight_back",
        grid=(HALVES * steps,),
        out_shape=[whole(g, BF) for g in grad_shapes],
        in_specs=specs,
        out_specs=[constant_spec(g) for g in grad_shapes],
        scratch_shapes=[pltpu.VMEM((groups, D, slice_width), F32)] * 2,
        compiler_params=params,
    )(*inputs)
    expert_grads = [
        lax.psum_scatter(g, "dp", scatter_dimension=0, tiled=True) for g in expert_grads
    ]
    expert_grads = [g.astype(F32) for g in expert_grads]
    if joined:
        part_up, part_down = expert_grads[0][:, :D], expert_grads[0][:, D:]
    else:
        part_up, part_down = expert_grads

    ordered = shard % 16 == 0

    def grads_shape(width):
        return whole((experts, groups, shard, width) if ordered else (D, width), BF)

    wide_block = BLOCK
    pair_spec = pl.BlockSpec((2, wide_block, LANES), lambda b: (0, b, 0))
    lanes_spec = tokens_of(LANES, wide_block)
    grad_out, gh, gslot, gla, logs, rv, vec = pl.pallas_call(
        partial(hidden_back_kernel, experts, capacity),
        name="hidden_back",
        grid=(tok // wide_block,),
        out_shape=(
            grads_shape(WIDTH),
            whole((tok, D), F32),
            whole((2, tok, LANES), BF),
            whole((tok, LANES), F32),
            whole((tok, LANES), F32),
            whole((D, LANES), F32),
            whole((8, D), F32),
        ),
        in_specs=[
            full,
            full,
            lanes_spec,
            tokens_of(D, wide_block),
            pl.BlockSpec((D, WIDTH), lambda b: (0, 1), pipeline_mode=pl.Buffered(1)),
            tail_spec,
            tokens_of(meta.shape[1], wide_block),
            tokens_of(D, wide_block),
            lanes_spec,
            lanes_spec,
            tokens_of(WIDTH, wide_block),
            pair_spec,
            lanes_spec,
            lanes_spec,
        ],
        out_specs=[full, tokens_of(D, wide_block), pair_spec, lanes_spec, lanes_spec, full, full],
        scratch_shapes=[pltpu.VMEM((D, WIDTH), F32)],
        compiler_params=pltpu.CompilerParams(vmem_limit_bytes=VMEM_LIMIT),
    )(
        *rows_back,
        rank,
        hidden,
        weights,
        weights,
        meta,
        cot_out,
        halt_slope,
        glf,
        mixed,
        so,
        gates,
        lse,
    )

    def reduced(sent):
        if not ordered:
            sent = sent.reshape(groups, experts, shard, sent.shape[1]).transpose(1, 0, 2, 3)
        return jnp.sum(exchange(sent).astype(F32), axis=0).astype(BF)

    part_out = reduced(grad_out)
    paired = ordered and experts == 8
    last_shape = grads_shape(WIDTH + 2 * LANES)
    if paired:
        last_shape = whole((2, experts // 2, groups, shard, WIDTH + 2 * LANES), BF)

    def reduced_last(grads):
        if not paired:
            return reduced(grads)
        other = lax.ppermute(grads, "fsdp", [(i, i ^ 1) for i in range(experts)])
        chip = (grads[0].astype(F32) + other[1].astype(F32)).astype(BF)
        same = [list(range(c, experts, 2)) for c in range(2)]
        came = lax.all_to_all(
            chip, "fsdp", split_axis=0, concat_axis=0, tiled=True, axis_index_groups=same
        )
        return jnp.sum(came.astype(F32), axis=0).astype(BF)

    anywhere = pl.BlockSpec(memory_space=pl.ANY)
    grad_in, grads = pl.pallas_call(
        partial(input_back_kernel, experts),
        name="input_back",
        out_shape=(whole((tok, D), BF), last_shape),
        in_specs=[anywhere] * 5 + [full] * 7,
        out_specs=[anywhere, full],
        scratch_shapes=[
            pltpu.VMEM((tok, D), BF),
            pltpu.VMEM((D, PACK), BF),
            pltpu.VMEM(meta.shape, jnp.int32),
            pltpu.VMEM((tok, D), F32),
            pltpu.VMEM((tok, LANES), F32),
            pltpu.VMEM((tok, D), BF),
            pltpu.VMEM((2, 2, tok, LANES), F32),
            pltpu.VMEM((BLOCK, WIDTH), BF),
            pltpu.VMEM((D, WIDTH), F32),
            pltpu.VMEM((D, LANES), F32),
            pltpu.VMEM((LANES, D), F32),
            pltpu.VMEM((2, tok, LANES), BF),
            pltpu.VMEM((2, tok, LANES), BF),
            pltpu.VMEM((LANES, tok), F32),
            pltpu.VMEM((2, tok, LANES), F32),
            pltpu.SemaphoreType.DMA((5,)),
            pltpu.SemaphoreType.DMA((tok // BLOCK,)),
        ],
        compiler_params=pltpu.CompilerParams(vmem_limit_bytes=VMEM_LIMIT),
    )(tokens, weights, meta, gh, gla, gslot, rv, vec, halt_grad, logs, slotq, kv)
    part = jnp.concatenate([reduced_last(grads), part_out], axis=2)
    came = lax.all_to_all(part, "dp", split_axis=0, concat_axis=0, tiled=True)
    total = jnp.sum(came.astype(F32), axis=0)
    kv_end = WIDTH + LANES
    router_end = kv_end + A_EXP + experts
    return (
        block_out,
        halt_out,
        grad_in,
        total[:, :WIDTH],
        total[:, WIDTH + 2 * LANES :].T,
        total[:, WIDTH:kv_end],
        total[:, kv_end:router_end],
        total[:, router_end : router_end + 5].T,
        part_up,
        part_down,
    )


def solution(mesh):
    both = ("dp", "fsdp")
    placed = (
        P(both, None),
        P(both),
        P(both),
        P(both, None),
        P(both, None),
        P(both, None),
        P(None, both),
        P(both, None),
        P(both, None),
        P(None, both),
        P("fsdp", None, "dp"),
        P("fsdp", "dp", None),
        P(both, None),
        P(both),
    )

    return jax.shard_map(
        on_device,
        mesh=mesh,
        in_specs=placed,
        out_specs=(
            P(both, None),
            P(both),
            P(both, None),
            P(both, None),
            P(None, both),
            P(both, None),
            P(both, None),
            P(None, both),
            P("fsdp", None, "dp"),
            P("fsdp", "dp", None),
        ),
        check_vma=False,
    )
```
